256 devices in a mesh: mem: 16 (over x, y_lo, core), lat: 16 (over y_hi, z).
Axes of the slice: x: 4, y: 4 (y_hi: 2, y_lo: 2; y = y_hi * 2 + y_lo), z: 8, core: 2. Of those that a mesh axis runs over, the one named last changes fastest.
Arguments:
- state: float32 [16, 641, 32, 160], P('mem', None, 'lat'), may hold values from -6 to 6
- conv_kernel: float32 [25, 641], replicated, may hold values from -1.25 to 1.25
- norm_gain: float32 [641], replicated, may hold values from 0.5 to 1.5
- up_weight: bfloat16 [641, 1282], replicated, may hold values from -0.25 to 0.25
- down_weight: bfloat16 [1282, 641], replicated, may hold values from -0.15625 to 0.15625
- field_head_weight: bfloat16 [641, 72], replicated, may hold values from -0.25 to 0.25
- target: float32 [72, 32, 160], P(None, 'lat'), may hold values from -9 to 9
- field_weight: float32 [72], replicated, may hold values from 0.3 to 3
Outputs:
- loss: float32 [], replicated
- grad_kernel: float32 [25, 641], replicated
- grad_gain: float32 [641], replicated
- grad_up: float32 [641, 1282], replicated
- grad_down: float32 [1282, 641], replicated
- grad_head: float32 [641, 72], replicated
The draws below stay inside these ranges and needn't reach their ends.
All inputs are finite; a program needn't handle non-finite values.
Results may differ from the reference program's by a relative error of at most 0.005.
The reference program's roundings to bfloat16 on the way count: a program that leaves them out, or rounds other values in their place, can miss the bound.
Values may be sent and summed in bfloat16 or wider, within the bound.
A program may use at most 128 MiB of HBM per device.

```python
import math
import jax
import jax.numpy as jnp
from jax import lax

C = 641
HID = 1282
FIELDS = 72
LON = 160
MEMBERS = 16
NLAT = 32


def level_of(rng, dims, cuts, low, high):
    level = 1.0
    for dim, shards_of in cuts:
        draws = jax.random.uniform(jax.random.fold_in(jax.random.fold_in(rng, 6), dim), (shards_of,), jnp.float32, low / len(cuts), high / len(cuts))
        level = level * jnp.repeat(jnp.exp(draws), dims[dim] // shards_of).reshape((-1,) + (1,) * (len(dims) - 1 - dim))
    return level


def centred(key, dims, spread, most, shards=(), held_as=jnp.bfloat16):
    loudness = level_of(key, dims, shards, -0.22, 0.18) if shards else 1.0
    drawn = jax.random.normal(key, dims, jnp.float32) * spread * loudness
    return jnp.minimum(jnp.maximum(drawn, -most), most).astype(held_as)


def setup_inputs(seed: int = 0) -> dict:
    seeds = jax.random.split(jax.random.key(seed), 9)
    state = centred(seeds[0], (MEMBERS, C, NLAT, LON), 1.0, 6.0, ((0, 16), (2, 16)), jnp.float32)
    conv_kernel = centred(seeds[1], (25, C), 25 ** -0.5, 1.25, (), jnp.float32)
    norm_gain = jnp.clip(1.0 + 0.1 * jax.random.normal(seeds[2], (C,), jnp.float32), 0.5, 1.5)
    up_weight = centred(seeds[3], (C, HID), C ** -0.5, 0.25)
    down_weight = centred(seeds[4], (HID, C), HID ** -0.5, 0.15625)
    field_head_weight = centred(seeds[5], (C, FIELDS), C ** -0.5, 0.25)
    target = centred(seeds[6], (FIELDS, NLAT, LON), 1.5, 9.0, ((1, 16),), jnp.float32)
    field_weight = jnp.clip(jnp.exp(jax.random.uniform(seeds[7], (FIELDS,), jnp.float32, math.log(0.3), math.log(3.0))), 0.3, 3.0)
    return dict(state=state, conv_kernel=conv_kernel, norm_gain=norm_gain, up_weight=up_weight, down_weight=down_weight, field_head_weight=field_head_weight, target=target, field_weight=field_weight)


DELTA = 0.1
EPSILON = 1e-05

def softened_absolute(diff):
    return jnp.sqrt(diff * diff + DELTA * DELTA) - DELTA

def softened_derivative(diff):
    return diff / jnp.sqrt(diff * diff + DELTA * DELTA)

def gelu_parts(before_activation):
    cumul = 0.5 * (1.0 + jax.scipy.special.erf(before_activation / math.sqrt(2.0)))
    density = jnp.exp(-0.5 * before_activation * before_activation) / math.sqrt(2.0 * math.pi)
    return (before_activation * cumul, cumul + before_activation * density)

def leading_product(left, right):
    return lax.dot_general(left, right, (((0,), (0,)), ((), ())), preferred_element_type=jnp.float32)

def tail_dot(left, right):
    return lax.dot_general(left, right, (((1,), (1,)), ((), ())), preferred_element_type=jnp.float32)

def stencil(window, kernel, height):
    result = jnp.zeros((window.shape[0], height, window.shape[2]), jnp.float32)
    for col_off in range(5):
        shifted = jnp.roll(window, 2 - col_off, axis=2)
        for row_off in range(5):
            result = result + kernel[row_off * 5 + col_off][:, None, None] * shifted[:, row_off:row_off + height]
    return result

def kernel_grad(window, upstream, height):
    terms = [None] * 25
    for col_off in range(5):
        shifted = jnp.roll(window, 2 - col_off, axis=2)
        for row_off in range(5):
            terms[row_off * 5 + col_off] = lax.optimization_barrier(jnp.sum(upstream * shifted[:, row_off:row_off + height], axis=(1, 2)))
    return jnp.stack(terms)

def forward_apply(field, window, kernel, gain, up_weight, down_weight, field_head_weight):
    height = field.shape[1]
    channels = field.shape[0]
    summed = (field + stencil(window, kernel, height)).reshape(channels, -1)
    center = summed - lax.optimization_barrier(jnp.mean(summed, axis=0))
    inverse_norm = lax.rsqrt(lax.optimization_barrier(jnp.mean(center * center, axis=0)) + EPSILON)
    normalized_input = center * inverse_norm
    gain_scaled = (normalized_input * gain[:, None]).astype(jnp.bfloat16)
    before_activation = leading_product(up_weight, gain_scaled)
    activ, unused = gelu_parts(before_activation)
    hidden_activation = activ.astype(jnp.bfloat16)
    output = summed + leading_product(down_weight, hidden_activation)
    rounded_values = output.astype(jnp.bfloat16)
    member_prediction = leading_product(field_head_weight, rounded_values)
    return (member_prediction, (normalized_input, inverse_norm, gain_scaled, before_activation, hidden_activation, rounded_values))

def backward(window, stored_residuals, cotangent, kernel, gain, up_weight, down_weight, field_head_weight):
    normalized_input, inverse_norm, gain_scaled, before_activation, hidden_activation, rounded_values = stored_residuals
    height = window.shape[1] - 4
    co_round = cotangent.astype(jnp.bfloat16)
    grad_head = tail_dot(rounded_values, co_round)
    d_output = jnp.dot(field_head_weight, co_round, preferred_element_type=jnp.float32)
    d_round = d_output.astype(jnp.bfloat16)
    grad_down = tail_dot(hidden_activation, d_round)
    d_hidden = jnp.dot(down_weight, d_round, preferred_element_type=jnp.float32)
    unused, slope = gelu_parts(before_activation)
    d_preact = (d_hidden * slope).astype(jnp.bfloat16)
    grad_up = tail_dot(gain_scaled, d_preact)
    d_scaled = jnp.dot(up_weight, d_preact, preferred_element_type=jnp.float32)
    grad_gain = lax.optimization_barrier(jnp.sum(d_scaled * normalized_input, axis=1))
    d_normed = d_scaled * gain[:, None]
    d_summed = d_output + inverse_norm * (d_normed - lax.optimization_barrier(jnp.mean(d_normed, axis=0)) - normalized_input * lax.optimization_barrier(jnp.mean(d_normed * normalized_input, axis=0)))
    upstream = d_summed.reshape(window.shape[0], height, window.shape[2])
    grad_kernel = kernel_grad(window, upstream, height)
    return (grad_kernel, grad_gain, grad_up, grad_down, grad_head)

def pad_rows(field):
    return jnp.pad(field, ((0, 0), (2, 2), (0, 0)))

def reference(state, conv_kernel, norm_gain, up_weight, down_weight, field_head_weight, target, field_weight):

    def apply_member(field):
        return forward_apply(field, pad_rows(field), conv_kernel, norm_gain, up_weight, down_weight, field_head_weight)[0]
    ensemble_predictions = lax.map(apply_member, state)
    observed_target = target.reshape(FIELDS, -1)
    row_index = jnp.arange(NLAT).astype(jnp.float32)
    area = jnp.cos(0.5 * math.pi * ((row_index + 0.5) / NLAT - 1.0))
    latitude_weights = field_weight[:, None] * jnp.repeat(area, LON)[None, :]
    member_states = MEMBERS

    def pairwise_update(loop_carry_state, single_member):
        return (loop_carry_state + lax.optimization_barrier(jnp.sum(softened_absolute(single_member[None] - ensemble_predictions), axis=0)), lax.optimization_barrier(jnp.sum(softened_derivative(single_member[None] - ensemble_predictions), axis=0)))
    pairwise_sum, pairwise_derivatives = lax.scan(pairwise_update, jnp.zeros(observed_target.shape, jnp.float32), ensemble_predictions)
    ensemble_spread = lax.optimization_barrier(jnp.mean(softened_absolute(ensemble_predictions - observed_target[None]), axis=0)) - pairwise_sum / (2.0 * member_states * (member_states - 1))
    member_count = NLAT * LON * FIELDS
    loss = jnp.sum(latitude_weights * ensemble_spread) / member_count
    member_adjoints = latitude_weights[None] * (softened_derivative(ensemble_predictions - observed_target[None]) - pairwise_derivatives / (member_states - 1)) / (member_states * math.sqrt(member_count))

    def grad_step(loop_carry_state, items):
        field, cotangent = items
        window = pad_rows(field)
        unused, stored_residuals = forward_apply(field, window, conv_kernel, norm_gain, up_weight, down_weight, field_head_weight)
        grads = backward(window, stored_residuals, cotangent, conv_kernel, norm_gain, up_weight, down_weight, field_head_weight)
        return (jax.tree.map(jnp.add, loop_carry_state, grads), None)
    start = (jnp.zeros((25, C), jnp.float32), jnp.zeros((C,), jnp.float32), jnp.zeros((C, HID), jnp.float32), jnp.zeros((HID, C), jnp.float32), jnp.zeros((C, FIELDS), jnp.float32))
    totals, unused = lax.scan(grad_step, start, (state, member_adjoints))
    return (loss, totals[0], totals[1], totals[2], totals[3], totals[4])
```

```python
import functools
import math

import jax
import jax.numpy as jnp
from jax import lax
from jax.experimental import pallas as pl
from jax.experimental.pallas import tpu as pltpu
from jax.sharding import Mesh
from jax.sharding import PartitionSpec as P

AXES = ("mem_0", "mem_1", "mem_2", "lat_0", "lat_1")
MESH_ID = pl.DeviceIdType.MESH
MAIN_ROWS, MAIN_COLS = 40, 10
MAIN = MAIN_ROWS * MAIN_COLS
SMALL_ROWS, SMALL_COLS = 4, 6
UNITS = MAIN + SMALL_ROWS * SMALL_COLS
PARTS = ((168, "xyz"), (168, "yxz"), (88, "zxy"))
SIZE = {"x": 4, "y": 4, "z": 8}


def place():
    x = lax.axis_index("mem_0")
    y = lax.axis_index("lat_0") * 2 + lax.axis_index("mem_1")
    z = lax.axis_index("lat_1")
    return {"x": x, "y": y, "z": z}


def device_at(axis, p):
    if axis == "x":
        return {"mem_0": p}
    if axis == "y":
        return {"lat_0": p // 2, "mem_1": p % 2}
    return {"lat_1": p}


def steps_of():
    plans, at = [], 0
    for size, order in PARTS:
        left, levels = size, []
        for a in order:
            left = -(-left // SIZE[a])
            levels.append((a, SIZE[a], left))
        plans.append((at, size, levels))
        at += size
    return plans


def peers_of(at):
    out = []
    for a in "xyz":
        for d in range(1, SIZE[a]):
            out.append(device_at(a, (at[a] + d) % SIZE[a]))
    return out


def total_kernel(p_ref, loss_ref, g_ref, loss_out, *scratch):
    plans = steps_of()
    at = place()
    core = lax.axis_index("mem_2")
    sibling = {"mem_2": 1 - core}
    it = iter(scratch)
    core_in = next(it)
    parts = []
    for _ in plans:
        parts.append([[next(it) for _ in range(4)] for _ in range(3)])
    loss_in = next(it)
    cs, cr, cs2, cr2 = next(it), next(it), next(it), next(it)
    rs_s, rs_r, ag_s, ag_r = next(it), next(it), next(it), next(it)
    ls, lr = next(it), next(it)

    barrier = pltpu.get_barrier_semaphore()
    everyone = [sibling] + peers_of(at)
    for dev in everyone:
        pl.semaphore_signal(barrier, inc=1, device_id=dev, device_id_type=MESH_ID)
    pl.semaphore_wait(barrier, len(everyone))

    def remote(src, dst, s, r, dev):
        return pltpu.make_async_remote_copy(
            src_ref=src, dst_ref=dst, send_sem=s, recv_sem=r, device_id=dev, device_id_type=MESH_ID
        )

    first = []
    for k, (off, size, levels) in enumerate(plans):
        c = remote(
            p_ref.at[1 - core, pl.ds(off, size)], core_in.at[pl.ds(off, size)], cs.at[k], cr.at[k], sibling
        )
        c.start()
        first.append(c)
    open_copies = []
    loss_steps = [("c", [sibling])] + [
        (a, [device_at(a, (at[a] + d) % SIZE[a]) for d in range(1, SIZE[a])]) for a in "xyz"
    ]
    loss_value = loss_ref[...]

    def loss_send(level, value):
        base = (0, 2, 6, 10)[level]
        sbase = (0, 1, 4, 7)[level]
        loss_in[base] = value
        started = []
        for d, dev in enumerate(loss_steps[level][1]):
            c = remote(loss_in.at[base], loss_in.at[base + 1 + d], ls.at[sbase + d], lr.at[sbase + d], dev)
            c.start()
            started.append(c)
        return started

    def loss_take(level, started):
        base = (0, 2, 6, 10)[level]
        for c in started:
            c.wait()
        total = loss_in[base]
        for d in range(len(started)):
            total = total + loss_in[base + 1 + d]
        return total

    loss_open = loss_send(0, loss_value)

    running = [None] * len(plans)
    for level in range(3):
        for k, (off, size, levels) in enumerate(plans):
            a, n, u = levels[level]
            send, recv, total, gather = parts[k][level]
            me = at[a]
            if level == 0:
                first[k].wait()
                send[...] = (p_ref[core, off : off + size] + core_in[off : off + size]).astype(jnp.bfloat16)
            else:
                ua = levels[level - 1][1:]
                prev_n, prev_u = ua
                pa = levels[level - 1][0]
                psend, precv, ptotal, _ = parts[k][level - 1]
                for c in running[k]:
                    c.wait_recv()
                base = at[pa] * prev_u
                if level == 1:
                    value = p_ref[core, pl.ds(off + base, prev_u)] + core_in[pl.ds(off + base, prev_u)]
                else:
                    value = ptotal[pl.ds(base, prev_u)]
                for d in range(prev_n - 1):
                    value = value + precv[d].astype(jnp.float32)
                total[0:prev_u] = value
                if n * u > prev_u:
                    total[prev_u:] = jnp.zeros((n * u - prev_u, 16, 128), jnp.float32)
                send[...] = total[...].astype(jnp.bfloat16)
            started = []
            for d in range(1, n):
                p = (me + d) % n
                c = remote(
                    send.at[pl.ds(p * u, u)],
                    recv.at[d - 1],
                    rs_s.at[k, level, d - 1],
                    rs_r.at[k, level, d - 1],
                    device_at(a, p),
                )
                c.start()
                started.append(c)
            running[k] = started
            open_copies += started
        loss_value = loss_take(level, loss_open)
        loss_open = loss_send(level + 1, loss_value)

    for level in (2, 1, 0):
        for k, (off, size, levels) in enumerate(plans):
            a, n, u = levels[level]
            send, recv, total, gather = parts[k][level]
            me = at[a]
            target = g_ref.at[core] if level == 0 else gather
            shift = off if level == 0 else 0
            mine = pl.ds(shift + me * u, u)
            if level == 2:
                for c in running[k]:
                    c.wait_recv()
                value = total[pl.ds(me * u, u)]
                for d in range(n - 1):
                    value = value + recv[d].astype(jnp.float32)
                target[mine] = value.astype(jnp.bfloat16)
                source = target.at[mine]
            else:
                below = parts[k][level + 1][3]
                for c in running[k]:
                    c.wait_recv()
                target[mine] = below[0:u]
                source = below.at[pl.ds(0, u)]
            started = []
            for d in range(1, n):
                c = remote(
                    source,
                    target.at[mine],
                    ag_s.at[k, level, d - 1],
                    ag_r.at[k, level, d - 1],
                    device_at(a, (me + d) % n),
                )
                c.start()
                started.append(c)
            running[k] = started
            open_copies += started
            if level == 0:
                c = remote(
                    g_ref.at[core, mine], g_ref.at[core, mine], cs2.at[k, 0], cr2.at[k, 0], sibling
                )
                c.start()
                open_copies.append(c)
                running[k] = (started, [c])
    loss_out[...] = loss_take(3, loss_open)
    last = []
    for d in range(1, 4):
        for k, (off, size, levels) in enumerate(plans):
            a, n, u = levels[0]
            for dd in range(d, d + 1) if d < 3 else range(3, n):
                if dd >= n:
                    continue
                started, sent = running[k]
                started[dd - 1].wait_recv()
                src = (at[a] + n - dd) % n
                piece = pl.ds(off + src * u, u)
                c = remote(g_ref.at[core, piece], g_ref.at[core, piece], cs2.at[k, dd], cr2.at[k, dd], sibling)
                c.start()
                sent.append(c)
                open_copies.append(c)
    for k in range(len(plans)):
        for c in running[k][1]:
            c.wait_recv()
    for c in open_copies:
        c.wait_send()


def total_of(partial, loss):
    plans = steps_of()
    scratch = [pltpu.VMEM((UNITS, 16, 128), jnp.float32)]
    for off, size, levels in plans:
        for a, n, u in levels:
            scratch += [
                pltpu.VMEM((n * u, 16, 128), jnp.bfloat16),
                pltpu.VMEM((n - 1, u, 16, 128), jnp.bfloat16),
                pltpu.VMEM((n * u, 16, 128), jnp.float32),
                pltpu.VMEM((n * u, 16, 128), jnp.bfloat16),
            ]
    scratch += [
        pltpu.VMEM((18, 8, 128), jnp.float32),
        pltpu.SemaphoreType.DMA((3,)),
        pltpu.SemaphoreType.DMA((3,)),
        pltpu.SemaphoreType.DMA((3, 8)),
        pltpu.SemaphoreType.DMA((3, 8)),
        pltpu.SemaphoreType.DMA((3, 3, 7)),
        pltpu.SemaphoreType.DMA((3, 3, 7)),
        pltpu.SemaphoreType.DMA((3, 3, 7)),
        pltpu.SemaphoreType.DMA((3, 3, 7)),
        pltpu.SemaphoreType.DMA((14,)),
        pltpu.SemaphoreType.DMA((14,)),
    ]
    vmem = pl.BlockSpec(memory_space=pltpu.VMEM)
    return pl.pallas_call(
        total_kernel,
        out_shape=(
            jax.ShapeDtypeStruct((2, UNITS, 16, 128), jnp.bfloat16),
            jax.ShapeDtypeStruct((8, 128), jnp.float32),
        ),
        in_specs=[vmem, vmem],
        out_specs=(vmem, vmem),
        scratch_shapes=scratch,
        compiler_params=pltpu.CompilerParams(
            collective_id=0, has_side_effects=True, vmem_limit_bytes=48 * 1024 * 1024
        ),
    )(partial, loss)


def unpack_kernel(g_ref, up_ref, down_ref, head_ref, kern_ref, gain_ref, small):
    for m, out in enumerate((up_ref, down_ref)):
        for j in range(MAIN_COLS):
            piece = g_ref[m, pl.ds(j, MAIN_ROWS, stride=MAIN_COLS)].astype(jnp.float32)
            out[0:640, j * 128 : (j + 1) * 128] = piece.reshape(640, 128)
        for j in range(SMALL_COLS):
            piece = g_ref[m, pl.ds(MAIN + j, SMALL_ROWS, stride=SMALL_COLS)].astype(jnp.float32)
            small[m, :, j * 128 : (j + 1) * 128] = piece.reshape(64, 128)
    head_ref[0:64, :] = small[0, :, 0:641]
    head_ref[64:72, :] = small[1, 0:8, 0:641]
    kern_ref[...] = small[1, 8:33, 0:641]
    gain_ref[...] = small[1, 33:34, 0:641]
    for m, out in enumerate((up_ref, down_ref)):
        r = 34 + 5 * m
        edge = small[1, 32:56, :]
        cols = jnp.transpose(edge)[0:641, r - 32 : r - 30]
        out[:, 1280:1282] = cols
        out[640:641, 0:640] = small[1, r + 2 : r + 3, 0:640]
        out[640:641, 640:1280] = small[1, r + 3 : r + 4, 0:640]
        out[640:641, 1280:1282] = small[1, r + 4 : r + 5, 0:2]


def unpacked(g):
    vmem = pl.BlockSpec(memory_space=pltpu.VMEM)
    f32 = jnp.float32
    return pl.pallas_call(
        unpack_kernel,
        out_shape=(
            jax.ShapeDtypeStruct((641, 1282), f32),
            jax.ShapeDtypeStruct((641, 1282), f32),
            jax.ShapeDtypeStruct((72, 641), f32),
            jax.ShapeDtypeStruct((25, 641), f32),
            jax.ShapeDtypeStruct((1, 641), f32),
        ),
        in_specs=[vmem],
        out_specs=(vmem,) * 5,
        scratch_shapes=[pltpu.VMEM((2, 64, 768), f32)],
        compiler_params=pltpu.CompilerParams(vmem_limit_bytes=48 * 1024 * 1024),
    )(g)


def packed(grad_kernel, grad_gain, grad_up, grad_down_t, grad_head_t):
    def main(g):
        return g[:640, :1280].reshape(40, 16, 10, 128).transpose(0, 2, 1, 3).reshape(400, 16, 128)

    def rows(a):
        return jnp.pad(a, ((0, 0), (0, 768 - a.shape[1])))

    def edges(g):
        return [
            rows(g[:, 1280:1282].T),
            rows(g[640:641, 0:640]),
            rows(g[640:641, 640:1280]),
            rows(g[640:641, 1280:1282]),
        ]

    def small(pieces):
        s = jnp.concatenate(pieces, axis=0)
        s = jnp.pad(s, ((0, 64 - s.shape[0]), (0, 0)))
        return s.reshape(4, 16, 6, 128).transpose(0, 2, 1, 3).reshape(24, 16, 128)

    s0 = small([rows(grad_head_t[:64])])
    s1 = small([rows(grad_head_t[64:]), rows(grad_kernel), rows(grad_gain[None])] + edges(grad_up) + edges(grad_down_t))
    return jnp.stack(
        [jnp.concatenate([main(grad_up), s0]), jnp.concatenate([main(grad_down_t), s1])]
    )


MEM = ("mem_0", "mem_1", "mem_2")
LAT = ("lat_0", "lat_1")
MEM_LAT = ("mem_0", "mem_1", "mem_2", "lat_0", "lat_1")


DELTA = 0.1
EPSILON = 1e-05


def extended(cells, sides, width):
    for axis, dim in sides:
        count = lax.axis_size(axis)
        ends = count - 1
        head = lax.slice_in_dim(cells, 0, width, axis=dim)
        tail = lax.slice_in_dim(cells, cells.shape[dim] - width, cells.shape[dim], axis=dim)
        cells = jnp.concatenate(
            [
                lax.ppermute(tail, axis, [(i, (i + 1) % count) for i in range(ends)]),
                cells,
                lax.ppermute(head, axis, [((i + 1) % count, i) for i in range(ends)]),
            ],
            axis=dim,
        )
    return cells


def cut_along(shard, dim, count):
    shape = shard.shape
    pieces = shard.reshape(*shape[:dim], count, shape[dim] // count, *shape[dim + 1 :])
    return jnp.moveaxis(pieces, dim, 0)


def joined_along(pieces, dim):
    pieces = jnp.moveaxis(pieces, 0, dim)
    shape = pieces.shape
    return pieces.reshape(*shape[:dim], shape[dim] * shape[dim + 1], *shape[dim + 2 :])


def moved_by_axis(pieces, axes, sequence):
    shape = [lax.axis_size(a) for a in axes]
    pieces = pieces.reshape(*shape, *pieces.shape[1:])
    for k in sequence:
        pieces = lax.all_to_all(pieces, axes[k], split_axis=k, concat_axis=k, tiled=True)
    return pieces.reshape(-1, *pieces.shape[len(axes) :])


def core_and_chips(shard, groups, sequence, split_dim, concat_dim):
    count = lax.axis_size(groups[0]) * lax.axis_size(groups[1])
    pieces = cut_along(shard, split_dim, count)
    return joined_along(moved_by_axis(pieces, groups, sequence), concat_dim)


def softened_absolute(diff):
    return jnp.sqrt(diff * diff + DELTA * DELTA) - DELTA


def softened_derivative(diff):
    return diff / jnp.sqrt(diff * diff + DELTA * DELTA)


def gelu_parts(before_activation):
    cumul = 0.5 * (1.0 + jax.scipy.special.erf(before_activation / math.sqrt(2.0)))
    density = jnp.exp(-0.5 * before_activation * before_activation) / math.sqrt(2.0 * math.pi)
    return (before_activation * cumul, cumul + before_activation * density)


def leading_product(left, right):
    return lax.dot_general(
        left, right, (((0,), (0,)), ((), ())), preferred_element_type=jnp.float32
    )


def tail_dot(left, right):
    return lax.dot_general(
        left, right, (((1,), (1,)), ((), ())), preferred_element_type=jnp.float32
    )


def stencil(window, kernel, height):
    result = jnp.zeros((window.shape[0], height, window.shape[2]), jnp.float32)
    for col_off in range(5):
        shifted = jnp.roll(window, 2 - col_off, axis=2)
        for row_off in range(5):
            result = (
                result
                + kernel[row_off * 5 + col_off][:, None, None]
                * shifted[:, row_off : row_off + height]
            )
    return result


def kernel_grad(window, upstream, height):
    terms = [None] * 25
    for col_off in range(5):
        shifted = jnp.roll(window, 2 - col_off, axis=2)
        for row_off in range(5):
            terms[row_off * 5 + col_off] = jnp.sum(
                upstream * shifted[:, row_off : row_off + height], axis=(1, 2)
            )
    return jnp.stack(terms)


def forward_apply(field, window, kernel, gain, up_weight, down_weight, field_head_weight):
    height = field.shape[1]
    channels = field.shape[0]
    summed = (field + stencil(window, kernel, height)).reshape(channels, -1)
    center = summed - jnp.mean(summed, axis=0)
    inverse_norm = lax.rsqrt(jnp.mean(center * center, axis=0) + EPSILON)
    normalized_input = center * inverse_norm
    gain_scaled = (normalized_input * gain[:, None]).astype(jnp.bfloat16)
    before_activation = leading_product(up_weight, gain_scaled)
    activ, unused = gelu_parts(before_activation)
    hidden_activation = activ.astype(jnp.bfloat16)
    output = summed + leading_product(down_weight, hidden_activation)
    rounded_values = output.astype(jnp.bfloat16)
    member_prediction = leading_product(field_head_weight, rounded_values)
    return (
        member_prediction,
        (
            normalized_input,
            inverse_norm,
            gain_scaled,
            before_activation,
            hidden_activation,
            rounded_values,
        ),
    )


def backward(window, stored_residuals, cotangent, gain, up_weight, down_weight, field_head_weight):
    (
        normalized_input,
        inverse_norm,
        gain_scaled,
        before_activation,
        hidden_activation,
        rounded_values,
    ) = stored_residuals
    height = window.shape[1] - 4
    grad_head = tail_dot(rounded_values, cotangent)
    d_output = jnp.dot(field_head_weight, cotangent, preferred_element_type=jnp.float32)
    d_round = d_output.astype(jnp.bfloat16)
    grad_down = tail_dot(hidden_activation, d_round)
    d_hidden = jnp.dot(down_weight, d_round, preferred_element_type=jnp.float32)
    unused, slope = gelu_parts(before_activation)
    d_preact = (d_hidden * slope).astype(jnp.bfloat16)
    grad_up = tail_dot(gain_scaled, d_preact)
    d_scaled = jnp.dot(up_weight, d_preact, preferred_element_type=jnp.float32)
    grad_gain = jnp.sum(d_scaled * normalized_input, axis=1)
    d_normed = d_scaled * gain[:, None]
    d_summed = d_output + inverse_norm * (
        d_normed
        - jnp.mean(d_normed, axis=0)
        - normalized_input * jnp.mean(d_normed * normalized_input, axis=0)
    )
    upstream = d_summed.reshape(window.shape[0], height, window.shape[2])
    grad_kernel = kernel_grad(window, upstream, height)
    return (grad_kernel, grad_gain, grad_up, grad_down, grad_head)


def local(
    state, conv_kernel, norm_gain, up_weight, down_weight, field_head_weight, target, field_weight
):
    field = state[0]
    member_states = lax.axis_size(MEM)
    height = field.shape[1]
    nlat = lax.axis_size(LAT) * height
    width = field.shape[2]
    nfields = target.shape[0]
    window = extended(field, ((LAT, 1),), 2)
    member_prediction, stored_residuals = forward_apply(
        field, window, conv_kernel, norm_gain, up_weight, down_weight, field_head_weight
    )
    grid_cell_values = member_prediction.shape[1]
    observed_target = target.reshape(nfields, grid_cell_values)
    row_float = (lax.axis_index(LAT) * height + jnp.arange(height)).astype(jnp.float32)
    area_rows = jnp.cos(0.5 * math.pi * ((row_float + 0.5) / nlat - 1.0))
    area = jnp.repeat(area_rows, width)
    member_count = nlat * width * nfields
    scale_grad = 1.0 / (member_states * math.sqrt(member_count))
    pair_norm = 2.0 * member_states * (member_states - 1)
    block = grid_cell_values // member_states
    outgoing = member_prediction.reshape(1, nfields, member_states, block)
    gathered_members = core_and_chips(
        outgoing, (("mem_0", "mem_1"), "mem_2"), (1, 0), 2, 0
    ).reshape(member_states, nfields, block)
    mine = lax.axis_index(MEM)
    truth_block = lax.dynamic_index_in_dim(
        observed_target.reshape(nfields, member_states, block), mine, 1, keepdims=False
    )
    area_block = lax.dynamic_index_in_dim(
        area.reshape(member_states, block), mine, 0, keepdims=False
    )
    differences = gathered_members[:, None] - gathered_members[None]
    ensemble_spread = (
        jnp.mean(softened_absolute(gathered_members - truth_block[None]), axis=0)
        - jnp.sum(softened_absolute(differences), axis=(0, 1)) / pair_norm
    )
    partial_value = jnp.sum(field_weight[:, None] * area_block[None, :] * ensemble_spread)
    pairwise_derivatives = jnp.sum(softened_derivative(differences), axis=1)
    member_cot = (
        field_weight[None, :, None]
        * area_block[None, None, :]
        * (
            softened_derivative(gathered_members - truth_block[None])
            - pairwise_derivatives / (member_states - 1)
        )
        * scale_grad
    )
    cot_rounded = member_cot.astype(jnp.bfloat16).reshape(member_states, nfields, 1, block)
    returned = core_and_chips(cot_rounded, (("mem_0", "mem_1"), "mem_2"), (1, 0), 0, 2)
    cotangent = returned.reshape(nfields, grid_cell_values)
    grads = backward(
        window, stored_residuals, cotangent, norm_gain, up_weight, down_weight, field_head_weight
    )
    grads_t = (grads[0], grads[1], grads[2], grads[3].T, grads[4].T)
    loss_tile = jnp.full((8, 128), partial_value / member_count, jnp.float32)
    total, loss_total = total_of(packed(*grads_t), loss_tile)
    up, down_t, head_t, kern, gain_row = unpacked(total)
    return (loss_total[0, 0], kern, gain_row[0], up, down_t.T, head_t.T)


def solution(mesh):
    finer = Mesh(mesh.devices.reshape(4, 2, 2, 2, 8), ("mem_0", "mem_1", "mem_2", "lat_0", "lat_1"))
    in_specs = (P(MEM, None, LAT, None), P(), P(), P(), P(), P(), P(None, LAT, None), P())
    out_specs = (P(), P(), P(), P(), P(), P())
    return jax.shard_map(local, mesh=finer, in_specs=in_specs, out_specs=out_specs, check_vma=False)
```

```python
import functools
import math

import jax
import jax.numpy as jnp
import numpy as np
from jax import lax
from jax.experimental import pallas as pl
from jax.experimental.pallas import tpu as pltpu
from jax.sharding import Mesh
from jax.sharding import PartitionSpec as P

AXES = ("mem_0", "mem_1", "mem_2", "lat_0", "lat_1")
MESH_ID = pl.DeviceIdType.MESH
MAIN_ROWS, MAIN_COLS = 40, 10
MAIN = MAIN_ROWS * MAIN_COLS
SMALL_ROWS, SMALL_COLS = 4, 6
UNITS = MAIN + SMALL_ROWS * SMALL_COLS
PARTS = ((168, "xyz"), (168, "yxz"), (88, "zxy"))
SIZE = {"x": 4, "y": 4, "z": 8}


def place():
    x = lax.axis_index("mem_0")
    y = lax.axis_index("lat_0") * 2 + lax.axis_index("mem_1")
    z = lax.axis_index("lat_1")
    return {"x": x, "y": y, "z": z}


def device_at(axis, p):
    if axis == "x":
        return {"mem_0": p}
    if axis == "y":
        return {"lat_0": p // 2, "mem_1": p % 2}
    return {"lat_1": p}


def steps_of():
    plans, at = [], 0
    for size, order in PARTS:
        left, levels = size, []
        for a in order:
            left = -(-left // SIZE[a])
            levels.append((a, SIZE[a], left))
        plans.append((at, size, levels))
        at += size
    return plans


def peers_of(at):
    out = []
    for a in "xyz":
        for d in range(1, SIZE[a]):
            out.append(device_at(a, (at[a] + d) % SIZE[a]))
    return out


def total_kernel(p_ref, loss_ref, g_ref, loss_out, *scratch):
    plans = steps_of()
    at = place()
    core = lax.axis_index("mem_2")
    sibling = {"mem_2": 1 - core}
    it = iter(scratch)
    core_in = next(it)
    parts = []
    for _ in plans:
        parts.append([[next(it) for _ in range(4)] for _ in range(3)])
    loss_in = next(it)
    cs, cr, cs2, cr2 = next(it), next(it), next(it), next(it)
    rs_s, rs_r, ag_s, ag_r = next(it), next(it), next(it), next(it)
    ls, lr = next(it), next(it)

    barrier = pltpu.get_barrier_semaphore()
    everyone = [sibling] + peers_of(at)
    for dev in everyone:
        pl.semaphore_signal(barrier, inc=1, device_id=dev, device_id_type=MESH_ID)
    pl.semaphore_wait(barrier, len(everyone))

    def remote(src, dst, s, r, dev):
        return pltpu.make_async_remote_copy(
            src_ref=src, dst_ref=dst, send_sem=s, recv_sem=r, device_id=dev, device_id_type=MESH_ID
        )

    first = []
    for k, (off, size, levels) in enumerate(plans):
        c = remote(
            p_ref.at[1 - core, pl.ds(off, size)], core_in.at[pl.ds(off, size)], cs.at[k], cr.at[k], sibling
        )
        c.start()
        first.append(c)
    open_copies = []
    loss_steps = [("c", [sibling])] + [
        (a, [device_at(a, (at[a] + d) % SIZE[a]) for d in range(1, SIZE[a])]) for a in "xyz"
    ]
    loss_value = loss_ref[...]

    def loss_send(level, value):
        base = (0, 2, 6, 10)[level]
        sbase = (0, 1, 4, 7)[level]
        loss_in[base] = value
        started = []
        for d, dev in enumerate(loss_steps[level][1]):
            c = remote(loss_in.at[base], loss_in.at[base + 1 + d], ls.at[sbase + d], lr.at[sbase + d], dev)
            c.start()
            started.append(c)
        return started

    def loss_take(level, started):
        base = (0, 2, 6, 10)[level]
        for c in started:
            c.wait()
        total = loss_in[base]
        for d in range(len(started)):
            total = total + loss_in[base + 1 + d]
        return total

    loss_open = loss_send(0, loss_value)

    running = [None] * len(plans)
    for level in range(3):
        for k, (off, size, levels) in enumerate(plans):
            a, n, u = levels[level]
            send, recv, total, gather = parts[k][level]
            me = at[a]
            if level == 0:
                first[k].wait()
                send[...] = (p_ref[core, off : off + size] + core_in[off : off + size]).astype(jnp.bfloat16)
            else:
                ua = levels[level - 1][1:]
                prev_n, prev_u = ua
                pa = levels[level - 1][0]
                psend, precv, ptotal, _ = parts[k][level - 1]
                for c in running[k]:
                    c.wait_recv()
                base = at[pa] * prev_u
                if level == 1:
                    value = p_ref[core, pl.ds(off + base, prev_u)] + core_in[pl.ds(off + base, prev_u)]
                else:
                    value = ptotal[pl.ds(base, prev_u)]
                for d in range(prev_n - 1):
                    value = value + precv[d].astype(jnp.float32)
                total[0:prev_u] = value
                if n * u > prev_u:
                    total[prev_u:] = jnp.zeros((n * u - prev_u, 16, 128), jnp.float32)
                send[...] = total[...].astype(jnp.bfloat16)
            started = []
            for d in range(1, n):
                p = (me + d) % n
                c = remote(
                    send.at[pl.ds(p * u, u)],
                    recv.at[d - 1],
                    rs_s.at[k, level, d - 1],
                    rs_r.at[k, level, d - 1],
                    device_at(a, p),
                )
                c.start()
                started.append(c)
            running[k] = started
            open_copies += started
        loss_value = loss_take(level, loss_open)
        loss_open = loss_send(level + 1, loss_value)

    for level in (2, 1, 0):
        for k, (off, size, levels) in enumerate(plans):
            a, n, u = levels[level]
            send, recv, total, gather = parts[k][level]
            me = at[a]
            target = g_ref.at[core] if level == 0 else gather
            shift = off if level == 0 else 0
            mine = pl.ds(shift + me * u, u)
            if level == 2:
                for c in running[k]:
                    c.wait_recv()
                value = total[pl.ds(me * u, u)]
                for d in range(n - 1):
                    value = value + recv[d].astype(jnp.float32)
                target[mine] = value.astype(jnp.bfloat16)
                source = target.at[mine]
            else:
                below = parts[k][level + 1][3]
                for c in running[k]:
                    c.wait_recv()
                target[mine] = below[0:u]
                source = below.at[pl.ds(0, u)]
            started = []
            for d in range(1, n):
                c = remote(
                    source,
                    target.at[mine],
                    ag_s.at[k, level, d - 1],
                    ag_r.at[k, level, d - 1],
                    device_at(a, (me + d) % n),
                )
                c.start()
                started.append(c)
            running[k] = started
            open_copies += started
            if level == 0:
                c = remote(
                    g_ref.at[core, mine], g_ref.at[core, mine], cs2.at[k, 0], cr2.at[k, 0], sibling
                )
                c.start()
                open_copies.append(c)
                running[k] = (started, [c])
    loss_out[...] = loss_take(3, loss_open)
    last = []
    for d in range(1, 4):
        for k, (off, size, levels) in enumerate(plans):
            a, n, u = levels[0]
            for dd in range(d, d + 1) if d < 3 else range(3, n):
                if dd >= n:
                    continue
                started, sent = running[k]
                started[dd - 1].wait_recv()
                src = (at[a] + n - dd) % n
                piece = pl.ds(off + src * u, u)
                c = remote(g_ref.at[core, piece], g_ref.at[core, piece], cs2.at[k, dd], cr2.at[k, dd], sibling)
                c.start()
                sent.append(c)
                open_copies.append(c)
    for k in range(len(plans)):
        for c in running[k][1]:
            c.wait_recv()
    for c in open_copies:
        c.wait_send()


def total_of(partial, loss):
    plans = steps_of()
    scratch = [pltpu.VMEM((UNITS, 16, 128), jnp.float32)]
    for off, size, levels in plans:
        for a, n, u in levels:
            scratch += [
                pltpu.VMEM((n * u, 16, 128), jnp.bfloat16),
                pltpu.VMEM((n - 1, u, 16, 128), jnp.bfloat16),
                pltpu.VMEM((n * u, 16, 128), jnp.float32),
                pltpu.VMEM((n * u, 16, 128), jnp.bfloat16),
            ]
    scratch += [
        pltpu.VMEM((18, 8, 128), jnp.float32),
        pltpu.SemaphoreType.DMA((3,)),
        pltpu.SemaphoreType.DMA((3,)),
        pltpu.SemaphoreType.DMA((3, 8)),
        pltpu.SemaphoreType.DMA((3, 8)),
        pltpu.SemaphoreType.DMA((3, 3, 7)),
        pltpu.SemaphoreType.DMA((3, 3, 7)),
        pltpu.SemaphoreType.DMA((3, 3, 7)),
        pltpu.SemaphoreType.DMA((3, 3, 7)),
        pltpu.SemaphoreType.DMA((14,)),
        pltpu.SemaphoreType.DMA((14,)),
    ]
    vmem = pl.BlockSpec(memory_space=pltpu.VMEM)
    return pl.pallas_call(
        total_kernel,
        out_shape=(
            jax.ShapeDtypeStruct((2, UNITS, 16, 128), jnp.bfloat16),
            jax.ShapeDtypeStruct((8, 128), jnp.float32),
        ),
        in_specs=[vmem, vmem],
        out_specs=(vmem, vmem),
        scratch_shapes=scratch,
        compiler_params=pltpu.CompilerParams(
            collective_id=0, has_side_effects=True, vmem_limit_bytes=48 * 1024 * 1024
        ),
    )(partial, loss)


def unpack_kernel(g_ref, up_ref, down_ref, head_ref, kern_ref, gain_ref, small):
    for m, out in enumerate((up_ref, down_ref)):
        for j in range(MAIN_COLS):
            piece = g_ref[m, j * MAIN_ROWS : (j + 1) * MAIN_ROWS].astype(jnp.float32)
            out[0:640, j * 128 : (j + 1) * 128] = piece.reshape(640, 128)
        for j in range(SMALL_COLS):
            piece = g_ref[m, MAIN + j * SMALL_ROWS : MAIN + (j + 1) * SMALL_ROWS].astype(jnp.float32)
            small[m, :, j * 128 : (j + 1) * 128] = piece.reshape(64, 128)
    head_ref[0:64, :] = small[0, :, 0:641]
    head_ref[64:72, :] = small[1, 0:8, 0:641]
    kern_ref[...] = small[1, 8:33, 0:641]
    gain_ref[...] = small[1, 33:34, 0:641]
    for m, out in enumerate((up_ref, down_ref)):
        r = 34 + 5 * m
        edge = small[1, 32:56, :]
        cols = jnp.transpose(edge)[0:641, r - 32 : r - 30]
        out[:, 1280:1282] = cols
        out[640:641, 0:640] = small[1, r + 2 : r + 3, 0:640]
        out[640:641, 640:1280] = small[1, r + 3 : r + 4, 0:640]


def unpacked(g):
    vmem = pl.BlockSpec(memory_space=pltpu.VMEM)
    f32 = jnp.float32
    return pl.pallas_call(
        unpack_kernel,
        out_shape=(
            jax.ShapeDtypeStruct((641, 1282), f32),
            jax.ShapeDtypeStruct((641, 1282), f32),
            jax.ShapeDtypeStruct((72, 641), f32),
            jax.ShapeDtypeStruct((25, 641), f32),
            jax.ShapeDtypeStruct((1, 641), f32),
        ),
        in_specs=[vmem],
        out_specs=(vmem,) * 5,
        scratch_shapes=[pltpu.VMEM((2, 64, 768), f32)],
        compiler_params=pltpu.CompilerParams(vmem_limit_bytes=48 * 1024 * 1024),
    )(g)


ROWS = 2
LON = 160
CELLS = ROWS * LON
C = 641
HID = 1282
FIELDS = 72
MEMBERS = 16
NLAT = 32
BLOCK = CELLS // MEMBERS
CHUNKS = 6
DELTA = 0.1
EPSILON = 1e-05


def contract(left, right, dims):
    return lax.dot_general(left, right, ((dims[:1], dims[1:]), ((), ())), preferred_element_type=jnp.float32)


def put(ref, value):
    for c in range(CHUNKS - 1):
        ref[c] = value[:, c * 128 : (c + 1) * 128]
    ref[CHUNKS - 1, :, 0:1] = value[:, 640:641]


def member_device(m):
    return {"mem_0": m // 4, "mem_1": (m // 2) % 2, "mem_2": m % 2}


def step_kernel(
    state,
    conv_kernel,
    gain,
    up,
    down_t,
    head_t,
    target,
    field_weight,
    area,
    p_ref,
    loss_ref,
    win,
    ck,
    gn,
    su,
    nr,
    inv,
    sc,
    rd,
    pre,
    slope,
    hid,
    hp,
    fcs,
    fs,
    fr,
    truth,
    co_s,
    co_r,
    co,
    dp,
    dsum,
    dsc,
    small,
    halo_s,
    halo_r,
    fc_s,
    fc_r,
    ct_s,
    ct_r,
):
    f32, bf16 = jnp.float32, jnp.bfloat16
    lat = lax.axis_index("lat_0") * 8 + lax.axis_index("lat_1")
    member = lax.axis_index("mem_0") * 4 + lax.axis_index("mem_1") * 2 + lax.axis_index("mem_2")

    def lat_device(d):
        p = (lat + d) % 16
        return {"lat_0": p // 8, "lat_1": p % 8}

    above, below = lat_device(1), lat_device(15)
    others = [member_device((member + d) % MEMBERS) for d in range(1, MEMBERS)]
    barrier = pltpu.get_barrier_semaphore()
    for dev in [above, below] + others:
        pl.semaphore_signal(barrier, inc=1, device_id=dev, device_id_type=MESH_ID)

    def remote(src, dst, s, r, dev):
        return pltpu.make_async_remote_copy(
            src_ref=src, dst_ref=dst, send_sem=s, recv_sem=r, device_id=dev, device_id_type=MESH_ID
        )

    win[CHUNKS - 1, 2:4] = jnp.zeros((2, 176, 128), f32)
    for c in range(CHUNKS - 1):
        win[c, 2:4, 8:168, :] = state[:, :, c * 128 : (c + 1) * 128]
    win[CHUNKS - 1, 2:4, 8:168, 0:1] = state[:, :, 640:641]
    pl.semaphore_wait(barrier, 2 + len(others))

    def halo(c):
        mine = win.at[c, 2:4, 8:168]
        return (
            remote(mine, win.at[c, 0:2, 8:168], halo_s.at[0, c], halo_r.at[0, c], above),
            remote(mine, win.at[c, 4:6, 8:168], halo_s.at[1, c], halo_r.at[1, c], below),
        )

    @pl.loop(0, CHUNKS)
    def _(c):
        for copy in halo(c):
            copy.start()

    ck[CHUNKS - 1] = jnp.zeros((25, 128), f32)
    put(ck, conv_kernel[...])
    gn[CHUNKS - 1] = jnp.zeros((1, 128), f32)
    put(gn, gain[...])
    hp[:, 640:768] = jnp.zeros((FIELDS, 128), bf16)
    hp[:, 0:641] = head_t[...]
    rd[:, 640:768] = jnp.zeros((CELLS, 128), bf16)
    su[CHUNKS - 1] = jnp.zeros((CELLS, 128), f32)
    dsc[CHUNKS - 1] = jnp.zeros((CELLS, 128), f32)
    small[...] = jnp.zeros((2, CHUNKS, 64, 128), f32)
    for i in range(ROWS):
        columns = jnp.transpose(target[:, i, :])
        for b in range(MEMBERS // ROWS):
            truth[i * (MEMBERS // ROWS) + b] = columns[b * BLOCK : (b + 1) * BLOCK, :]

    def wrap(c, rows):
        win[c, rows, 6:8, :] = win[c, rows, 166:168, :]
        win[c, rows, 168:170, :] = win[c, rows, 8:10, :]

    def taps(c, i, rows, acc):
        for a in rows:
            for b in range(5):
                acc = acc + ck[c, 5 * a + b : 5 * a + b + 1, :] * win[c, i + a, 6 + b : 166 + b, :]
        return acc

    own = ((2, 3), (1, 2))
    met = ((0, 1, 4), (0, 3, 4))

    @pl.loop(0, CHUNKS)
    def _(c):
        wrap(c, slice(2, 4))
        for i in range(ROWS):
            su[c, i * LON : (i + 1) * LON] = taps(c, i, own[i], win[c, 2 + i, 8:168, :])

    @pl.loop(0, CHUNKS)
    def _(c):
        for copy in halo(c):
            copy.wait_recv()

        @pl.when(lat == 0)
        def _():
            win[c, 0:2] = jnp.zeros((2, 176, 128), f32)

        @pl.when(lat == 15)
        def _():
            win[c, 4:6] = jnp.zeros((2, 176, 128), f32)

        wrap(c, slice(0, 2))
        wrap(c, slice(4, 6))
        for i in range(ROWS):
            su[c, i * LON : (i + 1) * LON] = taps(c, i, met[i], su[c, i * LON : (i + 1) * LON])

    total = su[0]
    for c in range(1, CHUNKS):
        total = total + su[c]
    mean = jnp.sum(total, axis=1, keepdims=True) * (1.0 / C)
    first_lane = (lax.broadcasted_iota(jnp.int32, (CELLS, 128), 1) < 1).astype(f32)
    square = jnp.zeros((CELLS, 128), f32)
    for c in range(CHUNKS):
        center = su[c] - mean
        if c == CHUNKS - 1:
            center = center * first_lane
        nr[c] = center
        square = square + center * center
    inverse = lax.rsqrt(jnp.sum(square, axis=1, keepdims=True) * (1.0 / C) + EPSILON)
    inv[...] = inverse
    for c in range(CHUNKS):
        normed = nr[c] * inverse
        nr[c] = normed
        sc[:, c * 128 : (c + 1) * 128] = (normed * gn[c]).astype(bf16)

    pre[...] = jnp.dot(sc[:, 0:C], up[...], preferred_element_type=f32)

    @pl.loop(0, CELLS // 16)
    def _(r):
        rows = pl.ds(pl.multiple_of(r * 16, 16), 16)
        x = pre[rows, :]
        cumul = 0.5 * (1.0 + lax.erf(x * (1.0 / math.sqrt(2.0))))
        density = jnp.exp(-0.5 * x * x) * (1.0 / math.sqrt(2.0 * math.pi))
        hid[rows, :] = (x * cumul).astype(bf16)
        slope[rows, :] = cumul + x * density

    mlp = contract(hid[...], down_t[...], (1, 1))
    for c in range(CHUNKS - 1):
        at = slice(c * 128, (c + 1) * 128)
        rd[:, at] = (su[c] + mlp[:, at]).astype(bf16)
    rd[:, 640:641] = (su[CHUNKS - 1, :, 0:1] + mlp[:, 640:641]).astype(bf16)
    fcs[...] = contract(rd[...], hp[...], (1, 1))

    for p in range(MEMBERS):
        fs[p] = fcs[p * BLOCK : (p + 1) * BLOCK, :]
    sent = []
    for d in range(1, MEMBERS):
        p = (member + d) % MEMBERS
        c = remote(fs.at[p], fr.at[member], fc_s.at[d - 1], fc_r.at[d - 1], others[d - 1])
        c.start()
        sent.append(c)
    fr[member] = fs[member]
    for c in sent:
        c.wait_recv()

    weight = field_weight[...] * area[pl.ds(2 * lat + member // (MEMBERS // ROWS), 1), 0:FIELDS]
    against = truth[member]
    members = fr[...]
    gap = members - against[None]
    square = gap * gap + DELTA * DELTA
    root = lax.rsqrt(square)
    miss = jnp.sum(square * root - DELTA, axis=0)
    slope_miss = gap * root
    apart = jnp.zeros((BLOCK, FIELDS), f32)
    pull = jnp.zeros((MEMBERS, BLOCK, FIELDS), f32)
    for n in range(MEMBERS):
        gap = members - fr[n][None]
        square = gap * gap + DELTA * DELTA
        root = lax.rsqrt(square)
        apart = apart + jnp.sum(square * root - DELTA, axis=0)
        pull = pull + gap * root
    cells = NLAT * LON * FIELDS
    spread = miss * (1.0 / MEMBERS) - apart * (1.0 / (2.0 * MEMBERS * (MEMBERS - 1)))
    loss_ref[...] = jnp.full((8, 128), jnp.sum(weight * spread) * (1.0 / cells), f32)
    cotangent = weight[None] * (slope_miss - pull * (1.0 / (MEMBERS - 1))) * (1.0 / (MEMBERS * math.sqrt(cells)))
    co_s[...] = cotangent.astype(bf16)
    back = []
    for d in range(1, MEMBERS):
        p = (member + d) % MEMBERS
        c = remote(co_s.at[p], co_r.at[member], ct_s.at[d - 1], ct_r.at[d - 1], others[d - 1])
        c.start()
        back.append(c)
    co_r[member] = co_s[member]
    for c in back:
        c.wait_recv()
    for p in range(MEMBERS):
        fcs[p * BLOCK : (p + 1) * BLOCK, :] = co_r[p].astype(f32)
    co[...] = fcs[...].astype(bf16)

    d_output = jnp.dot(co[...], hp[...], preferred_element_type=f32)
    for c in range(CHUNKS):
        dsum[c] = d_output[:, c * 128 : (c + 1) * 128]
    d_round = d_output[:, 0:C].astype(bf16)
    pre[...] = jnp.dot(d_round, down_t[...], preferred_element_type=f32)

    @pl.loop(0, CELLS // 16)
    def _(r):
        rows = pl.ds(pl.multiple_of(r * 16, 16), 16)
        dp[rows, :] = (pre[rows, :] * slope[rows, :]).astype(bf16)

    def weight_grad(m, left, right_ref, edge_row):
        for q in range(5):
            part = contract(left, right_ref[:, q * 256 : (q + 1) * 256], (0, 0))
            for h in range(2):
                j = 2 * q + h
                lanes = slice(h * 128, (h + 1) * 128)
                p_ref[m, j * MAIN_ROWS : (j + 1) * MAIN_ROWS] = part[0:640, lanes].reshape(MAIN_ROWS, 16, 128)
                small[1, j % 5, edge_row + 2 + j // 5 : edge_row + 3 + j // 5, :] = part[640:641, lanes]
        edge = contract(right_ref[:, 1280:1282], left, (0, 0))
        for c in range(CHUNKS - 1):
            small[1, c, edge_row : edge_row + 2, :] = edge[:, c * 128 : (c + 1) * 128]
        small[1, CHUNKS - 1, edge_row : edge_row + 2, 0:1] = edge[:, 640:641]

    weight_grad(1, d_round, hid, 39)
    weight_grad(0, sc[:, 0:C], dp, 34)
    head_grad = contract(co[...], rd[...], (0, 0))
    for c in range(CHUNKS):
        small[0, c, 0:64, :] = head_grad[0:64, c * 128 : (c + 1) * 128]
        small[1, c, 0:8, :] = head_grad[64:72, c * 128 : (c + 1) * 128]
    put(dsc, contract(dp[...], up[...], (1, 1)))
    mean_a = jnp.zeros((CELLS, 128), f32)
    mean_b = jnp.zeros((CELLS, 128), f32)
    for c in range(CHUNKS):
        both = dsc[c] * nr[c]
        small[1, c, 33:34, :] = jnp.sum(both, axis=0, keepdims=True)
        mean_a = mean_a + dsc[c] * gn[c]
        mean_b = mean_b + both * gn[c]
    mean_a = jnp.sum(mean_a, axis=1, keepdims=True) * (1.0 / C)
    mean_b = jnp.sum(mean_b, axis=1, keepdims=True) * (1.0 / C)
    for c in range(CHUNKS):
        dsum[c] = dsum[c] + inv[...] * (dsc[c] * gn[c] - mean_a - nr[c] * mean_b)

    @pl.loop(0, CHUNKS)
    def _(c):
        for a in range(5):
            acc = [jnp.zeros((8, 128), f32) for _ in range(5)]
            for i in range(ROWS):
                for t in range(LON // 8):
                    d = dsum[c, i * LON + 8 * t : i * LON + 8 * t + 8, :]
                    for b in range(5):
                        acc[b] = acc[b] + d * win[c, i + a, 6 + b + 8 * t : 14 + b + 8 * t, :]
            for b in range(5):
                tap = 8 + 5 * a + b
                small[1, c, tap : tap + 1, :] = jnp.sum(acc[b], axis=0, keepdims=True)

    for m in range(2):
        for c in range(CHUNKS):
            p_ref[m, MAIN + c * SMALL_ROWS : MAIN + (c + 1) * SMALL_ROWS] = small[m, c].reshape(SMALL_ROWS, 16, 128)

    @pl.loop(0, CHUNKS)
    def _(c):
        for copy in halo(c):
            copy.wait_send()

    for c in sent + back:
        c.wait_send()


def gradients(state, conv_kernel, gain, up, down_t, head_t, target, field_weight, area):
    f32, bf16 = jnp.float32, jnp.bfloat16
    vmem = pl.BlockSpec(memory_space=pltpu.VMEM)
    V = pltpu.VMEM
    dma = pltpu.SemaphoreType.DMA
    return pl.pallas_call(
        step_kernel,
        out_shape=(
            jax.ShapeDtypeStruct((2, UNITS, 16, 128), f32),
            jax.ShapeDtypeStruct((8, 128), f32),
        ),
        in_specs=[vmem] * 9,
        out_specs=(vmem, vmem),
        scratch_shapes=[
            V((CHUNKS, 6, 176, 128), f32),
            V((CHUNKS, 25, 128), f32),
            V((CHUNKS, 1, 128), f32),
            V((CHUNKS, CELLS, 128), f32),
            V((CHUNKS, CELLS, 128), f32),
            V((CELLS, 1), f32),
            V((CELLS, 768), bf16),
            V((CELLS, 768), bf16),
            V((CELLS, HID), f32),
            V((CELLS, HID), f32),
            V((CELLS, HID), bf16),
            V((FIELDS, 768), bf16),
            V((CELLS, FIELDS), f32),
            V((MEMBERS, BLOCK, FIELDS), f32),
            V((MEMBERS, BLOCK, FIELDS), f32),
            V((MEMBERS, BLOCK, FIELDS), f32),
            V((MEMBERS, BLOCK, FIELDS), bf16),
            V((MEMBERS, BLOCK, FIELDS), bf16),
            V((CELLS, FIELDS), bf16),
            V((CELLS, HID), bf16),
            V((CHUNKS, CELLS, 128), f32),
            V((CHUNKS, CELLS, 128), f32),
            V((2, CHUNKS, 64, 128), f32),
            dma((2, CHUNKS)),
            dma((2, CHUNKS)),
            dma((MEMBERS - 1,)),
            dma((MEMBERS - 1,)),
            dma((MEMBERS - 1,)),
            dma((MEMBERS - 1,)),
        ],
        compiler_params=pltpu.CompilerParams(
            collective_id=1, has_side_effects=True, vmem_limit_bytes=56 * 1024 * 1024
        ),
    )(state, conv_kernel, gain, up, down_t, head_t, target, field_weight, area)


def local(
    state, conv_kernel, norm_gain, up_weight, down_weight, field_head_weight, target, field_weight
):
    rows = (np.arange(NLAT, dtype=np.float32) + np.float32(0.5)) / np.float32(NLAT) - np.float32(1.0)
    area = np.broadcast_to(np.cos(np.float32(0.5 * math.pi) * rows)[:, None], (NLAT, 128))
    partial, loss = gradients(
        jnp.transpose(state[0], (1, 2, 0)),
        conv_kernel,
        norm_gain[None],
        up_weight,
        down_weight.T,
        field_head_weight.T,
        target,
        field_weight[None],
        jnp.asarray(area, jnp.float32),
    )
    total, loss_total = total_of(partial, loss)
    up, down_t, head_t, kern, gain_row = unpacked(total)
    return (loss_total[0, 0], kern, gain_row[0], up, down_t.T, head_t.T)


def solution(mesh):
    finer = Mesh(mesh.devices.reshape(4, 2, 2, 2, 8), AXES)
    mem, lat = AXES[:3], AXES[3:]
    in_specs = (P(mem, None, lat, None), P(), P(), P(), P(), P(), P(None, lat, None), P())
    out_specs = (P(), P(), P(), P(), P(), P())
    return jax.shard_map(local, mesh=finer, in_specs=in_specs, out_specs=out_specs, check_vma=False)
```

```python
import math

import jax
import jax.numpy as jnp
import numpy as np
from jax import lax
from jax.experimental import pallas as pl
from jax.experimental.pallas import tpu as pltpu
from jax.sharding import Mesh
from jax.sharding import PartitionSpec as P

AXES = ("mem_0", "mem_1", "mem_2", "lat_0", "lat_1")
MESH_ID = pl.DeviceIdType.MESH
ROWS = 2
LON = 160
CELLS = ROWS * LON
C = 641
HID = 1282
FIELDS = 72
MEMBERS = 16
NLAT = 32
BLOCK = CELLS // MEMBERS
CHUNKS = 6
DELTA = 0.1
EPSILON = 1e-05
AREA = np.cos(
    np.float32(0.5 * math.pi)
    * ((np.arange(NLAT, dtype=np.float32) + np.float32(0.5)) / np.float32(NLAT) - np.float32(1.0))
)

TALL, WIDE = 40, 5
HALF = TALL * WIDE
SMALL = 2 * HALF
SMALL_TALL = 4
UNITS = SMALL + SMALL_TALL * CHUNKS
SIZE = {"x": 4, "y": 4, "z": 8}
PARTS = ((0, 192, "xyz", True), (192, 192, "yxz", True), (384, 40, "xyz", False))


def steps_of(size, order):
    levels = []
    for a in order:
        size = -(-size // SIZE[a])
        levels.append((a, SIZE[a], size))
    return levels


PLANS = tuple((off, size, steps_of(size, order), relay) for off, size, order, relay in PARTS)


def contract(left, right, dims):
    return lax.dot_general(left, right, ((dims[:1], dims[1:]), ((), ())), preferred_element_type=jnp.float32)


def put(ref, value):
    for c in range(CHUNKS - 1):
        ref[c] = value[:, c * 128 : (c + 1) * 128]
    ref[CHUNKS - 1, :, 0:1] = value[:, 640:641]


def member_device(m):
    return {"mem_0": m // 4, "mem_1": (m // 2) % 2, "mem_2": m % 2}


def device_at(axis, p):
    if axis == "x":
        return {"mem_0": p}
    if axis == "y":
        return {"lat_0": p // 2, "mem_1": p % 2}
    return {"lat_1": p}


def remote(src, dst, s, r, dev):
    return pltpu.make_async_remote_copy(
        src_ref=src, dst_ref=dst, send_sem=s, recv_sem=r, device_id=dev, device_id_type=MESH_ID
    )


class Total:
    def __init__(self, g_ref, own, away, core_in, parts, loss_in, sems):
        self.g, self.own, self.away, self.core_in, self.parts, self.loss_in = g_ref, own, away, core_in, parts, loss_in
        self.sems = sems
        self.core = lax.axis_index("mem_2")
        self.sibling = {"mem_2": 1 - self.core}
        self.at = {
            "x": lax.axis_index("mem_0"),
            "y": lax.axis_index("lat_0") * 2 + lax.axis_index("mem_1"),
            "z": lax.axis_index("lat_1"),
        }
        self.open = []
        self.first = {}
        self.running = {}

    def peers(self):
        out = []
        for a in "yz":
            out += [device_at(a, (self.at[a] + d) % SIZE[a]) for d in range(1, SIZE[a])]
        return out

    def begin(self, src, dst, s, r, dev):
        c = remote(src, dst, s, r, dev)
        c.start()
        self.open.append(c)
        return c

    def loss_send(self, level, value):
        base, sbase = (0, 2, 6, 10)[level], (0, 1, 4, 7)[level]
        ls, lr = self.sems["loss"]
        if level == 0:
            devices = [self.sibling]
        else:
            a = "xyz"[level - 1]
            devices = [device_at(a, (self.at[a] + d) % SIZE[a]) for d in range(1, SIZE[a])]
        self.loss_in[base] = value
        self.loss_open = [
            self.begin(self.loss_in.at[base], self.loss_in.at[base + 1 + d], ls.at[sbase + d], lr.at[sbase + d], dev)
            for d, dev in enumerate(devices)
        ]

    def loss_take(self, level):
        base = (0, 2, 6, 10)[level]
        for c in self.loss_open:
            c.wait_recv()
        total = self.loss_in[base]
        for d in range(len(self.loss_open)):
            total = total + self.loss_in[base + 1 + d]
        return total

    def loss_next(self, level):
        self.loss_send(level + 1, self.loss_take(level))

    def pair(self, k):
        off, size = PLANS[k][:2]
        s, r = self.sems["pair"]
        units = pl.ds(off, size)
        self.first[k] = self.begin(self.away.at[units], self.core_in.at[units], s.at[k], r.at[k], self.sibling)

    def held(self, start, count):
        return self.own[pl.ds(start, count)] + self.core_in[pl.ds(start, count)]

    def scatter_first(self, k):
        off, size, levels, relay = PLANS[k]
        a, n, u = levels[0]
        send, recv = self.parts[k][0][:2]
        self.first[k].wait_recv()
        send[...] = self.held(off, size).astype(jnp.bfloat16)
        if not relay:
            self.scatter_sends(k, 0)
            return
        s, r = self.sems["relay"]
        h = u // 2
        me = self.at[a]
        up, down, far = (me + 1) % n, (me + n - 1) % n, (me + 2) % n
        into = self.parts[k][0][4]
        dev_up, dev_down = device_at(a, up), device_at(a, down)
        b = lambda i, src, dst, dev: self.begin(src, dst, s.at[k, i], r.at[k, i], dev)
        self.running[k] = [
            b(0, send.at[pl.ds(far * u, h)], into.at[0], dev_up),
            b(1, send.at[pl.ds(far * u + h, h)], into.at[1], dev_down),
            b(2, send.at[pl.ds(up * u + h, h)], recv.at[0, pl.ds(h, h)], dev_up),
            b(3, send.at[pl.ds(down * u, h)], recv.at[1, pl.ds(0, h)], dev_down),
        ]

    def relay(self, k):
        off, size, levels, _ = PLANS[k]
        a, n, u = levels[0]
        recv, into, outof = self.parts[k][0][1], self.parts[k][0][4], self.parts[k][0][5]
        s, r = self.sems["relay"]
        h = u // 2
        me = self.at[a]
        up, down = (me + 1) % n, (me + n - 1) % n
        for i, (dev, start, half) in enumerate(((up, off + up * u, 0), (down, off + down * u + h, h))):
            self.running[k][i].wait_recv()
            outof[i] = (self.held(start, h) + into[i].astype(jnp.float32)).astype(jnp.bfloat16)
            self.running[k].append(
                self.begin(outof.at[i], recv.at[i, pl.ds(half, h)], s.at[k, 4 + i], r.at[k, 4 + i], device_at(a, dev))
            )
        self.running[k] = self.running[k][2:]

    def scatter_sends(self, k, level):
        a, n, u = PLANS[k][2][level]
        send, recv = self.parts[k][level][:2]
        s, r = self.sems["scatter"]
        self.running[k] = []
        for d in range(1, n):
            p = (self.at[a] + d) % n
            self.running[k].append(
                self.begin(
                    send.at[pl.ds(p * u, u)], recv.at[d - 1], s.at[k, level, d - 1], r.at[k, level, d - 1], device_at(a, p)
                )
            )

    def gathered_sum(self, k, level):
        off, size, levels, relay = PLANS[k]
        a, n, u = levels[level]
        recv, total = self.parts[k][level][1:3]
        for c in self.running[k]:
            c.wait_recv()
        me = self.at[a]
        value = self.held(off + me * u, u) if level == 0 else total[pl.ds(me * u, u)]
        for d in range(2 if relay and level == 0 else n - 1):
            value = value + recv[d].astype(jnp.float32)
        return value

    def scatter(self, k, level):
        a, n, u = PLANS[k][2][level]
        below = PLANS[k][2][level - 1][2]
        send, recv, total = self.parts[k][level][:3]
        total[0:below] = self.gathered_sum(k, level - 1)
        if n * u > below:
            total[below:] = jnp.zeros((n * u - below, 16, 128), jnp.float32)
        send[...] = total[...].astype(jnp.bfloat16)
        self.scatter_sends(k, level)

    def gather(self, k, level):
        a, n, u = PLANS[k][2][level]
        into = self.parts[k][level][3]
        me = self.at[a]
        mine = pl.ds(me * u, u)
        s, r = self.sems["gather"]
        if level == 2:
            into[mine] = self.gathered_sum(k, 2).astype(jnp.bfloat16)
            source = into.at[mine]
        else:
            below = self.parts[k][level + 1][3]
            for c in self.running[k]:
                c.wait_recv()
            into[mine] = below[0:u]
            source = below.at[pl.ds(0, u)]
        self.running[k] = [
            self.begin(
                source, into.at[mine], s.at[k, level, d - 1], r.at[k, level, d - 1], device_at(a, (me + d) % n)
            )
            for d in range(1, n)
        ]

    def to_sibling(self, k, i, start, count):
        s, r = self.sems["back"]
        piece = self.g.at[self.core, pl.ds(start, count)]
        self.last.append(self.begin(piece, piece, s.at[k, i], r.at[k, i], self.sibling))

    last = None

    def gather_last(self):
        self.last = []
        s, r = self.sems["gather"]
        s2, r2 = self.sems["relay_back"]
        flights = {}
        for k, (off, size, levels, relay) in enumerate(PLANS):
            a, n, u = levels[0]
            me = self.at[a]
            below = self.parts[k][1][3]
            for c in self.running[k]:
                c.wait_recv()
            mine = pl.ds(off + me * u, u)
            self.g[self.core, mine] = below[0:u]
            if relay:
                h = u // 2
                up, down = device_at(a, (me + 1) % n), device_at(a, (me + n - 1) % n)
                lo, hi = pl.ds(off + me * u, h), pl.ds(off + me * u + h, h)
                b = lambda i, part, src, dev: self.begin(
                    src, self.g.at[self.core, part], s2.at[k, i], r2.at[k, i], dev
                )
                flights[k] = [
                    b(0, lo, below.at[pl.ds(0, h)], up),
                    b(1, hi, below.at[pl.ds(h, h)], down),
                    b(2, hi, below.at[pl.ds(h, h)], up),
                    b(3, lo, below.at[pl.ds(0, h)], down),
                ]
            else:
                flights[k] = [
                    self.begin(
                        below.at[pl.ds(0, u)],
                        self.g.at[self.core, mine],
                        s.at[k, 0, d - 1],
                        r.at[k, 0, d - 1],
                        device_at(a, (me + d) % n),
                    )
                    for d in range(1, n)
                ]
            self.to_sibling(k, 0, off + me * u, u)
        for k, (off, size, levels, relay) in enumerate(PLANS):
            a, n, u = levels[0]
            me = self.at[a]
            if not relay:
                continue
            h = u // 2
            up, down = (me + 1) % n, (me + n - 1) % n
            for i, (start, dev) in enumerate(((off + down * u, up), (off + up * u + h, down))):
                flights[k][i].wait_recv()
                piece = self.g.at[self.core, pl.ds(start, h)]
                flights[k].append(
                    self.begin(piece, piece, s2.at[k, 4 + i], r2.at[k, 4 + i], device_at(a, dev))
                )
                self.to_sibling(k, 1 + i, start, h)
        for k, (off, size, levels, relay) in enumerate(PLANS):
            a, n, u = levels[0]
            me = self.at[a]
            h = u // 2
            up, down, far = (me + 1) % n, (me + n - 1) % n, (me + 2) % n
            if relay:
                starts = (off + down * u + h, off + up * u, off + far * u, off + far * u + h)
                for i, start in enumerate(starts):
                    flights[k][2 + i].wait_recv()
                    self.to_sibling(k, 3 + i, start, h)
            else:
                for d in range(1, n):
                    flights[k][d - 1].wait_recv()
                    self.to_sibling(k, d, off + ((me + n - d) % n) * u, u)
        for c in self.last:
            c.wait_recv()


def total_scratch():
    bf16, f32 = jnp.bfloat16, jnp.float32
    V = pltpu.VMEM
    parts = []
    for off, size, levels, relay in PLANS:
        part = []
        for level, (a, n, u) in enumerate(levels):
            relays = relay and level == 0
            one = [
                V((n * u, 16, 128), bf16),
                V((2 if relays else n - 1, u, 16, 128), bf16),
                V((n * u if level else 1, 16, 128), f32),
                V((n * u if level else 1, 16, 128), bf16),
            ]
            if relays:
                one += [V((2, u // 2, 16, 128), bf16), V((2, u // 2, 16, 128), bf16)]
            part.append(one)
        parts.append(part)
    dma = pltpu.SemaphoreType.DMA
    sems = {
        "pair": (dma((3,)), dma((3,))),
        "relay": (dma((3, 6)), dma((3, 6))),
        "relay_back": (dma((3, 6)), dma((3, 6))),
        "scatter": (dma((3, 3, 7)), dma((3, 3, 7))),
        "gather": (dma((3, 3, 7)), dma((3, 3, 7))),
        "back": (dma((3, 7)), dma((3, 7))),
        "loss": (dma((14,)), dma((14,))),
    }
    return dict(
        own=V((UNITS, 16, 128), f32),
        away=V((UNITS, 16, 128), f32),
        core_in=V((UNITS, 16, 128), f32),
        parts=parts,
        loss_in=V((18, 8, 128), f32),
        sems=sems,
    )


def step_kernel(
    state,
    conv_kernel,
    gain,
    up_hbm,
    down_hbm,
    head_t,
    target,
    field_weight,
    g_ref,
    loss_ref,
    w,
    total_refs,
):
    win, ck, gn, su, nr, inv, sc, rd = (w[i] for i in ("win", "ck", "gn", "su", "nr", "inv", "sc", "rd"))
    pre, slope, hid, hp, fcs, fs, fr = (w[i] for i in ("pre", "slope", "hid", "hp", "fcs", "fs", "fr"))
    truth, co_s, co_r, co, dp, dsum, dsc = (w[i] for i in ("truth", "co_s", "co_r", "co", "dp", "dsum", "dsc"))
    small, thin_s, thin_r, up, down_t, drr = (w[i] for i in ("small", "thin_s", "thin_r", "up", "down_t", "drr"))
    halo_s, halo_r, fc_s, fc_r, ct_s, ct_r, wt = (w[i] for i in ("halo_s", "halo_r", "fc_s", "fc_r", "ct_s", "ct_r", "wt"))
    total = Total(g_ref, **total_refs)
    f32, bf16 = jnp.float32, jnp.bfloat16
    lat = lax.axis_index("lat_0") * 8 + lax.axis_index("lat_1")
    member = lax.axis_index("mem_0") * 4 + lax.axis_index("mem_1") * 2 + lax.axis_index("mem_2")

    def lat_device(d):
        p = (lat + d) % 16
        return {"lat_0": p // 8, "lat_1": p % 8}

    above, below = lat_device(1), lat_device(15)
    others = [member_device((member + d) % MEMBERS) for d in range(1, MEMBERS)]
    barrier = pltpu.get_barrier_semaphore()
    greeted = [above, below] + others + total.peers()
    for dev in greeted:
        pl.semaphore_signal(barrier, inc=1, device_id=dev, device_id_type=MESH_ID)
    weights = [pltpu.make_async_copy(up_hbm, up, wt.at[0]), pltpu.make_async_copy(down_hbm, down_t, wt.at[1])]
    for c in weights:
        c.start()

    win[CHUNKS - 1] = jnp.zeros((6, 176, 128), f32)
    for c in range(CHUNKS - 1):
        win[c, 2:4, 8:168, :] = state[:, :, c * 128 : (c + 1) * 128]
    win[CHUNKS - 1, 2:4, 8:168, 0:1] = state[:, :, 640:641]
    thin_s[...] = jnp.zeros((8, LON), f32)
    for i in range(ROWS):
        thin_s[i : i + 1, :] = jnp.transpose(win[CHUNKS - 1, 2 + i, 8:168, :])[0:1, :]
    pl.semaphore_wait(barrier, len(greeted))

    def halo(c):
        mine = win.at[c, 2:4, 8:168]
        return (
            remote(mine, win.at[c, 0:2, 8:168], halo_s.at[0, c], halo_r.at[0, c], above),
            remote(mine, win.at[c, 4:6, 8:168], halo_s.at[1, c], halo_r.at[1, c], below),
        )

    thin = (
        remote(thin_s, thin_r.at[0], halo_s.at[0, CHUNKS - 1], halo_r.at[0, CHUNKS - 1], above),
        remote(thin_s, thin_r.at[1], halo_s.at[1, CHUNKS - 1], halo_r.at[1, CHUNKS - 1], below),
    )
    for copy in thin:
        copy.start()

    @pl.loop(0, CHUNKS - 1)
    def _(c):
        for copy in halo(c):
            copy.start()

    ck[CHUNKS - 1] = jnp.zeros((25, 128), f32)
    put(ck, conv_kernel[...])
    gn[CHUNKS - 1] = jnp.zeros((1, 128), f32)
    put(gn, gain[...].reshape(1, C))
    hp[:, 640:768] = jnp.zeros((FIELDS, 128), bf16)
    hp[:, 0:641] = head_t[...]
    rd[:, 640:768] = jnp.zeros((CELLS, 128), bf16)
    su[CHUNKS - 1] = jnp.zeros((CELLS, 128), f32)
    dsc[CHUNKS - 1] = jnp.zeros((CELLS, 128), f32)
    small[...] = jnp.zeros((2, CHUNKS, 64, 128), f32)
    for i in range(ROWS):
        columns = jnp.transpose(target[:, i, :])
        for b in range(MEMBERS // ROWS):
            truth[i * (MEMBERS // ROWS) + b] = columns[b * BLOCK : (b + 1) * BLOCK, :]

    def wrap(c, rows):
        win[c, rows, 6:8, :] = win[c, rows, 166:168, :]
        win[c, rows, 168:170, :] = win[c, rows, 8:10, :]

    def taps(c, i, rows, acc):
        for a in rows:
            for b in range(5):
                acc = acc + ck[c, 5 * a + b : 5 * a + b + 1, :] * win[c, i + a, 6 + b : 166 + b, :]
        return acc

    own = ((2, 3), (1, 2))
    met = ((0, 1, 4), (0, 3, 4))

    @pl.loop(0, CHUNKS)
    def _(c):
        wrap(c, slice(2, 4))
        for i in range(ROWS):
            su[c, i * LON : (i + 1) * LON] = taps(c, i, own[i], win[c, 2 + i, 8:168, :])

    def meet(c):
        @pl.when(lat == 0)
        def _():
            win[c, 0:2] = jnp.zeros((2, 176, 128), f32)

        @pl.when(lat == 15)
        def _():
            win[c, 4:6] = jnp.zeros((2, 176, 128), f32)

        wrap(c, slice(0, 2))
        wrap(c, slice(4, 6))
        for i in range(ROWS):
            su[c, i * LON : (i + 1) * LON] = taps(c, i, met[i], su[c, i * LON : (i + 1) * LON])

    for side, copy in enumerate(thin):
        copy.wait_recv()
        column = jnp.transpose(thin_r[side])
        for i in range(ROWS):
            win[CHUNKS - 1, 4 * side + i, 8:168, 0:1] = column[:, i : i + 1]
    meet(CHUNKS - 1)

    @pl.loop(0, CHUNKS - 1)
    def _(c):
        for copy in halo(c):
            copy.wait_recv()
        meet(c)

    level = su[0]
    for c in range(1, CHUNKS):
        level = level + su[c]
    mean = jnp.sum(level, axis=1, keepdims=True) * (1.0 / C)
    first_lane = (lax.broadcasted_iota(jnp.int32, (CELLS, 128), 1) < 1).astype(f32)
    square = jnp.zeros((CELLS, 128), f32)
    for c in range(CHUNKS):
        center = su[c] - mean
        if c == CHUNKS - 1:
            center = center * first_lane
        nr[c] = center
        square = square + center * center
    inverse = lax.rsqrt(jnp.sum(square, axis=1, keepdims=True) * (1.0 / C) + EPSILON)
    inv[...] = inverse
    for c in range(CHUNKS):
        normed = nr[c] * inverse
        nr[c] = normed
        sc[:, c * 128 : (c + 1) * 128] = (normed * gn[c]).astype(bf16)

    for c in weights:
        c.wait()
    pre[...] = jnp.dot(sc[:, 0:C], up[...], preferred_element_type=f32)

    @pl.loop(0, CELLS // 16)
    def _(r):
        rows = pl.ds(pl.multiple_of(r * 16, 16), 16)
        x = pre[rows, :]
        cumul = 0.5 * (1.0 + lax.erf(x * (1.0 / math.sqrt(2.0))))
        density = jnp.exp(-0.5 * x * x) * (1.0 / math.sqrt(2.0 * math.pi))
        hid[rows, :] = (x * cumul).astype(bf16)
        slope[rows, :] = cumul + x * density

    mlp = contract(hid[...], down_t[...], (1, 1))
    for c in range(CHUNKS - 1):
        at = slice(c * 128, (c + 1) * 128)
        rd[:, at] = (su[c] + mlp[:, at]).astype(bf16)
    rd[:, 640:641] = (su[CHUNKS - 1, :, 0:1] + mlp[:, 640:641]).astype(bf16)
    fcs[...] = contract(rd[...], hp[...], (1, 1))

    for p in range(MEMBERS):
        fs[p] = fcs[p * BLOCK : (p + 1) * BLOCK, :]
    sent = []
    for d in range(1, MEMBERS):
        p = (member + d) % MEMBERS
        c = remote(fs.at[p], fr.at[member], fc_s.at[d - 1], fc_r.at[d - 1], others[d - 1])
        c.start()
        sent.append(c)
    fr[member] = fs[member]
    for c in sent:
        c.wait_recv()

    row = 2 * lat + member // (MEMBERS // ROWS)
    area = jnp.float32(AREA[0])
    for i in range(1, NLAT):
        area = jnp.where(row == i, jnp.float32(AREA[i]), area)
    weight = field_weight[...] * area
    against = truth[member]
    members = fr[...]
    gap = members - against[None]
    square = gap * gap + DELTA * DELTA
    root = lax.rsqrt(square)
    miss = jnp.sum(square * root - DELTA, axis=0)
    slope_miss = gap * root
    apart = jnp.zeros((BLOCK, FIELDS), f32)
    pull = jnp.zeros((MEMBERS, BLOCK, FIELDS), f32)
    for n in range(MEMBERS):
        gap = members - fr[n][None]
        square = gap * gap + DELTA * DELTA
        root = lax.rsqrt(square)
        apart = apart + jnp.sum(square * root - DELTA, axis=0)
        pull = pull + gap * root
    cells = NLAT * LON * FIELDS
    spread = miss * (1.0 / MEMBERS) - apart * (1.0 / (2.0 * MEMBERS * (MEMBERS - 1)))
    cotangent = weight[None] * (slope_miss - pull * (1.0 / (MEMBERS - 1))) * (1.0 / (MEMBERS * math.sqrt(cells)))
    co_s[...] = cotangent.astype(bf16)
    back = []
    for d in range(1, MEMBERS):
        p = (member + d) % MEMBERS
        c = remote(co_s.at[p], co_r.at[member], ct_s.at[d - 1], ct_r.at[d - 1], others[d - 1])
        c.start()
        back.append(c)
    co_r[member] = co_s[member]
    total.loss_send(0, jnp.full((8, 128), jnp.sum(weight * spread) * (1.0 / cells), f32))
    for c in back:
        c.wait_recv()
    for p in range(MEMBERS):
        fcs[p * BLOCK : (p + 1) * BLOCK, :] = co_r[p].astype(f32)
    co[...] = fcs[...].astype(bf16)

    d_output = jnp.dot(co[...], hp[...], preferred_element_type=f32)
    for c in range(CHUNKS):
        dsum[c] = d_output[:, c * 128 : (c + 1) * 128]
    drr[...] = d_output.astype(bf16)

    def half_grad(base, left, right, which, out):
        for s, wide in ((0, 256), (256, 256), (512, 128)):
            columns = pl.ds(pl.multiple_of(which * 640 + s, 128), wide)
            part = contract(left[:, 0:640], right[:, columns], (0, 0))
            for h in range(wide // 128):
                j = base + (s // 128 + h) * TALL
                out[j : j + TALL] = part[:, h * 128 : (h + 1) * 128].reshape(TALL, 16, 128)

    def edge_grad(left, right, r):
        line = contract(left[:, 640:641], right[...], (0, 0))
        for j in range(2 * WIDE):
            small[1, j % 5, r + 2 + j // 5 : r + 3 + j // 5, :] = line[:, j * 128 : (j + 1) * 128]
        edge = contract(right[:, 1280:1282], left[...], (0, 0))
        for c in range(CHUNKS):
            small[1, c, r : r + 2, :] = edge[:, c * 128 : (c + 1) * 128]

    core = total.core
    half_grad(0, drr, hid, 1 - core, total.away)
    total.pair(0)
    half_grad(0, drr, hid, core, total.own)
    pre[...] = jnp.dot(drr[:, 0:C], down_t[...], preferred_element_type=f32)

    @pl.loop(0, CELLS // 16)
    def _(r):
        rows = pl.ds(pl.multiple_of(r * 16, 16), 16)
        dp[rows, :] = (pre[rows, :] * slope[rows, :]).astype(bf16)

    half_grad(HALF, sc, dp, 1 - core, total.away)
    total.pair(1)
    total.scatter_first(0)
    half_grad(HALF, sc, dp, core, total.own)
    total.loss_next(0)
    edge_grad(drr, hid, 39)
    edge_grad(sc, dp, 34)
    head_grad = contract(co[...], rd[...], (0, 0))
    for c in range(CHUNKS):
        small[0, c, 0:64, :] = head_grad[0:64, c * 128 : (c + 1) * 128]
        small[1, c, 0:8, :] = head_grad[64:72, c * 128 : (c + 1) * 128]
    total.scatter_first(1)
    put(dsc, contract(dp[...], up[...], (1, 1)))
    mean_a = jnp.zeros((CELLS, 128), f32)
    mean_b = jnp.zeros((CELLS, 128), f32)
    for c in range(CHUNKS):
        both = dsc[c] * nr[c]
        small[1, c, 33:34, :] = jnp.sum(both, axis=0, keepdims=True)
        mean_a = mean_a + dsc[c] * gn[c]
        mean_b = mean_b + both * gn[c]
    mean_a = jnp.sum(mean_a, axis=1, keepdims=True) * (1.0 / C)
    mean_b = jnp.sum(mean_b, axis=1, keepdims=True) * (1.0 / C)
    for c in range(CHUNKS):
        dsum[c] = dsum[c] + inv[...] * (dsc[c] * gn[c] - mean_a - nr[c] * mean_b)

    total.relay(0)
    total.loss_next(1)

    @pl.loop(0, CHUNKS)
    def _(c):
        for a in range(5):
            acc = [jnp.zeros((8, 128), f32) for _ in range(5)]
            for i in range(ROWS):
                for t in range(LON // 8):
                    d = dsum[c, i * LON + 8 * t : i * LON + 8 * t + 8, :]
                    for b in range(5):
                        acc[b] = acc[b] + d * win[c, i + a, 6 + b + 8 * t : 14 + b + 8 * t, :]
            for b in range(5):
                tap = 8 + 5 * a + b
                small[1, c, tap : tap + 1, :] = jnp.sum(acc[b], axis=0, keepdims=True)

    for c in range(CHUNKS):
        units = slice(SMALL + c * SMALL_TALL, SMALL + (c + 1) * SMALL_TALL)
        total.away[units] = small[1 - core, c].reshape(SMALL_TALL, 16, 128)
        total.own[units] = small[core, c].reshape(SMALL_TALL, 16, 128)
    total.pair(2)
    total.relay(1)
    total.scatter_first(2)
    for step in (1, 2):
        for part in range(3):
            total.scatter(part, step)
        if step == 1:
            total.loss_next(2)
    for step in (2, 1):
        for part in range(3):
            total.gather(part, step)
    total.gather_last()
    loss_ref[...] = total.loss_take(3)

    @pl.loop(0, CHUNKS - 1)
    def _(c):
        for copy in halo(c):
            copy.wait_send()

    for c in list(thin) + sent + back + total.open:
        c.wait_send()


def gradients(state, conv_kernel, gain, up, down_t, head_t, target, field_weight):
    f32, bf16 = jnp.float32, jnp.bfloat16
    vmem = pl.BlockSpec(memory_space=pltpu.VMEM)
    anywhere = pl.BlockSpec(memory_space=pl.ANY)
    V = pltpu.VMEM
    dma = pltpu.SemaphoreType.DMA
    work = dict(
        win=V((CHUNKS, 6, 176, 128), f32),
        ck=V((CHUNKS, 25, 128), f32),
        gn=V((CHUNKS, 1, 128), f32),
        su=V((CHUNKS, CELLS, 128), f32),
        nr=V((CHUNKS, CELLS, 128), f32),
        inv=V((CELLS, 1), f32),
        sc=V((CELLS, 768), bf16),
        rd=V((CELLS, 768), bf16),
        pre=V((CELLS, HID), f32),
        slope=V((CELLS, HID), f32),
        hid=V((CELLS, HID), bf16),
        hp=V((FIELDS, 768), bf16),
        fcs=V((CELLS, FIELDS), f32),
        fs=V((MEMBERS, BLOCK, FIELDS), f32),
        fr=V((MEMBERS, BLOCK, FIELDS), f32),
        truth=V((MEMBERS, BLOCK, FIELDS), f32),
        co_s=V((MEMBERS, BLOCK, FIELDS), bf16),
        co_r=V((MEMBERS, BLOCK, FIELDS), bf16),
        co=V((CELLS, FIELDS), bf16),
        dp=V((CELLS, HID), bf16),
        dsum=V((CHUNKS, CELLS, 128), f32),
        dsc=V((CHUNKS, CELLS, 128), f32),
        small=V((2, CHUNKS, 64, 128), f32),
        thin_s=V((8, LON), f32),
        thin_r=V((2, 8, LON), f32),
        up=V((C, HID), bf16),
        down_t=V((C, HID), bf16),
        drr=V((CELLS, 768), bf16),
        halo_s=dma((2, CHUNKS)),
        halo_r=dma((2, CHUNKS)),
        fc_s=dma((MEMBERS - 1,)),
        fc_r=dma((MEMBERS - 1,)),
        ct_s=dma((MEMBERS - 1,)),
        ct_r=dma((MEMBERS - 1,)),
        wt=dma((2,)),
    )
    refs, tree = jax.tree.flatten((work, total_scratch()))

    def kernel(*args):
        step_kernel(*args[:10], *jax.tree.unflatten(tree, args[10:]))

    return pl.pallas_call(
        kernel,
        out_shape=(
            jax.ShapeDtypeStruct((2, UNITS, 16, 128), bf16),
            jax.ShapeDtypeStruct((8, 128), f32),
        ),
        in_specs=[vmem, vmem, vmem, anywhere, anywhere, vmem, vmem, vmem],
        out_specs=(vmem, vmem),
        scratch_shapes=refs,
        compiler_params=pltpu.CompilerParams(
            collective_id=0, has_side_effects=True, vmem_limit_bytes=58 * 1024 * 1024
        ),
    )(state, conv_kernel, gain, up, down_t, head_t, target, field_weight)


def unpack_kernel(g_ref, loss, up_ref, down_ref, head_ref, kern_ref, gain_ref, loss_ref, small):
    for m, out in enumerate((down_ref, up_ref)):
        for core in range(2):
            for j in range(WIDE):
                start = m * HALF + j * TALL
                piece = g_ref[core, start : start + TALL].astype(jnp.float32)
                lane = (core * WIDE + j) * 128
                out[0:640, lane : lane + 128] = piece.reshape(640, 128)
    for core in range(2):
        for c in range(CHUNKS):
            start = SMALL + c * SMALL_TALL
            piece = g_ref[core, start : start + SMALL_TALL].astype(jnp.float32)
            small[core, :, c * 128 : (c + 1) * 128] = piece.reshape(64, 128)
    head_ref[0:64, :] = small[0, :, 0:641]
    head_ref[64:72, :] = small[1, 0:8, 0:641]
    kern_ref[...] = small[1, 8:33, 0:641]
    gain_ref[...] = small[1, 33:34, 0:641]
    loss_ref[...] = loss[0:1, 0:1]
    for r, out in ((34, up_ref), (39, down_ref)):
        edge = small[1, 32:56, :]
        out[:, 1280:1282] = jnp.transpose(edge)[0:641, r - 32 : r - 30]
        out[640:641, 0:640] = small[1, r + 2 : r + 3, 0:640]
        out[640:641, 640:1280] = small[1, r + 3 : r + 4, 0:640]


def unpacked(g, loss):
    vmem = pl.BlockSpec(memory_space=pltpu.VMEM)
    shapes = ((C, HID), (C, HID), (FIELDS, C), (25, C), (1, C), (1, 1))
    return pl.pallas_call(
        unpack_kernel,
        out_shape=tuple(jax.ShapeDtypeStruct(s, jnp.float32) for s in shapes),
        in_specs=[vmem, vmem],
        out_specs=(vmem,) * 6,
        scratch_shapes=[pltpu.VMEM((2, 64, 768), jnp.float32)],
        compiler_params=pltpu.CompilerParams(vmem_limit_bytes=48 * 1024 * 1024),
    )(g, loss)


def local(
    state, conv_kernel, norm_gain, up_weight, down_weight, field_head_weight, target, field_weight
):
    total, loss = gradients(
        jnp.transpose(state[0], (1, 2, 0)),
        conv_kernel,
        norm_gain,
        up_weight,
        down_weight.T,
        field_head_weight.T,
        target,
        field_weight[None],
    )
    up, down_t, head_t, kern, gain_row, loss = unpacked(total, loss)
    return (loss.reshape(()), kern, gain_row.reshape(C), up, down_t.T, head_t.T)


def solution(mesh):
    finer = Mesh(mesh.devices.reshape(4, 2, 2, 2, 8), AXES)
    mem, lat = AXES[:3], AXES[3:]
    in_specs = (P(mem, None, lat, None), P(), P(), P(), P(), P(), P(None, lat, None), P())
    out_specs = (P(), P(), P(), P(), P(), P())
    return jax.shard_map(local, mesh=finer, in_specs=in_specs, out_specs=out_specs, check_vma=False)
```

```python
import math

import jax
import jax.numpy as jnp
import numpy as np
from jax import lax
from jax.experimental import pallas as pl
from jax.experimental.pallas import tpu as pltpu
from jax.sharding import Mesh
from jax.sharding import PartitionSpec as P

AXES = ("mem_0", "mem_1", "mem_2", "lat_0", "lat_1")
MESH_ID = pl.DeviceIdType.MESH
ROWS = 2
LON = 160
CELLS = ROWS * LON
C = 641
HID = 1282
FIELDS = 72
MEMBERS = 16
NLAT = 32
BLOCK = CELLS // MEMBERS
CHUNKS = 6
DELTA = 0.1
EPSILON = 1e-05
AREA = np.cos(
    np.float32(0.5 * math.pi)
    * ((np.arange(NLAT, dtype=np.float32) + np.float32(0.5)) / np.float32(NLAT) - np.float32(1.0))
)

TALL, WIDE = 40, 5
HALF = TALL * WIDE
SMALL = 2 * HALF
SMALL_TALL = 4
UNITS = SMALL + SMALL_TALL * CHUNKS
SIZE = {"x": 4, "y": 4, "z": 8}
PARTS = ((0, 100, "xy"), (100, 100, "yx"), (200, 100, "xy"), (300, 100, "yx"), (400, 24, "xy"))
GROUPS = ((0, 1), (2, 3, 4))


def levels_of(size, order):
    levels = []
    for a in order:
        size = -(-size // SIZE[a])
        levels.append((a, SIZE[a], size))
    return levels


PLANS = tuple((off, size, levels_of(size, order)) for off, size, order in PARTS)


def group_of(group):
    starts, at = {}, 0
    for k in GROUPS[group]:
        starts[k] = at
        at += PLANS[k][2][1][2]
    return starts, at, -(-at // SIZE["z"])


def contract(left, right, dims):
    return lax.dot_general(left, right, ((dims[:1], dims[1:]), ((), ())), preferred_element_type=jnp.float32)


def put(ref, value):
    for c in range(CHUNKS - 1):
        ref[c] = value[:, c * 128 : (c + 1) * 128]
    ref[CHUNKS - 1, :, 0:1] = value[:, 640:641]


def member_device(m):
    return {"mem_0": m // 4, "mem_1": (m // 2) % 2, "mem_2": m % 2}


def device_at(axis, p):
    if axis == "x":
        return {"mem_0": p}
    if axis == "y":
        return {"lat_0": p // 2, "mem_1": p % 2}
    return {"lat_1": p}


def remote(src, dst, s, r, dev):
    return pltpu.make_async_remote_copy(
        src_ref=src, dst_ref=dst, send_sem=s, recv_sem=r, device_id=dev, device_id_type=MESH_ID
    )


class Total:
    def __init__(self, g_ref, own, away, core_in, parts, groups, loss_in, sems):
        self.g, self.own, self.away, self.core_in, self.parts, self.loss_in = g_ref, own, away, core_in, parts, loss_in
        self.sems, self.groups, self.last = sems, groups, []
        self.core = lax.axis_index("mem_2")
        self.sibling = {"mem_2": 1 - self.core}
        self.at = {
            "x": lax.axis_index("mem_0"),
            "y": lax.axis_index("lat_0") * 2 + lax.axis_index("mem_1"),
            "z": lax.axis_index("lat_1"),
        }
        self.open = []
        self.first = {}
        self.running = {}

    def peers(self):
        out = []
        for a in "yz":
            out += [device_at(a, (self.at[a] + d) % SIZE[a]) for d in range(1, SIZE[a])]
        return out

    def begin(self, src, dst, s, r, dev):
        c = remote(src, dst, s, r, dev)
        c.start()
        self.open.append(c)
        return c

    def loss_send(self, level, value):
        base, sbase = (0, 2, 6, 10)[level], (0, 1, 4, 7)[level]
        ls, lr = self.sems["loss"]
        if level == 0:
            devices = [self.sibling]
        else:
            a = "xyz"[level - 1]
            devices = [device_at(a, (self.at[a] + d) % SIZE[a]) for d in range(1, SIZE[a])]
        self.loss_in[base] = value
        self.loss_open = [
            self.begin(self.loss_in.at[base], self.loss_in.at[base + 1 + d], ls.at[sbase + d], lr.at[sbase + d], dev)
            for d, dev in enumerate(devices)
        ]

    def loss_take(self, level):
        base = (0, 2, 6, 10)[level]
        for c in self.loss_open:
            c.wait_recv()
        total = self.loss_in[base]
        for d in range(len(self.loss_open)):
            total = total + self.loss_in[base + 1 + d]
        return total

    def loss_next(self, level):
        self.loss_send(level + 1, self.loss_take(level))

    def pair(self, k):
        off, size = PLANS[k][:2]
        s, r = self.sems["pair"]
        units = pl.ds(off, size)
        self.first[k] = self.begin(self.away.at[units], self.core_in.at[units], s.at[k], r.at[k], self.sibling)

    def held(self, start, count):
        return self.own[pl.ds(start, count)] + self.core_in[pl.ds(start, count)]

    def arrive(self, key):
        for c in self.running[key]:
            c.wait_recv()
        self.running[key] = []

    def spread(self, key, send, recv, sems, row, axis, u):
        s, r = self.sems[sems]
        n = SIZE[axis]
        self.running[key] = []
        for d in range(1, n):
            p = (self.at[axis] + d) % n
            self.running[key].append(
                self.begin(send.at[pl.ds(p * u, u)], recv.at[d - 1], s.at[row, d - 1], r.at[row, d - 1], device_at(axis, p))
            )

    def share(self, key, source, into, sems, row, axis, start):
        s, r = self.sems[sems]
        n = SIZE[axis]
        self.running[key] = [
            self.begin(
                source, into.at[start], s.at[row, d - 1], r.at[row, d - 1], device_at(axis, (self.at[axis] + d) % n)
            )
            for d in range(1, n)
        ]

    def scatter_0(self, k):
        off, size, levels = PLANS[k]
        a, n, u = levels[0]
        send, recv = self.parts[k][:2]
        self.first[k].wait_recv()
        send[...] = self.held(off, size).astype(jnp.bfloat16)
        self.spread(k, send, recv, "scatter_0", k, a, u)

    def scatter_1(self, k):
        off, size, levels = PLANS[k]
        a, n, below = levels[0]
        b, m, u = levels[1]
        came, total, send, recv = self.parts[k][1:5]
        self.arrive(k)
        value = self.held(off + self.at[a] * below, below)
        for d in range(n - 1):
            value = value + came[d].astype(jnp.float32)
        total[0:below] = value
        if m * u > below:
            total[below:] = jnp.zeros((m * u - below, 16, 128), jnp.float32)
        send[...] = total[...].astype(jnp.bfloat16)
        self.spread(k, send, recv, "scatter_1", k, b, u)

    def scatter_2(self, group):
        starts, used, u = group_of(group)
        total, send, recv = self.groups[group][:3]
        if 8 * u > used:
            total[used:] = jnp.zeros((8 * u - used, 16, 128), jnp.float32)
        for k in GROUPS[group]:
            b, m, below = PLANS[k][2][1]
            held, came = self.parts[k][2], self.parts[k][4]
            self.arrive(k)
            value = held[pl.ds(self.at[b] * below, below)]
            for d in range(m - 1):
                value = value + came[d].astype(jnp.float32)
            total[starts[k] : starts[k] + below] = value
        send[...] = total[...].astype(jnp.bfloat16)
        self.spread(("z", group), send, recv, "scatter_2", group, "z", u)

    def gather_2(self, group):
        starts, used, u = group_of(group)
        total, send, recv, into = self.groups[group]
        self.arrive(("z", group))
        mine = pl.ds(self.at["z"] * u, u)
        value = total[mine]
        for d in range(7):
            value = value + recv[d].astype(jnp.float32)
        into[mine] = value.astype(jnp.bfloat16)
        self.share(("z", group), into.at[mine], into, "gather_2", group, "z", mine)

    def gather_1(self, k):
        group = 0 if k in GROUPS[0] else 1
        b, m, u = PLANS[k][2][1]
        start = group_of(group)[0][k]
        source, into = self.groups[group][3], self.parts[k][5]
        self.arrive(("z", group))
        mine = pl.ds(self.at[b] * u, u)
        into[mine] = source[start : start + u]
        self.share(k, source.at[pl.ds(start, u)], into, "gather_1", k, b, mine)

    def to_sibling(self, k, i, start, count):
        s, r = self.sems["back"]
        piece = self.g.at[self.core, pl.ds(start, count)]
        self.last.append(self.begin(piece, piece, s.at[k, i], r.at[k, i], self.sibling))

    def gather_0(self, k):
        off, size, levels = PLANS[k]
        a, n, u = levels[0]
        source = self.parts[k][5]
        self.arrive(k)
        mine = pl.ds(off + self.at[a] * u, u)
        self.g[self.core, mine] = source[0:u]
        self.share(k, source.at[pl.ds(0, u)], self.g.at[self.core], "gather_0", k, a, mine)
        self.to_sibling(k, 0, off + self.at[a] * u, u)

    def hand_over(self, k):
        off, size, levels = PLANS[k]
        a, n, u = levels[0]
        for d in range(1, n):
            self.running[k][d - 1].wait_recv()
            self.to_sibling(k, d, off + ((self.at[a] + n - d) % n) * u, u)

    def finish(self):
        for c in self.last:
            c.wait_recv()


def total_scratch():
    bf16, f32 = jnp.bfloat16, jnp.float32
    V = pltpu.VMEM
    parts, groups = [], []
    for off, size, levels in PLANS:
        (a, n, u), (b, m, v) = levels
        parts.append(
            [
                V((size, 16, 128), bf16),
                V((n - 1, u, 16, 128), bf16),
                V((m * v, 16, 128), f32),
                V((m * v, 16, 128), bf16),
                V((m - 1, v, 16, 128), bf16),
                V((m * v, 16, 128), bf16),
            ]
        )
    for group in range(len(GROUPS)):
        u = group_of(group)[2]
        groups.append(
            [V((8 * u, 16, 128), f32), V((8 * u, 16, 128), bf16), V((7, u, 16, 128), bf16), V((8 * u, 16, 128), bf16)]
        )
    dma = pltpu.SemaphoreType.DMA
    count = len(PLANS)
    pairs = dict(
        pair=(count,),
        scatter_0=(count, 3),
        scatter_1=(count, 3),
        scatter_2=(2, 7),
        gather_2=(2, 7),
        gather_1=(count, 3),
        gather_0=(count, 3),
        back=(count, 4),
        loss=(14,),
    )
    return dict(
        own=V((UNITS, 16, 128), f32),
        away=V((UNITS, 16, 128), f32),
        core_in=V((UNITS, 16, 128), f32),
        parts=parts,
        groups=groups,
        loss_in=V((18, 8, 128), f32),
        sems={name: (dma(shape), dma(shape)) for name, shape in pairs.items()},
    )


def step_kernel(
    state,
    conv_kernel,
    gain,
    up_hbm,
    down_hbm,
    head_t,
    target,
    field_weight,
    g_ref,
    loss_ref,
    w,
    total_refs,
):
    win, ck, gn, su, nr, inv, sc, rd = (w[i] for i in ("win", "ck", "gn", "su", "nr", "inv", "sc", "rd"))
    pre, slope, hid, hp, fcs, fs, fr = (w[i] for i in ("pre", "slope", "hid", "hp", "fcs", "fs", "fr"))
    truth, co_s, co_r, co, dp, dsum, dsc = (w[i] for i in ("truth", "co_s", "co_r", "co", "dp", "dsum", "dsc"))
    small, thin_s, thin_r, up, down_t, drr = (w[i] for i in ("small", "thin_s", "thin_r", "up", "down_t", "drr"))
    halo_s, halo_r, fc_s, fc_r, ct_s, ct_r, wt = (w[i] for i in ("halo_s", "halo_r", "fc_s", "fc_r", "ct_s", "ct_r", "wt"))
    total = Total(g_ref, **total_refs)
    f32, bf16 = jnp.float32, jnp.bfloat16
    lat = lax.axis_index("lat_0") * 8 + lax.axis_index("lat_1")
    member = lax.axis_index("mem_0") * 4 + lax.axis_index("mem_1") * 2 + lax.axis_index("mem_2")

    def lat_device(d):
        p = (lat + d) % 16
        return {"lat_0": p // 8, "lat_1": p % 8}

    above, below = lat_device(1), lat_device(15)
    others = [member_device((member + d) % MEMBERS) for d in range(1, MEMBERS)]
    barrier = pltpu.get_barrier_semaphore()
    greeted = [above, below] + others + total.peers()
    for dev in greeted:
        pl.semaphore_signal(barrier, inc=1, device_id=dev, device_id_type=MESH_ID)
    weights = [pltpu.make_async_copy(up_hbm, up, wt.at[0]), pltpu.make_async_copy(down_hbm, down_t, wt.at[1])]
    for c in weights:
        c.start()

    win[CHUNKS - 1] = jnp.zeros((6, 176, 128), f32)
    for c in range(CHUNKS - 1):
        win[c, 2:4, 8:168, :] = state[:, :, c * 128 : (c + 1) * 128]
    win[CHUNKS - 1, 2:4, 8:168, 0:1] = state[:, :, 640:641]
    thin_s[...] = jnp.zeros((8, LON), f32)
    for i in range(ROWS):
        thin_s[i : i + 1, :] = jnp.transpose(win[CHUNKS - 1, 2 + i, 8:168, :])[0:1, :]
    pl.semaphore_wait(barrier, len(greeted))

    def halo(c):
        mine = win.at[c, 2:4, 8:168]
        return (
            remote(mine, win.at[c, 0:2, 8:168], halo_s.at[0, c], halo_r.at[0, c], above),
            remote(mine, win.at[c, 4:6, 8:168], halo_s.at[1, c], halo_r.at[1, c], below),
        )

    thin = (
        remote(thin_s, thin_r.at[0], halo_s.at[0, CHUNKS - 1], halo_r.at[0, CHUNKS - 1], above),
        remote(thin_s, thin_r.at[1], halo_s.at[1, CHUNKS - 1], halo_r.at[1, CHUNKS - 1], below),
    )
    for copy in thin:
        copy.start()

    @pl.loop(0, CHUNKS - 1)
    def _(c):
        for copy in halo(c):
            copy.start()

    ck[CHUNKS - 1] = jnp.zeros((25, 128), f32)
    put(ck, conv_kernel[...])
    gn[CHUNKS - 1] = jnp.zeros((1, 128), f32)
    put(gn, gain[...].reshape(1, C))
    hp[:, 640:768] = jnp.zeros((FIELDS, 128), bf16)
    hp[:, 0:641] = head_t[...]
    rd[:, 640:768] = jnp.zeros((CELLS, 128), bf16)
    su[CHUNKS - 1] = jnp.zeros((CELLS, 128), f32)
    dsc[CHUNKS - 1] = jnp.zeros((CELLS, 128), f32)
    small[...] = jnp.zeros((2, CHUNKS, 64, 128), f32)
    for i in range(ROWS):
        columns = jnp.transpose(target[:, i, :])
        for b in range(MEMBERS // ROWS):
            truth[i * (MEMBERS // ROWS) + b] = columns[b * BLOCK : (b + 1) * BLOCK, :]

    def wrap(c, rows):
        win[c, rows, 6:8, :] = win[c, rows, 166:168, :]
        win[c, rows, 168:170, :] = win[c, rows, 8:10, :]

    def taps(c, i, rows, acc):
        for a in rows:
            for b in range(5):
                acc = acc + ck[c, 5 * a + b : 5 * a + b + 1, :] * win[c, i + a, 6 + b : 166 + b, :]
        return acc

    own = ((2, 3), (1, 2))
    met = ((0, 1, 4), (0, 3, 4))

    @pl.loop(0, CHUNKS)
    def _(c):
        wrap(c, slice(2, 4))
        for i in range(ROWS):
            su[c, i * LON : (i + 1) * LON] = taps(c, i, own[i], win[c, 2 + i, 8:168, :])

    def meet(c):
        @pl.when(lat == 0)
        def _():
            win[c, 0:2] = jnp.zeros((2, 176, 128), f32)

        @pl.when(lat == 15)
        def _():
            win[c, 4:6] = jnp.zeros((2, 176, 128), f32)

        wrap(c, slice(0, 2))
        wrap(c, slice(4, 6))
        for i in range(ROWS):
            su[c, i * LON : (i + 1) * LON] = taps(c, i, met[i], su[c, i * LON : (i + 1) * LON])

    for side, copy in enumerate(thin):
        copy.wait_recv()
        column = jnp.transpose(thin_r[side])
        for i in range(ROWS):
            win[CHUNKS - 1, 4 * side + i, 8:168, 0:1] = column[:, i : i + 1]
    meet(CHUNKS - 1)

    @pl.loop(0, CHUNKS - 1)
    def _(c):
        for copy in halo(c):
            copy.wait_recv()
        meet(c)

    level = su[0]
    for c in range(1, CHUNKS):
        level = level + su[c]
    mean = jnp.sum(level, axis=1, keepdims=True) * (1.0 / C)
    first_lane = (lax.broadcasted_iota(jnp.int32, (CELLS, 128), 1) < 1).astype(f32)
    square = jnp.zeros((CELLS, 128), f32)
    for c in range(CHUNKS):
        center = su[c] - mean
        if c == CHUNKS - 1:
            center = center * first_lane
        nr[c] = center
        square = square + center * center
    inverse = lax.rsqrt(jnp.sum(square, axis=1, keepdims=True) * (1.0 / C) + EPSILON)
    inv[...] = inverse
    for c in range(CHUNKS):
        normed = nr[c] * inverse
        nr[c] = normed
        sc[:, c * 128 : (c + 1) * 128] = (normed * gn[c]).astype(bf16)

    for c in weights:
        c.wait()
    pre[...] = jnp.dot(sc[:, 0:C], up[...], preferred_element_type=f32)

    @pl.loop(0, CELLS // 16)
    def _(r):
        rows = pl.ds(pl.multiple_of(r * 16, 16), 16)
        x = pre[rows, :]
        cumul = 0.5 * (1.0 + lax.erf(x * (1.0 / math.sqrt(2.0))))
        density = jnp.exp(-0.5 * x * x) * (1.0 / math.sqrt(2.0 * math.pi))
        hid[rows, :] = (x * cumul).astype(bf16)
        slope[rows, :] = cumul + x * density

    mlp = contract(hid[...], down_t[...], (1, 1))
    for c in range(CHUNKS - 1):
        at = slice(c * 128, (c + 1) * 128)
        rd[:, at] = (su[c] + mlp[:, at]).astype(bf16)
    rd[:, 640:641] = (su[CHUNKS - 1, :, 0:1] + mlp[:, 640:641]).astype(bf16)
    fcs[...] = contract(rd[...], hp[...], (1, 1))

    for p in range(MEMBERS):
        fs[p] = fcs[p * BLOCK : (p + 1) * BLOCK, :]
    sent = []
    for d in range(1, MEMBERS):
        p = (member + d) % MEMBERS
        c = remote(fs.at[p], fr.at[member], fc_s.at[d - 1], fc_r.at[d - 1], others[d - 1])
        c.start()
        sent.append(c)
    fr[member] = fs[member]
    for c in sent:
        c.wait_recv()

    row = 2 * lat + member // (MEMBERS // ROWS)
    area = jnp.float32(AREA[0])
    for i in range(1, NLAT):
        area = jnp.where(row == i, jnp.float32(AREA[i]), area)
    weight = field_weight[...] * area
    against = truth[member]
    members = fr[...]
    gap = members - against[None]
    square = gap * gap + DELTA * DELTA
    root = lax.rsqrt(square)
    miss = jnp.sum(square * root - DELTA, axis=0)
    slope_miss = gap * root
    apart = jnp.zeros((BLOCK, FIELDS), f32)
    pull = jnp.zeros((MEMBERS, BLOCK, FIELDS), f32)
    for n in range(MEMBERS):
        gap = members - fr[n][None]
        square = gap * gap + DELTA * DELTA
        root = lax.rsqrt(square)
        apart = apart + jnp.sum(square * root - DELTA, axis=0)
        pull = pull + gap * root
    cells = NLAT * LON * FIELDS
    spread = miss * (1.0 / MEMBERS) - apart * (1.0 / (2.0 * MEMBERS * (MEMBERS - 1)))
    cotangent = weight[None] * (slope_miss - pull * (1.0 / (MEMBERS - 1))) * (1.0 / (MEMBERS * math.sqrt(cells)))
    co_s[...] = cotangent.astype(bf16)
    back = []
    for d in range(1, MEMBERS):
        p = (member + d) % MEMBERS
        c = remote(co_s.at[p], co_r.at[member], ct_s.at[d - 1], ct_r.at[d - 1], others[d - 1])
        c.start()
        back.append(c)
    co_r[member] = co_s[member]
    total.loss_send(0, jnp.full((8, 128), jnp.sum(weight * spread) * (1.0 / cells), f32))
    for c in back:
        c.wait_recv()
    for p in range(MEMBERS):
        fcs[p * BLOCK : (p + 1) * BLOCK, :] = co_r[p].astype(f32)
    co[...] = fcs[...].astype(bf16)

    d_output = jnp.dot(co[...], hp[...], preferred_element_type=f32)
    for c in range(CHUNKS):
        dsum[c] = d_output[:, c * 128 : (c + 1) * 128]
    drr[...] = d_output.astype(bf16)

    def half_grad(base, left, right, which, out, then=()):
        for i, (s, wide) in enumerate(((0, 256), (256, 256), (512, 128))):
            columns = pl.ds(pl.multiple_of(which * 640 + s, 128), wide)
            part = contract(left[:, 0:640], right[:, columns], (0, 0))
            for h in range(wide // 128):
                j = base + (s // 128 + h) * TALL
                out[j : j + TALL] = part[:, h * 128 : (h + 1) * 128].reshape(TALL, 16, 128)
            if i in then:
                total.pair(then[i])

    def edge_grad(left, right, r):
        line = contract(left[:, 640:641], right[...], (0, 0))
        for j in range(2 * WIDE):
            small[1, j % 5, r + 2 + j // 5 : r + 3 + j // 5, :] = line[:, j * 128 : (j + 1) * 128]
        edge = contract(right[:, 1280:1282], left[...], (0, 0))
        for c in range(CHUNKS):
            small[1, c, r : r + 2, :] = edge[:, c * 128 : (c + 1) * 128]

    core = total.core
    half_grad(0, drr, hid, 1 - core, total.away, {1: 0, 2: 1})
    half_grad(0, drr, hid, core, total.own)
    pre[...] = jnp.dot(drr[:, 0:C], down_t[...], preferred_element_type=f32)

    @pl.loop(0, CELLS // 16)
    def _(r):
        rows = pl.ds(pl.multiple_of(r * 16, 16), 16)
        dp[rows, :] = (pre[rows, :] * slope[rows, :]).astype(bf16)

    total.scatter_0(0)
    total.scatter_0(1)
    half_grad(HALF, sc, dp, 1 - core, total.away, {1: 2, 2: 3})
    half_grad(HALF, sc, dp, core, total.own)
    total.loss_next(0)
    head_grad = contract(co[...], rd[...], (0, 0))
    for c in range(CHUNKS):
        small[0, c, 0:64, :] = head_grad[0:64, c * 128 : (c + 1) * 128]
        small[1, c, 0:8, :] = head_grad[64:72, c * 128 : (c + 1) * 128]
    total.scatter_0(2)
    total.scatter_0(3)
    edge_grad(drr, hid, 39)
    edge_grad(sc, dp, 34)
    put(dsc, contract(dp[...], up[...], (1, 1)))
    mean_a = jnp.zeros((CELLS, 128), f32)
    mean_b = jnp.zeros((CELLS, 128), f32)
    for c in range(CHUNKS):
        both = dsc[c] * nr[c]
        small[1, c, 33:34, :] = jnp.sum(both, axis=0, keepdims=True)
        mean_a = mean_a + dsc[c] * gn[c]
        mean_b = mean_b + both * gn[c]
    mean_a = jnp.sum(mean_a, axis=1, keepdims=True) * (1.0 / C)
    mean_b = jnp.sum(mean_b, axis=1, keepdims=True) * (1.0 / C)
    for c in range(CHUNKS):
        dsum[c] = dsum[c] + inv[...] * (dsc[c] * gn[c] - mean_a - nr[c] * mean_b)

    total.scatter_1(0)
    total.scatter_1(1)
    total.loss_next(1)

    @pl.loop(0, CHUNKS)
    def _(c):
        for a in range(5):
            acc = [jnp.zeros((8, 128), f32) for _ in range(5)]
            for i in range(ROWS):
                for t in range(LON // 8):
                    d = dsum[c, i * LON + 8 * t : i * LON + 8 * t + 8, :]
                    for b in range(5):
                        acc[b] = acc[b] + d * win[c, i + a, 6 + b + 8 * t : 14 + b + 8 * t, :]
            for b in range(5):
                tap = 8 + 5 * a + b
                small[1, c, tap : tap + 1, :] = jnp.sum(acc[b], axis=0, keepdims=True)

    for c in range(CHUNKS):
        units = slice(SMALL + c * SMALL_TALL, SMALL + (c + 1) * SMALL_TALL)
        total.away[units] = small[1 - core, c].reshape(SMALL_TALL, 16, 128)
        total.own[units] = small[core, c].reshape(SMALL_TALL, 16, 128)
    total.pair(4)
    total.scatter_2(0)
    total.scatter_0(4)
    total.scatter_1(2)
    total.scatter_1(3)
    total.loss_next(2)
    total.scatter_1(4)
    total.gather_2(0)
    total.scatter_2(1)
    total.gather_1(0)
    total.gather_1(1)
    total.gather_2(1)
    total.gather_0(0)
    total.gather_0(1)
    total.gather_1(2)
    total.gather_1(3)
    total.gather_1(4)
    for part in (2, 3, 4):
        total.gather_0(part)
    for part in range(5):
        total.hand_over(part)
    total.finish()
    loss_ref[...] = total.loss_take(3)

    @pl.loop(0, CHUNKS - 1)
    def _(c):
        for copy in halo(c):
            copy.wait_send()

    for c in list(thin) + sent + back + total.open:
        c.wait_send()


def gradients(state, conv_kernel, gain, up, down_t, head_t, target, field_weight):
    f32, bf16 = jnp.float32, jnp.bfloat16
    vmem = pl.BlockSpec(memory_space=pltpu.VMEM)
    anywhere = pl.BlockSpec(memory_space=pltpu.HBM)
    V = pltpu.VMEM
    dma = pltpu.SemaphoreType.DMA
    work = dict(
        win=V((CHUNKS, 6, 176, 128), f32),
        ck=V((CHUNKS, 25, 128), f32),
        gn=V((CHUNKS, 1, 128), f32),
        su=V((CHUNKS, CELLS, 128), f32),
        nr=V((CHUNKS, CELLS, 128), f32),
        inv=V((CELLS, 1), f32),
        sc=V((CELLS, 768), bf16),
        rd=V((CELLS, 768), bf16),
        pre=V((CELLS, HID), f32),
        slope=V((CELLS, HID), f32),
        hid=V((CELLS, HID), bf16),
        hp=V((FIELDS, 768), bf16),
        fcs=V((CELLS, FIELDS), f32),
        fs=V((MEMBERS, BLOCK, FIELDS), f32),
        fr=V((MEMBERS, BLOCK, FIELDS), f32),
        truth=V((MEMBERS, BLOCK, FIELDS), f32),
        co_s=V((MEMBERS, BLOCK, FIELDS), bf16),
        co_r=V((MEMBERS, BLOCK, FIELDS), bf16),
        co=V((CELLS, FIELDS), bf16),
        dp=V((CELLS, HID), bf16),
        dsum=V((CHUNKS, CELLS, 128), f32),
        dsc=V((CHUNKS, CELLS, 128), f32),
        small=V((2, CHUNKS, 64, 128), f32),
        thin_s=V((8, LON), f32),
        thin_r=V((2, 8, LON), f32),
        up=V((C, HID), bf16),
        down_t=V((C, HID), bf16),
        drr=V((CELLS, 768), bf16),
        halo_s=dma((2, CHUNKS)),
        halo_r=dma((2, CHUNKS)),
        fc_s=dma((MEMBERS - 1,)),
        fc_r=dma((MEMBERS - 1,)),
        ct_s=dma((MEMBERS - 1,)),
        ct_r=dma((MEMBERS - 1,)),
        wt=dma((2,)),
    )
    refs, tree = jax.tree.flatten((work, total_scratch()))

    def kernel(*args):
        step_kernel(*args[:10], *jax.tree.unflatten(tree, args[10:]))

    return pl.pallas_call(
        kernel,
        out_shape=(
            jax.ShapeDtypeStruct((2, UNITS, 16, 128), bf16),
            jax.ShapeDtypeStruct((8, 128), f32),
        ),
        in_specs=[vmem, vmem, vmem, anywhere, anywhere, vmem, vmem, vmem],
        out_specs=(vmem, vmem),
        scratch_shapes=refs,
        compiler_params=pltpu.CompilerParams(
            collective_id=0, has_side_effects=True, vmem_limit_bytes=42 * 1024 * 1024
        ),
    )(state, conv_kernel, gain, up, down_t, head_t, target, field_weight)


def unpack_kernel(g_ref, loss, up_hbm, down_hbm, head_ref, kern_ref, gain_ref, loss_ref, up_ref, down_ref, small, sem):
    for core in range(2):
        for c in range(CHUNKS):
            start = SMALL + c * SMALL_TALL
            piece = g_ref[core, start : start + SMALL_TALL].astype(jnp.float32)
            small[core, :, c * 128 : (c + 1) * 128] = piece.reshape(64, 128)
    copies = []
    for m, r, out, hbm in ((0, 39, down_ref, down_hbm), (1, 34, up_ref, up_hbm)):
        edge = small[1, 32:56, :]
        out[:, 1280:1282] = jnp.transpose(edge)[0:C, r - 32 : r - 30]
        out[640:641, 0:640] = small[1, r + 2 : r + 3, 0:640]
        out[640:641, 640:1280] = small[1, r + 3 : r + 4, 0:640]
        for b in range(5):
            for core in range(2):
                for j in range(WIDE):
                    start = m * HALF + j * TALL + b * 8
                    piece = g_ref[core, start : start + 8].astype(jnp.float32)
                    lane = (core * WIDE + j) * 128
                    out[b * 128 : (b + 1) * 128, lane : lane + 128] = piece.reshape(128, 128)
            rows = pl.ds(b * 128, 128 if b < 4 else 129)
            copies.append(pltpu.make_async_copy(out.at[rows], hbm.at[rows], sem.at[m * 5 + b]))
            copies[-1].start()
    head_ref[0:64, :] = small[0, :, 0:C]
    head_ref[64:72, :] = small[1, 0:8, 0:C]
    kern_ref[...] = small[1, 8:33, 0:C]
    gain_ref[...] = small[1, 33:34, 0:C].reshape(C)
    loss_ref[...] = loss[0:1, 0:1]
    for c in copies:
        c.wait()


def unpacked(g, loss):
    vmem = pl.BlockSpec(memory_space=pltpu.VMEM)
    hbm = pl.BlockSpec(memory_space=pl.ANY)
    shapes = ((C, HID), (C, HID), (FIELDS, C), (25, C), (C,), (1, 1))
    return pl.pallas_call(
        unpack_kernel,
        out_shape=tuple(jax.ShapeDtypeStruct(s, jnp.float32) for s in shapes),
        in_specs=[vmem, vmem],
        out_specs=(hbm, hbm, vmem, vmem, vmem, vmem),
        scratch_shapes=[
            pltpu.VMEM((C, HID), jnp.float32),
            pltpu.VMEM((C, HID), jnp.float32),
            pltpu.VMEM((2, 64, 768), jnp.float32),
            pltpu.SemaphoreType.DMA((10,)),
        ],
        compiler_params=pltpu.CompilerParams(vmem_limit_bytes=24 * 1024 * 1024),
    )(g, loss)


def local(
    state, conv_kernel, norm_gain, up_weight, down_weight, field_head_weight, target, field_weight
):
    total, loss = gradients(
        jnp.transpose(state[0], (1, 2, 0)),
        conv_kernel,
        norm_gain,
        up_weight,
        down_weight.T,
        field_head_weight.T,
        target,
        field_weight[None],
    )
    up, down_t, head_t, kern, gain_row, loss = unpacked(total, loss)
    return (loss.reshape(()), kern, gain_row, up, down_t.T, head_t.T)


def solution(mesh):
    finer = Mesh(mesh.devices.reshape(4, 2, 2, 2, 8), AXES)
    mem, lat = AXES[:3], AXES[3:]
    in_specs = (P(mem, None, lat, None), P(), P(), P(), P(), P(), P(None, lat, None), P())
    out_specs = (P(), P(), P(), P(), P(), P())
    return jax.shard_map(local, mesh=finer, in_specs=in_specs, out_specs=out_specs, check_vma=False)
```

```python
import math

import jax
import jax.numpy as jnp
import numpy as np
from jax import lax
from jax.experimental import pallas as pl
from jax.experimental.pallas import tpu as pltpu
from jax.sharding import Mesh
from jax.sharding import PartitionSpec as P

AXES = ("mem_0", "mem_1", "mem_2", "lat_0", "lat_1")
MESH_ID = pl.DeviceIdType.MESH
ROWS = 2
LON = 160
CELLS = ROWS * LON
C = 641
HID = 1282
FIELDS = 72
MEMBERS = 16
NLAT = 32
BLOCK = CELLS // MEMBERS
CHUNKS = 6
DELTA = 0.1
EPSILON = 1e-05
AREA = np.cos(
    np.float32(0.5 * math.pi)
    * ((np.arange(NLAT, dtype=np.float32) + np.float32(0.5)) / np.float32(NLAT) - np.float32(1.0))
)

TALL, WIDE = 40, 5
HALF = TALL * WIDE
SMALL = 2 * HALF
SMALL_TALL = 4
UNITS = SMALL + SMALL_TALL * CHUNKS
SIZE = {"x": 4, "y": 4, "z": 8}
PARTS = ((0, 100, "xy"), (100, 100, "yx"), (200, 100, "xy"), (300, 100, "yx"), (400, 24, "xy"))
GROUPS = ((0, 1), (2, 3, 4))


def levels_of(size, order):
    levels = []
    for a in order:
        size = -(-size // SIZE[a])
        levels.append((a, SIZE[a], size))
    return levels


PLANS = tuple((off, size, levels_of(size, order)) for off, size, order in PARTS)


def group_of(group):
    starts, at = {}, 0
    for k in GROUPS[group]:
        starts[k] = at
        at += PLANS[k][2][1][2]
    return starts, at, -(-at // SIZE["z"])


def contract(left, right, dims):
    return lax.dot_general(left, right, ((dims[:1], dims[1:]), ((), ())), preferred_element_type=jnp.float32)


def put(ref, value):
    for c in range(CHUNKS - 1):
        ref[c] = value[:, c * 128 : (c + 1) * 128]
    ref[CHUNKS - 1, :, 0:1] = value[:, 640:641]


def member_device(m):
    return {"mem_0": m // 4, "mem_1": (m // 2) % 2, "mem_2": m % 2}


def device_at(axis, p):
    if axis == "x":
        return {"mem_0": p}
    if axis == "y":
        return {"lat_0": p // 2, "mem_1": p % 2}
    return {"lat_1": p}


def remote(src, dst, s, r, dev):
    return pltpu.make_async_remote_copy(
        src_ref=src, dst_ref=dst, send_sem=s, recv_sem=r, device_id=dev, device_id_type=MESH_ID
    )


class Total:
    def __init__(self, g_ref, own, away, core_in, parts, groups, loss_in, sems):
        self.g, self.own, self.away, self.core_in, self.parts, self.loss_in = g_ref, own, away, core_in, parts, loss_in
        self.sems, self.groups, self.last = sems, groups, []
        self.core = lax.axis_index("mem_2")
        self.sibling = {"mem_2": 1 - self.core}
        self.at = {
            "x": lax.axis_index("mem_0"),
            "y": lax.axis_index("lat_0") * 2 + lax.axis_index("mem_1"),
            "z": lax.axis_index("lat_1"),
        }
        self.open = []
        self.first = {}
        self.running = {}

    def peers(self):
        out = []
        for a in "yz":
            out += [device_at(a, (self.at[a] + d) % SIZE[a]) for d in range(1, SIZE[a])]
        return out

    def begin(self, src, dst, s, r, dev):
        c = remote(src, dst, s, r, dev)
        c.start()
        self.open.append(c)
        return c

    def loss_send(self, level, value):
        base, sbase = (0, 2, 6, 10)[level], (0, 1, 4, 7)[level]
        ls, lr = self.sems["loss"]
        if level == 0:
            devices = [self.sibling]
        else:
            a = "xyz"[level - 1]
            devices = [device_at(a, (self.at[a] + d) % SIZE[a]) for d in range(1, SIZE[a])]
        self.loss_in[base] = value
        self.loss_open = [
            self.begin(self.loss_in.at[base], self.loss_in.at[base + 1 + d], ls.at[sbase + d], lr.at[sbase + d], dev)
            for d, dev in enumerate(devices)
        ]

    def loss_take(self, level):
        base = (0, 2, 6, 10)[level]
        for c in self.loss_open:
            c.wait_recv()
        total = self.loss_in[base]
        for d in range(len(self.loss_open)):
            total = total + self.loss_in[base + 1 + d]
        return total

    def loss_next(self, level):
        self.loss_send(level + 1, self.loss_take(level))

    def pair(self, k):
        off, size = PLANS[k][:2]
        s, r = self.sems["pair"]
        units = pl.ds(off, size)
        self.first[k] = self.begin(self.away.at[units], self.core_in.at[units], s.at[k], r.at[k], self.sibling)

    def held(self, start, count):
        return self.own[pl.ds(start, count)] + self.core_in[pl.ds(start, count)]

    def arrive(self, key):
        for c in self.running[key]:
            c.wait_recv()
        self.running[key] = []

    def spread(self, key, send, recv, sems, row, axis, u):
        s, r = self.sems[sems]
        n = SIZE[axis]
        self.running[key] = []
        for d in range(1, n):
            p = (self.at[axis] + d) % n
            self.running[key].append(
                self.begin(send.at[pl.ds(p * u, u)], recv.at[d - 1], s.at[row, d - 1], r.at[row, d - 1], device_at(axis, p))
            )

    def share(self, key, source, into, sems, row, axis, start):
        s, r = self.sems[sems]
        n = SIZE[axis]
        self.running[key] = [
            self.begin(
                source, into.at[start], s.at[row, d - 1], r.at[row, d - 1], device_at(axis, (self.at[axis] + d) % n)
            )
            for d in range(1, n)
        ]

    def scatter_0(self, k):
        off, size, levels = PLANS[k]
        a, n, u = levels[0]
        send, recv = self.parts[k][:2]
        self.first[k].wait_recv()
        send[...] = self.held(off, size).astype(jnp.bfloat16)
        self.spread(k, send, recv, "scatter_0", k, a, u)

    def scatter_1(self, k):
        off, size, levels = PLANS[k]
        a, n, below = levels[0]
        b, m, u = levels[1]
        came, total, send, recv = self.parts[k][1:5]
        self.arrive(k)
        value = self.held(off + self.at[a] * below, below)
        for d in range(n - 1):
            value = value + came[d].astype(jnp.float32)
        total[0:below] = value
        if m * u > below:
            total[below:] = jnp.zeros((m * u - below, 16, 128), jnp.float32)
        send[...] = total[...].astype(jnp.bfloat16)
        self.spread(k, send, recv, "scatter_1", k, b, u)

    def scatter_2(self, group):
        starts, used, u = group_of(group)
        total, send, recv = self.groups[group][:3]
        if 8 * u > used:
            total[used:] = jnp.zeros((8 * u - used, 16, 128), jnp.float32)
        for k in GROUPS[group]:
            b, m, below = PLANS[k][2][1]
            held, came = self.parts[k][2], self.parts[k][4]
            self.arrive(k)
            value = held[pl.ds(self.at[b] * below, below)]
            for d in range(m - 1):
                value = value + came[d].astype(jnp.float32)
            total[starts[k] : starts[k] + below] = value
        send[...] = total[...].astype(jnp.bfloat16)
        self.spread(("z", group), send, recv, "scatter_2", group, "z", u)

    def gather_2(self, group):
        starts, used, u = group_of(group)
        total, send, recv, into = self.groups[group]
        self.arrive(("z", group))
        mine = pl.ds(self.at["z"] * u, u)
        value = total[mine]
        for d in range(7):
            value = value + recv[d].astype(jnp.float32)
        into[mine] = value.astype(jnp.bfloat16)
        self.share(("z", group), into.at[mine], into, "gather_2", group, "z", mine)

    def gather_1(self, k):
        group = 0 if k in GROUPS[0] else 1
        b, m, u = PLANS[k][2][1]
        start = group_of(group)[0][k]
        source, into = self.groups[group][3], self.parts[k][5]
        self.arrive(("z", group))
        mine = pl.ds(self.at[b] * u, u)
        into[mine] = source[start : start + u]
        self.share(k, source.at[pl.ds(start, u)], into, "gather_1", k, b, mine)

    def to_sibling(self, k, i, start, count):
        s, r = self.sems["back"]
        piece = self.g.at[self.core, pl.ds(start, count)]
        self.last.append(self.begin(piece, piece, s.at[k, i], r.at[k, i], self.sibling))

    def gather_0(self, k):
        off, size, levels = PLANS[k]
        a, n, u = levels[0]
        source = self.parts[k][5]
        self.arrive(k)
        mine = pl.ds(off + self.at[a] * u, u)
        self.g[self.core, mine] = source[0:u]
        self.share(k, source.at[pl.ds(0, u)], self.g.at[self.core], "gather_0", k, a, mine)
        self.to_sibling(k, 0, off + self.at[a] * u, u)

    def hand_over(self, k):
        off, size, levels = PLANS[k]
        a, n, u = levels[0]
        for d in range(1, n):
            self.running[k][d - 1].wait_recv()
            self.to_sibling(k, d, off + ((self.at[a] + n - d) % n) * u, u)

    def finish(self):
        for c in self.last:
            c.wait_recv()


def total_scratch():
    bf16, f32 = jnp.bfloat16, jnp.float32
    V = pltpu.VMEM
    parts, groups = [], []
    for off, size, levels in PLANS:
        (a, n, u), (b, m, v) = levels
        parts.append(
            [
                V((size, 16, 128), bf16),
                V((n - 1, u, 16, 128), bf16),
                V((m * v, 16, 128), f32),
                V((m * v, 16, 128), bf16),
                V((m - 1, v, 16, 128), bf16),
                V((m * v, 16, 128), bf16),
            ]
        )
    for group in range(len(GROUPS)):
        u = group_of(group)[2]
        groups.append(
            [V((8 * u, 16, 128), f32), V((8 * u, 16, 128), bf16), V((7, u, 16, 128), bf16), V((8 * u, 16, 128), bf16)]
        )
    dma = pltpu.SemaphoreType.DMA
    count = len(PLANS)
    pairs = dict(
        pair=(count,),
        scatter_0=(count, 3),
        scatter_1=(count, 3),
        scatter_2=(2, 7),
        gather_2=(2, 7),
        gather_1=(count, 3),
        gather_0=(count, 3),
        back=(count, 4),
        loss=(14,),
    )
    return dict(
        own=V((UNITS, 16, 128), f32),
        away=V((UNITS, 16, 128), f32),
        core_in=V((UNITS, 16, 128), f32),
        parts=parts,
        groups=groups,
        loss_in=V((18, 8, 128), f32),
        sems={name: (dma(shape), dma(shape)) for name, shape in pairs.items()},
    )


def step_kernel(
    state_hbm,
    conv_hbm,
    gain_hbm,
    up_hbm,
    down_hbm,
    head_hbm,
    target_hbm,
    field_hbm,
    g_ref,
    loss_ref,
    w,
    total_refs,
):
    win, ck, gn, su, nr, inv, sc, rd = (w[i] for i in ("win", "ck", "gn", "su", "nr", "inv", "sc", "rd"))
    pre, slope, hid, hp, fcs, fs, fr = (w[i] for i in ("pre", "slope", "hid", "hp", "fcs", "fs", "fr"))
    truth, co_s, co_r, co, dp, dsum, dsc = (w[i] for i in ("truth", "co_s", "co_r", "co", "dp", "dsum", "dsc"))
    small, thin_s, thin_r, up, down_t, drr = (w[i] for i in ("small", "thin_s", "thin_r", "up", "down_t", "drr"))
    halo_s, halo_r, fc_s, fc_r, ct_s, ct_r, wt = (w[i] for i in ("halo_s", "halo_r", "fc_s", "fc_r", "ct_s", "ct_r", "wt"))
    total = Total(g_ref, **total_refs)
    f32, bf16 = jnp.float32, jnp.bfloat16
    lat = lax.axis_index("lat_0") * 8 + lax.axis_index("lat_1")
    member = lax.axis_index("mem_0") * 4 + lax.axis_index("mem_1") * 2 + lax.axis_index("mem_2")

    def lat_device(d):
        p = (lat + d) % 16
        return {"lat_0": p // 8, "lat_1": p % 8}

    above, below = lat_device(1), lat_device(15)
    others = [member_device((member + d) % MEMBERS) for d in range(1, MEMBERS)]
    barrier = pltpu.get_barrier_semaphore()
    greeted = [above, below] + others + total.peers()
    for dev in greeted:
        pl.semaphore_signal(barrier, inc=1, device_id=dev, device_id_type=MESH_ID)
    state, conv_kernel, gain, head_t, target, field_weight = (
        w[i] for i in ("state", "conv_kernel", "gain", "head_t", "target", "field_weight")
    )
    loads = [
        pltpu.make_async_copy(src, dst, wt.at[i])
        for i, (src, dst) in enumerate(
            (
                (state_hbm, state),
                (conv_hbm, conv_kernel),
                (gain_hbm, gain),
                (head_hbm, head_t),
                (target_hbm, target),
                (field_hbm, field_weight),
                (up_hbm, up),
                (down_hbm, down_t),
            )
        )
    ]
    for c in loads:
        c.start()
    weights = loads[6:]

    win[CHUNKS - 1] = jnp.zeros((6, 176, 128), f32)
    loads[0].wait()
    for c in range(CHUNKS - 1):
        win[c, 2:4, 8:168, :] = state[:, :, c * 128 : (c + 1) * 128]
    win[CHUNKS - 1, 2:4, 8:168, 0:1] = state[:, :, 640:641]
    thin_s[...] = jnp.zeros((8, LON), f32)
    for i in range(ROWS):
        thin_s[i : i + 1, :] = jnp.transpose(win[CHUNKS - 1, 2 + i, 8:168, :])[0:1, :]
    pl.semaphore_wait(barrier, len(greeted))

    def halo(c):
        mine = win.at[c, 2:4, 8:168]
        return (
            remote(mine, win.at[c, 0:2, 8:168], halo_s.at[0, c], halo_r.at[0, c], above),
            remote(mine, win.at[c, 4:6, 8:168], halo_s.at[1, c], halo_r.at[1, c], below),
        )

    thin = (
        remote(thin_s, thin_r.at[0], halo_s.at[0, CHUNKS - 1], halo_r.at[0, CHUNKS - 1], above),
        remote(thin_s, thin_r.at[1], halo_s.at[1, CHUNKS - 1], halo_r.at[1, CHUNKS - 1], below),
    )
    for copy in thin:
        copy.start()

    @pl.loop(0, CHUNKS - 1)
    def _(c):
        for copy in halo(c):
            copy.start()

    for c in loads[1:6]:
        c.wait()
    ck[CHUNKS - 1] = jnp.zeros((25, 128), f32)
    put(ck, conv_kernel[...])
    gn[CHUNKS - 1] = jnp.zeros((1, 128), f32)
    put(gn, gain[...].reshape(1, C))
    hp[:, 640:768] = jnp.zeros((FIELDS, 128), bf16)
    hp[:, 0:641] = head_t[...]
    rd[:, 640:768] = jnp.zeros((CELLS, 128), bf16)
    su[CHUNKS - 1] = jnp.zeros((CELLS, 128), f32)
    dsc[CHUNKS - 1] = jnp.zeros((CELLS, 128), f32)
    small[...] = jnp.zeros((2, CHUNKS, 64, 128), f32)
    for i in range(ROWS):
        columns = jnp.transpose(target[:, i, :])
        for b in range(MEMBERS // ROWS):
            truth[i * (MEMBERS // ROWS) + b] = columns[b * BLOCK : (b + 1) * BLOCK, :]

    def wrap(c, rows):
        win[c, rows, 6:8, :] = win[c, rows, 166:168, :]
        win[c, rows, 168:170, :] = win[c, rows, 8:10, :]

    def taps(c, i, rows, acc):
        for a in rows:
            for b in range(5):
                acc = acc + ck[c, 5 * a + b : 5 * a + b + 1, :] * win[c, i + a, 6 + b : 166 + b, :]
        return acc

    own = ((2, 3), (1, 2))
    met = ((0, 1, 4), (0, 3, 4))

    @pl.loop(0, CHUNKS)
    def _(c):
        wrap(c, slice(2, 4))
        for i in range(ROWS):
            su[c, i * LON : (i + 1) * LON] = taps(c, i, own[i], win[c, 2 + i, 8:168, :])

    def meet(c):
        @pl.when(lat == 0)
        def _():
            win[c, 0:2] = jnp.zeros((2, 176, 128), f32)

        @pl.when(lat == 15)
        def _():
            win[c, 4:6] = jnp.zeros((2, 176, 128), f32)

        wrap(c, slice(0, 2))
        wrap(c, slice(4, 6))
        for i in range(ROWS):
            su[c, i * LON : (i + 1) * LON] = taps(c, i, met[i], su[c, i * LON : (i + 1) * LON])

    for side, copy in enumerate(thin):
        copy.wait_recv()
        column = jnp.transpose(thin_r[side])
        for i in range(ROWS):
            win[CHUNKS - 1, 4 * side + i, 8:168, 0:1] = column[:, i : i + 1]
    meet(CHUNKS - 1)

    @pl.loop(0, CHUNKS - 1)
    def _(c):
        for copy in halo(c):
            copy.wait_recv()
        meet(c)

    level = su[0]
    for c in range(1, CHUNKS):
        level = level + su[c]
    mean = jnp.sum(level, axis=1, keepdims=True) * (1.0 / C)
    first_lane = (lax.broadcasted_iota(jnp.int32, (CELLS, 128), 1) < 1).astype(f32)
    square = jnp.zeros((CELLS, 128), f32)
    for c in range(CHUNKS):
        center = su[c] - mean
        if c == CHUNKS - 1:
            center = center * first_lane
        nr[c] = center
        square = square + center * center
    inverse = lax.rsqrt(jnp.sum(square, axis=1, keepdims=True) * (1.0 / C) + EPSILON)
    inv[...] = inverse
    for c in range(CHUNKS):
        normed = nr[c] * inverse
        nr[c] = normed
        sc[:, c * 128 : (c + 1) * 128] = (normed * gn[c]).astype(bf16)

    for c in weights:
        c.wait()
    pre[...] = jnp.dot(sc[:, 0:C], up[...], preferred_element_type=f32)

    @pl.loop(0, CELLS // 16)
    def _(r):
        rows = pl.ds(pl.multiple_of(r * 16, 16), 16)
        x = pre[rows, :]
        cumul = 0.5 * (1.0 + lax.erf(x * (1.0 / math.sqrt(2.0))))
        density = jnp.exp(-0.5 * x * x) * (1.0 / math.sqrt(2.0 * math.pi))
        hid[rows, :] = (x * cumul).astype(bf16)
        slope[rows, :] = cumul + x * density

    mlp = contract(hid[...], down_t[...], (1, 1))
    for c in range(CHUNKS - 1):
        at = slice(c * 128, (c + 1) * 128)
        rd[:, at] = (su[c] + mlp[:, at]).astype(bf16)
    rd[:, 640:641] = (su[CHUNKS - 1, :, 0:1] + mlp[:, 640:641]).astype(bf16)
    fcs[...] = contract(rd[...], hp[...], (1, 1))

    for p in range(MEMBERS):
        fs[p] = fcs[p * BLOCK : (p + 1) * BLOCK, :]
    sent = []
    for d in range(1, MEMBERS):
        p = (member + d) % MEMBERS
        c = remote(fs.at[p], fr.at[member], fc_s.at[d - 1], fc_r.at[d - 1], others[d - 1])
        c.start()
        sent.append(c)
    fr[member] = fs[member]
    for c in sent:
        c.wait_recv()

    row = 2 * lat + member // (MEMBERS // ROWS)
    area = jnp.float32(AREA[0])
    for i in range(1, NLAT):
        area = jnp.where(row == i, jnp.float32(AREA[i]), area)
    weight = field_weight[...] * area
    against = truth[member]
    members = fr[...]
    gap = members - against[None]
    square = gap * gap + DELTA * DELTA
    root = lax.rsqrt(square)
    miss = jnp.sum(square * root - DELTA, axis=0)
    slope_miss = gap * root
    apart = jnp.zeros((BLOCK, FIELDS), f32)
    pull = jnp.zeros((MEMBERS, BLOCK, FIELDS), f32)
    for n in range(MEMBERS):
        gap = members - fr[n][None]
        square = gap * gap + DELTA * DELTA
        root = lax.rsqrt(square)
        apart = apart + jnp.sum(square * root - DELTA, axis=0)
        pull = pull + gap * root
    cells = NLAT * LON * FIELDS
    spread = miss * (1.0 / MEMBERS) - apart * (1.0 / (2.0 * MEMBERS * (MEMBERS - 1)))
    cotangent = weight[None] * (slope_miss - pull * (1.0 / (MEMBERS - 1))) * (1.0 / (MEMBERS * math.sqrt(cells)))
    co_s[...] = cotangent.astype(bf16)
    back = []
    for d in range(1, MEMBERS):
        p = (member + d) % MEMBERS
        c = remote(co_s.at[p], co_r.at[member], ct_s.at[d - 1], ct_r.at[d - 1], others[d - 1])
        c.start()
        back.append(c)
    co_r[member] = co_s[member]
    total.loss_send(0, jnp.full((8, 128), jnp.sum(weight * spread) * (1.0 / cells), f32))
    for c in back:
        c.wait_recv()
    for p in range(MEMBERS):
        fcs[p * BLOCK : (p + 1) * BLOCK, :] = co_r[p].astype(f32)
    co[...] = fcs[...].astype(bf16)

    d_output = jnp.dot(co[...], hp[...], preferred_element_type=f32)
    for c in range(CHUNKS):
        dsum[c] = d_output[:, c * 128 : (c + 1) * 128]
    drr[...] = d_output.astype(bf16)

    def half_grad(base, left, right, which, out, then=()):
        for i, (s, wide) in enumerate(((0, 256), (256, 256), (512, 128))):
            columns = pl.ds(pl.multiple_of(which * 640 + s, 128), wide)
            part = contract(left[:, 0:640], right[:, columns], (0, 0))
            for h in range(wide // 128):
                j = base + (s // 128 + h) * TALL
                out[j : j + TALL] = part[:, h * 128 : (h + 1) * 128].reshape(TALL, 16, 128)
            if i in then:
                total.pair(then[i])

    def edge_grad(left, right, r):
        line = contract(left[:, 640:641], right[...], (0, 0))
        for j in range(2 * WIDE):
            small[1, j % 5, r + 2 + j // 5 : r + 3 + j // 5, :] = line[:, j * 128 : (j + 1) * 128]
        edge = contract(right[:, 1280:1282], left[...], (0, 0))
        for c in range(CHUNKS):
            small[1, c, r : r + 2, :] = edge[:, c * 128 : (c + 1) * 128]

    core = total.core
    half_grad(0, drr, hid, 1 - core, total.away, {1: 0, 2: 1})
    half_grad(0, drr, hid, core, total.own)
    pre[...] = jnp.dot(drr[:, 0:C], down_t[...], preferred_element_type=f32)

    @pl.loop(0, CELLS // 16)
    def _(r):
        rows = pl.ds(pl.multiple_of(r * 16, 16), 16)
        dp[rows, :] = (pre[rows, :] * slope[rows, :]).astype(bf16)

    total.scatter_0(0)
    total.scatter_0(1)
    half_grad(HALF, sc, dp, 1 - core, total.away, {1: 2, 2: 3})
    half_grad(HALF, sc, dp, core, total.own)
    total.loss_next(0)
    head_grad = contract(co[...], rd[...], (0, 0))
    for c in range(CHUNKS):
        small[0, c, 0:64, :] = head_grad[0:64, c * 128 : (c + 1) * 128]
        small[1, c, 0:8, :] = head_grad[64:72, c * 128 : (c + 1) * 128]
    total.scatter_0(2)
    total.scatter_0(3)
    edge_grad(drr, hid, 39)
    edge_grad(sc, dp, 34)
    put(dsc, contract(dp[...], up[...], (1, 1)))
    mean_a = jnp.zeros((CELLS, 128), f32)
    mean_b = jnp.zeros((CELLS, 128), f32)
    for c in range(CHUNKS):
        both = dsc[c] * nr[c]
        small[1, c, 33:34, :] = jnp.sum(both, axis=0, keepdims=True)
        mean_a = mean_a + dsc[c] * gn[c]
        mean_b = mean_b + both * gn[c]
    mean_a = jnp.sum(mean_a, axis=1, keepdims=True) * (1.0 / C)
    mean_b = jnp.sum(mean_b, axis=1, keepdims=True) * (1.0 / C)
    for c in range(CHUNKS):
        dsum[c] = dsum[c] + inv[...] * (dsc[c] * gn[c] - mean_a - nr[c] * mean_b)

    total.scatter_1(0)
    total.scatter_1(1)
    total.loss_next(1)

    @pl.loop(0, CHUNKS)
    def _(c):
        for a in range(5):
            acc = [jnp.zeros((8, 128), f32) for _ in range(5)]
            for i in range(ROWS):
                for t in range(LON // 8):
                    d = dsum[c, i * LON + 8 * t : i * LON + 8 * t + 8, :]
                    for b in range(5):
                        acc[b] = acc[b] + d * win[c, i + a, 6 + b + 8 * t : 14 + b + 8 * t, :]
            for b in range(5):
                tap = 8 + 5 * a + b
                small[1, c, tap : tap + 1, :] = jnp.sum(acc[b], axis=0, keepdims=True)

    for c in range(CHUNKS):
        units = slice(SMALL + c * SMALL_TALL, SMALL + (c + 1) * SMALL_TALL)
        total.away[units] = small[1 - core, c].reshape(SMALL_TALL, 16, 128)
        total.own[units] = small[core, c].reshape(SMALL_TALL, 16, 128)
    total.pair(4)
    total.scatter_2(0)
    total.scatter_0(4)
    total.scatter_1(2)
    total.scatter_1(3)
    total.loss_next(2)
    total.scatter_1(4)
    total.gather_2(0)
    total.scatter_2(1)
    total.gather_1(0)
    total.gather_1(1)
    total.gather_2(1)
    total.gather_0(0)
    total.gather_0(1)
    total.gather_1(2)
    total.gather_1(3)
    total.gather_1(4)
    for part in (2, 3, 4):
        total.gather_0(part)
    for part in range(5):
        total.hand_over(part)
    total.finish()
    loss_ref[...] = total.loss_take(3)

    @pl.loop(0, CHUNKS - 1)
    def _(c):
        for copy in halo(c):
            copy.wait_send()

    for c in list(thin) + sent + back + total.open:
        c.wait_send()


def gradients(state, conv_kernel, gain, up, down_t, head_t, target, field_weight):
    f32, bf16 = jnp.float32, jnp.bfloat16
    vmem = pl.BlockSpec(memory_space=pltpu.VMEM)
    anywhere = pl.BlockSpec(memory_space=pltpu.HBM)
    V = pltpu.VMEM
    dma = pltpu.SemaphoreType.DMA
    work = dict(
        win=V((CHUNKS, 6, 176, 128), f32),
        ck=V((CHUNKS, 25, 128), f32),
        gn=V((CHUNKS, 1, 128), f32),
        su=V((CHUNKS, CELLS, 128), f32),
        nr=V((CHUNKS, CELLS, 128), f32),
        inv=V((CELLS, 1), f32),
        sc=V((CELLS, 768), bf16),
        rd=V((CELLS, 768), bf16),
        pre=V((CELLS, HID), f32),
        slope=V((CELLS, HID), f32),
        hid=V((CELLS, HID), bf16),
        hp=V((FIELDS, 768), bf16),
        fcs=V((CELLS, FIELDS), f32),
        fs=V((MEMBERS, BLOCK, FIELDS), f32),
        fr=V((MEMBERS, BLOCK, FIELDS), f32),
        truth=V((MEMBERS, BLOCK, FIELDS), f32),
        co_s=V((MEMBERS, BLOCK, FIELDS), bf16),
        co_r=V((MEMBERS, BLOCK, FIELDS), bf16),
        co=V((CELLS, FIELDS), bf16),
        dp=V((CELLS, HID), bf16),
        dsum=V((CHUNKS, CELLS, 128), f32),
        dsc=V((CHUNKS, CELLS, 128), f32),
        small=V((2, CHUNKS, 64, 128), f32),
        thin_s=V((8, LON), f32),
        thin_r=V((2, 8, LON), f32),
        up=V((C, HID), bf16),
        down_t=V((C, HID), bf16),
        drr=V((CELLS, 768), bf16),
        halo_s=dma((2, CHUNKS)),
        halo_r=dma((2, CHUNKS)),
        fc_s=dma((MEMBERS - 1,)),
        fc_r=dma((MEMBERS - 1,)),
        ct_s=dma((MEMBERS - 1,)),
        ct_r=dma((MEMBERS - 1,)),
        wt=dma((8,)),
        state=V((ROWS, LON, C), f32),
        conv_kernel=V((25, C), f32),
        gain=V((C,), f32),
        head_t=V((FIELDS, C), bf16),
        target=V((FIELDS, ROWS, LON), f32),
        field_weight=V((1, FIELDS), f32),
    )
    refs, tree = jax.tree.flatten((work, total_scratch()))

    def kernel(*args):
        step_kernel(*args[:10], *jax.tree.unflatten(tree, args[10:]))

    return pl.pallas_call(
        kernel,
        out_shape=(
            jax.ShapeDtypeStruct((2, UNITS, 16, 128), bf16),
            jax.ShapeDtypeStruct((8, 128), f32),
        ),
        in_specs=[anywhere] * 8,
        out_specs=(vmem, vmem),
        scratch_shapes=refs,
        compiler_params=pltpu.CompilerParams(
            collective_id=0, has_side_effects=True, vmem_limit_bytes=48 * 1024 * 1024
        ),
    )(
        *(
            pltpu.with_memory_space_constraint(a, pltpu.HBM)
            for a in (state, conv_kernel, gain, up, down_t, head_t, target, field_weight)
        )
    )


def unpack_kernel(g_ref, loss, up_hbm, down_hbm, head_ref, kern_ref, gain_ref, loss_ref, up_ref, down_ref, small, sem):
    for core in range(2):
        for c in range(CHUNKS):
            start = SMALL + c * SMALL_TALL
            piece = g_ref[core, start : start + SMALL_TALL].astype(jnp.float32)
            small[core, :, c * 128 : (c + 1) * 128] = piece.reshape(64, 128)
    copies = []
    for m, r, out, hbm in ((0, 39, down_ref, down_hbm), (1, 34, up_ref, up_hbm)):
        edge = small[1, 32:56, :]
        out[:, 1280:1282] = jnp.transpose(edge)[0:C, r - 32 : r - 30]
        out[640:641, 0:640] = small[1, r + 2 : r + 3, 0:640]
        out[640:641, 640:1280] = small[1, r + 3 : r + 4, 0:640]
        for b in range(5):
            for core in range(2):
                for j in range(WIDE):
                    start = m * HALF + j * TALL + b * 8
                    piece = g_ref[core, start : start + 8].astype(jnp.float32)
                    lane = (core * WIDE + j) * 128
                    out[b * 128 : (b + 1) * 128, lane : lane + 128] = piece.reshape(128, 128)
            rows = pl.ds(b * 128, 128 if b < 4 else 129)
            copies.append(pltpu.make_async_copy(out.at[rows], hbm.at[rows], sem.at[m * 5 + b]))
            copies[-1].start()
    head_ref[0:64, :] = small[0, :, 0:C]
    head_ref[64:72, :] = small[1, 0:8, 0:C]
    kern_ref[...] = small[1, 8:33, 0:C]
    gain_ref[...] = small[1, 33:34, 0:C].reshape(C)
    loss_ref[...] = loss[0:1, 0:1]
    for c in copies:
        c.wait()


def unpacked(g, loss):
    vmem = pl.BlockSpec(memory_space=pltpu.VMEM)
    hbm = pl.BlockSpec(memory_space=pl.ANY)
    shapes = ((C, HID), (C, HID), (FIELDS, C), (25, C), (C,), (1, 1))
    return pl.pallas_call(
        unpack_kernel,
        out_shape=tuple(jax.ShapeDtypeStruct(s, jnp.float32) for s in shapes),
        in_specs=[vmem, vmem],
        out_specs=(hbm, hbm, vmem, vmem, vmem, vmem),
        scratch_shapes=[
            pltpu.VMEM((C, HID), jnp.float32),
            pltpu.VMEM((C, HID), jnp.float32),
            pltpu.VMEM((2, 64, 768), jnp.float32),
            pltpu.SemaphoreType.DMA((10,)),
        ],
        compiler_params=pltpu.CompilerParams(vmem_limit_bytes=24 * 1024 * 1024),
    )(g, loss)


def local(
    state, conv_kernel, norm_gain, up_weight, down_weight, field_head_weight, target, field_weight
):
    total, loss = gradients(
        jnp.transpose(state[0], (1, 2, 0)),
        conv_kernel,
        norm_gain,
        up_weight,
        down_weight.T,
        field_head_weight.T,
        target,
        field_weight[None],
    )
    up, down_t, head_t, kern, gain_row, loss = unpacked(total, loss)
    return (loss.reshape(()), kern, gain_row, up, down_t.T, head_t.T)


def solution(mesh):
    finer = Mesh(mesh.devices.reshape(4, 2, 2, 2, 8), AXES)
    mem, lat = AXES[:3], AXES[3:]
    in_specs = (P(mem, None, lat, None), P(), P(), P(), P(), P(), P(None, lat, None), P())
    out_specs = (P(), P(), P(), P(), P(), P())
    return jax.shard_map(local, mesh=finer, in_specs=in_specs, out_specs=out_specs, check_vma=False)
```

```python
import math

import jax
import jax.numpy as jnp
import numpy as np
from jax import lax
from jax.experimental import pallas as pl
from jax.experimental.pallas import tpu as pltpu
from jax.sharding import Mesh
from jax.sharding import PartitionSpec as P

AXES = ("mem_0", "mem_1", "mem_2", "lat_0", "lat_1")
MESH_ID = pl.DeviceIdType.MESH
ROWS = 2
LON = 160
CELLS = ROWS * LON
C = 641
HID = 1282
FIELDS = 72
MEMBERS = 16
NLAT = 32
BLOCK = CELLS // MEMBERS
CHUNKS = 6
DELTA = 0.1
EPSILON = 1e-05
AREA = np.cos(
    np.float32(0.5 * math.pi)
    * ((np.arange(NLAT, dtype=np.float32) + np.float32(0.5)) / np.float32(NLAT) - np.float32(1.0))
)

TALL, WIDE = 40, 5
HALF = TALL * WIDE
SMALL = 2 * HALF
SMALL_TALL = 4
UNITS = SMALL + SMALL_TALL * CHUNKS
SIZE = {"x": 4, "y": 4, "z": 8}
PARTS = ((0, 100, "xy"), (100, 100, "yx"), (200, 100, "xy"), (300, 100, "yx"), (400, 24, "xy"))
GROUPS = ((0, 1), (2, 3), (4,))


def levels_of(size, order):
    levels = []
    for a in order:
        size = -(-size // SIZE[a])
        levels.append((a, SIZE[a], size))
    return levels


PLANS = tuple((off, size, levels_of(size, order)) for off, size, order in PARTS)


def group_of(group):
    starts, at = {}, 0
    for k in GROUPS[group]:
        starts[k] = at
        at += PLANS[k][2][1][2]
    return starts, at, -(-at // SIZE["z"])


def contract(left, right, dims):
    return lax.dot_general(left, right, ((dims[:1], dims[1:]), ((), ())), preferred_element_type=jnp.float32)


def put(ref, value):
    for c in range(CHUNKS - 1):
        ref[c] = value[:, c * 128 : (c + 1) * 128]
    ref[CHUNKS - 1, :, 0:1] = value[:, 640:641]


def member_device(m):
    return {"mem_0": m // 4, "mem_1": (m // 2) % 2, "mem_2": m % 2}


def device_at(axis, p):
    if axis == "x":
        return {"mem_0": p}
    if axis == "y":
        return {"lat_0": p // 2, "mem_1": p % 2}
    return {"lat_1": p}


def remote(src, dst, s, r, dev):
    return pltpu.make_async_remote_copy(
        src_ref=src, dst_ref=dst, send_sem=s, recv_sem=r, device_id=dev, device_id_type=MESH_ID
    )


class Total:
    def __init__(self, g_ref, own, away, core_in, parts, groups, loss_in, sems):
        self.g, self.own, self.away, self.core_in, self.parts, self.loss_in = g_ref, own, away, core_in, parts, loss_in
        self.sems, self.groups, self.last = sems, groups, []
        self.core = lax.axis_index("mem_2")
        self.sibling = {"mem_2": 1 - self.core}
        self.at = {
            "x": lax.axis_index("mem_0"),
            "y": lax.axis_index("lat_0") * 2 + lax.axis_index("mem_1"),
            "z": lax.axis_index("lat_1"),
        }
        self.open = []
        self.first = {}
        self.running = {}

    def peers(self):
        out = []
        for a in "yz":
            out += [device_at(a, (self.at[a] + d) % SIZE[a]) for d in range(1, SIZE[a])]
        return out

    def begin(self, src, dst, s, r, dev):
        c = remote(src, dst, s, r, dev)
        c.start()
        self.open.append(c)
        return c

    def loss_send(self, level, value):
        base, sbase = (0, 2, 6, 10)[level], (0, 1, 4, 7)[level]
        ls, lr = self.sems["loss"]
        if level == 0:
            devices = [self.sibling]
        else:
            a = "xyz"[level - 1]
            devices = [device_at(a, (self.at[a] + d) % SIZE[a]) for d in range(1, SIZE[a])]
        self.loss_in[base] = value
        self.loss_open = [
            self.begin(self.loss_in.at[base], self.loss_in.at[base + 1 + d], ls.at[sbase + d], lr.at[sbase + d], dev)
            for d, dev in enumerate(devices)
        ]

    def loss_take(self, level):
        base = (0, 2, 6, 10)[level]
        for c in self.loss_open:
            c.wait_recv()
        total = self.loss_in[base]
        for d in range(len(self.loss_open)):
            total = total + self.loss_in[base + 1 + d]
        return total

    def loss_next(self, level):
        self.loss_send(level + 1, self.loss_take(level))

    def pair(self, k):
        off, size = PLANS[k][:2]
        s, r = self.sems["pair"]
        units = pl.ds(off, size)
        self.first[k] = self.begin(self.away.at[units], self.core_in.at[units], s.at[k], r.at[k], self.sibling)

    def held(self, start, count):
        return self.own[pl.ds(start, count)] + self.core_in[pl.ds(start, count)]

    def arrive(self, key):
        for c in self.running[key]:
            c.wait_recv()
        self.running[key] = []

    def spread(self, key, send, recv, sems, row, axis, u):
        s, r = self.sems[sems]
        n = SIZE[axis]
        self.running[key] = []
        for d in range(1, n):
            p = (self.at[axis] + d) % n
            self.running[key].append(
                self.begin(send.at[pl.ds(p * u, u)], recv.at[d - 1], s.at[row, d - 1], r.at[row, d - 1], device_at(axis, p))
            )

    def share(self, key, source, into, sems, row, axis, start):
        s, r = self.sems[sems]
        n = SIZE[axis]
        self.running[key] = [
            self.begin(
                source, into.at[start], s.at[row, d - 1], r.at[row, d - 1], device_at(axis, (self.at[axis] + d) % n)
            )
            for d in range(1, n)
        ]

    def scatter_0(self, k):
        off, size, levels = PLANS[k]
        a, n, u = levels[0]
        send, recv = self.parts[k][:2]
        self.first[k].wait_recv()
        send[...] = self.held(off, size).astype(jnp.bfloat16)
        self.spread(k, send, recv, "scatter_0", k, a, u)

    def scatter_1(self, k):
        off, size, levels = PLANS[k]
        a, n, below = levels[0]
        b, m, u = levels[1]
        came, total, send, recv = self.parts[k][1:5]
        self.arrive(k)
        value = self.held(off + self.at[a] * below, below)
        for d in range(n - 1):
            value = value + came[d].astype(jnp.float32)
        total[0:below] = value
        if m * u > below:
            total[below:] = jnp.zeros((m * u - below, 16, 128), jnp.float32)
        send[...] = total[...].astype(jnp.bfloat16)
        self.spread(k, send, recv, "scatter_1", k, b, u)

    def scatter_2(self, group):
        starts, used, u = group_of(group)
        total, send, recv = self.groups[group][:3]
        if 8 * u > used:
            total[used:] = jnp.zeros((8 * u - used, 16, 128), jnp.float32)
        for k in GROUPS[group]:
            b, m, below = PLANS[k][2][1]
            held, came = self.parts[k][2], self.parts[k][4]
            self.arrive(k)
            value = held[pl.ds(self.at[b] * below, below)]
            for d in range(m - 1):
                value = value + came[d].astype(jnp.float32)
            total[starts[k] : starts[k] + below] = value
        send[...] = total[...].astype(jnp.bfloat16)
        self.spread(("z", group), send, recv, "scatter_2", group, "z", u)

    def gather_2(self, group):
        starts, used, u = group_of(group)
        total, send, recv, into = self.groups[group]
        self.arrive(("z", group))
        mine = pl.ds(self.at["z"] * u, u)
        value = total[mine]
        for d in range(7):
            value = value + recv[d].astype(jnp.float32)
        into[mine] = value.astype(jnp.bfloat16)
        self.share(("z", group), into.at[mine], into, "gather_2", group, "z", mine)

    def gather_1(self, k):
        group = [g for g, members in enumerate(GROUPS) if k in members][0]
        b, m, u = PLANS[k][2][1]
        start = group_of(group)[0][k]
        source, into = self.groups[group][3], self.parts[k][5]
        self.arrive(("z", group))
        mine = pl.ds(self.at[b] * u, u)
        into[mine] = source[start : start + u]
        self.share(k, source.at[pl.ds(start, u)], into, "gather_1", k, b, mine)

    def to_sibling(self, k, i, start, count):
        s, r = self.sems["back"]
        piece = self.g.at[self.core, pl.ds(start, count)]
        self.last.append(self.begin(piece, piece, s.at[k, i], r.at[k, i], self.sibling))

    def gather_0(self, k):
        off, size, levels = PLANS[k]
        a, n, u = levels[0]
        source = self.parts[k][5]
        self.arrive(k)
        mine = pl.ds(off + self.at[a] * u, u)
        self.g[self.core, mine] = source[0:u]
        self.share(k, source.at[pl.ds(0, u)], self.g.at[self.core], "gather_0", k, a, mine)
        self.to_sibling(k, 0, off + self.at[a] * u, u)

    def hand_over(self, k):
        off, size, levels = PLANS[k]
        a, n, u = levels[0]
        for d in range(1, n):
            self.running[k][d - 1].wait_recv()
            self.to_sibling(k, d, off + ((self.at[a] + n - d) % n) * u, u)

    def finish(self):
        for c in self.last:
            c.wait_recv()


def total_scratch():
    bf16, f32 = jnp.bfloat16, jnp.float32
    V = pltpu.VMEM
    parts, groups = [], []
    for off, size, levels in PLANS:
        (a, n, u), (b, m, v) = levels
        parts.append(
            [
                V((size, 16, 128), bf16),
                V((n - 1, u, 16, 128), bf16),
                V((m * v, 16, 128), f32),
                V((m * v, 16, 128), bf16),
                V((m - 1, v, 16, 128), bf16),
                V((m * v, 16, 128), bf16),
            ]
        )
    for group in range(len(GROUPS)):
        u = group_of(group)[2]
        groups.append(
            [V((8 * u, 16, 128), f32), V((8 * u, 16, 128), bf16), V((7, u, 16, 128), bf16), V((8 * u, 16, 128), bf16)]
        )
    dma = pltpu.SemaphoreType.DMA
    count = len(PLANS)
    pairs = dict(
        pair=(count,),
        scatter_0=(count, 3),
        scatter_1=(count, 3),
        scatter_2=(3, 7),
        gather_2=(3, 7),
        gather_1=(count, 3),
        gather_0=(count, 3),
        back=(count, 4),
        loss=(14,),
    )
    return dict(
        own=V((UNITS, 16, 128), f32),
        away=V((UNITS, 16, 128), f32),
        core_in=V((UNITS, 16, 128), f32),
        parts=parts,
        groups=groups,
        loss_in=V((18, 8, 128), f32),
        sems={name: (dma(shape), dma(shape)) for name, shape in pairs.items()},
    )


def step_kernel(
    state_hbm,
    conv_hbm,
    gain_hbm,
    up_hbm,
    down_hbm,
    head_hbm,
    target_hbm,
    field_hbm,
    g_ref,
    loss_ref,
    w,
    total_refs,
):
    win, ck, gn, su, nr, inv, sc, rd = (w[i] for i in ("win", "ck", "gn", "su", "nr", "inv", "sc", "rd"))
    pre, slope, hid, hp, fcs, fs, fr = (w[i] for i in ("pre", "slope", "hid", "hp", "fcs", "fs", "fr"))
    truth, co_s, co_r, co, dp, dsum, dsc = (w[i] for i in ("truth", "co_s", "co_r", "co", "dp", "dsum", "dsc"))
    small, thin_s, thin_r, up, down_t, drr = (w[i] for i in ("small", "thin_s", "thin_r", "up", "down_t", "drr"))
    halo_s, halo_r, fc_s, fc_r, ct_s, ct_r, wt = (w[i] for i in ("halo_s", "halo_r", "fc_s", "fc_r", "ct_s", "ct_r", "wt"))
    total = Total(g_ref, **total_refs)
    f32, bf16 = jnp.float32, jnp.bfloat16
    lat = lax.axis_index("lat_0") * 8 + lax.axis_index("lat_1")
    member = lax.axis_index("mem_0") * 4 + lax.axis_index("mem_1") * 2 + lax.axis_index("mem_2")

    def lat_device(d):
        p = (lat + d) % 16
        return {"lat_0": p // 8, "lat_1": p % 8}

    above, below = lat_device(1), lat_device(15)
    others = [member_device((member + d) % MEMBERS) for d in range(1, MEMBERS)]
    barrier = pltpu.get_barrier_semaphore()
    greeted = [above, below] + others + total.peers()
    for dev in greeted:
        pl.semaphore_signal(barrier, inc=1, device_id=dev, device_id_type=MESH_ID)
    state, conv_kernel, gain, head_t, target, field_weight = (
        w[i] for i in ("state", "conv_kernel", "gain", "head_t", "target", "field_weight")
    )
    loads = [
        pltpu.make_async_copy(src, dst, wt.at[i])
        for i, (src, dst) in enumerate(
            (
                (state_hbm, state),
                (conv_hbm, conv_kernel),
                (gain_hbm, gain),
                (head_hbm, head_t),
                (target_hbm, target),
                (field_hbm, field_weight),
                (up_hbm, up),
                (down_hbm, down_t),
            )
        )
    ]
    for c in loads:
        c.start()
    weights = loads[6:]

    win[CHUNKS - 1] = jnp.zeros((6, 176, 128), f32)
    loads[0].wait()
    for c in range(CHUNKS - 1):
        win[c, 2:4, 8:168, :] = state[:, :, c * 128 : (c + 1) * 128]
    win[CHUNKS - 1, 2:4, 8:168, 0:1] = state[:, :, 640:641]
    thin_s[...] = jnp.zeros((8, LON), f32)
    for i in range(ROWS):
        thin_s[i : i + 1, :] = jnp.transpose(win[CHUNKS - 1, 2 + i, 8:168, :])[0:1, :]
    pl.semaphore_wait(barrier, len(greeted))

    def halo(c):
        mine = win.at[c, 2:4, 8:168]
        return (
            remote(mine, win.at[c, 0:2, 8:168], halo_s.at[0, c], halo_r.at[0, c], above),
            remote(mine, win.at[c, 4:6, 8:168], halo_s.at[1, c], halo_r.at[1, c], below),
        )

    thin = (
        remote(thin_s, thin_r.at[0], halo_s.at[0, CHUNKS - 1], halo_r.at[0, CHUNKS - 1], above),
        remote(thin_s, thin_r.at[1], halo_s.at[1, CHUNKS - 1], halo_r.at[1, CHUNKS - 1], below),
    )
    for copy in thin:
        copy.start()

    @pl.loop(0, CHUNKS - 1)
    def _(c):
        for copy in halo(c):
            copy.start()

    for c in loads[1:6]:
        c.wait()
    ck[CHUNKS - 1] = jnp.zeros((25, 128), f32)
    put(ck, conv_kernel[...])
    gn[CHUNKS - 1] = jnp.zeros((1, 128), f32)
    put(gn, gain[...].reshape(1, C))
    hp[:, 640:768] = jnp.zeros((FIELDS, 128), bf16)
    hp[:, 0:641] = head_t[...]
    rd[:, 640:768] = jnp.zeros((CELLS, 128), bf16)
    su[CHUNKS - 1] = jnp.zeros((CELLS, 128), f32)
    dsc[CHUNKS - 1] = jnp.zeros((CELLS, 128), f32)
    small[...] = jnp.zeros((2, CHUNKS, 64, 128), f32)
    for i in range(ROWS):
        columns = jnp.transpose(target[:, i, :])
        for b in range(MEMBERS // ROWS):
            truth[i * (MEMBERS // ROWS) + b] = columns[b * BLOCK : (b + 1) * BLOCK, :]

    def wrap(c, rows):
        win[c, rows, 6:8, :] = win[c, rows, 166:168, :]
        win[c, rows, 168:170, :] = win[c, rows, 8:10, :]

    def taps(c, i, rows, acc):
        for a in rows:
            for b in range(5):
                acc = acc + ck[c, 5 * a + b : 5 * a + b + 1, :] * win[c, i + a, 6 + b : 166 + b, :]
        return acc

    own = ((2, 3), (1, 2))
    met = ((0, 1, 4), (0, 3, 4))

    @pl.loop(0, CHUNKS)
    def _(c):
        wrap(c, slice(2, 4))
        for i in range(ROWS):
            su[c, i * LON : (i + 1) * LON] = taps(c, i, own[i], win[c, 2 + i, 8:168, :])

    def meet(c):
        @pl.when(lat == 0)
        def _():
            win[c, 0:2] = jnp.zeros((2, 176, 128), f32)

        @pl.when(lat == 15)
        def _():
            win[c, 4:6] = jnp.zeros((2, 176, 128), f32)

        wrap(c, slice(0, 2))
        wrap(c, slice(4, 6))
        for i in range(ROWS):
            su[c, i * LON : (i + 1) * LON] = taps(c, i, met[i], su[c, i * LON : (i + 1) * LON])

    for side, copy in enumerate(thin):
        copy.wait_recv()
        column = jnp.transpose(thin_r[side])
        for i in range(ROWS):
            win[CHUNKS - 1, 4 * side + i, 8:168, 0:1] = column[:, i : i + 1]
    meet(CHUNKS - 1)

    @pl.loop(0, CHUNKS - 1)
    def _(c):
        for copy in halo(c):
            copy.wait_recv()
        meet(c)

    level = su[0]
    for c in range(1, CHUNKS):
        level = level + su[c]
    mean = jnp.sum(level, axis=1, keepdims=True) * (1.0 / C)
    first_lane = (lax.broadcasted_iota(jnp.int32, (CELLS, 128), 1) < 1).astype(f32)
    square = jnp.zeros((CELLS, 128), f32)
    for c in range(CHUNKS):
        center = su[c] - mean
        if c == CHUNKS - 1:
            center = center * first_lane
        nr[c] = center
        square = square + center * center
    inverse = lax.rsqrt(jnp.sum(square, axis=1, keepdims=True) * (1.0 / C) + EPSILON)
    inv[...] = inverse
    for c in range(CHUNKS):
        normed = nr[c] * inverse
        nr[c] = normed
        sc[:, c * 128 : (c + 1) * 128] = (normed * gn[c]).astype(bf16)

    for c in weights:
        c.wait()
    pre[...] = jnp.dot(sc[:, 0:C], up[...], preferred_element_type=f32)

    @pl.loop(0, CELLS // 16)
    def _(r):
        rows = pl.ds(pl.multiple_of(r * 16, 16), 16)
        x = pre[rows, :]
        cumul = 0.5 * (1.0 + lax.erf(x * (1.0 / math.sqrt(2.0))))
        density = jnp.exp(-0.5 * x * x) * (1.0 / math.sqrt(2.0 * math.pi))
        hid[rows, :] = (x * cumul).astype(bf16)
        slope[rows, :] = cumul + x * density

    mlp = contract(hid[...], down_t[...], (1, 1))
    for c in range(CHUNKS - 1):
        at = slice(c * 128, (c + 1) * 128)
        rd[:, at] = (su[c] + mlp[:, at]).astype(bf16)
    rd[:, 640:641] = (su[CHUNKS - 1, :, 0:1] + mlp[:, 640:641]).astype(bf16)
    fcs[...] = contract(rd[...], hp[...], (1, 1))

    for p in range(MEMBERS):
        fs[p] = fcs[p * BLOCK : (p + 1) * BLOCK, :]
    sent = []
    for d in range(1, MEMBERS):
        p = (member + d) % MEMBERS
        c = remote(fs.at[p], fr.at[member], fc_s.at[d - 1], fc_r.at[d - 1], others[d - 1])
        c.start()
        sent.append(c)
    fr[member] = fs[member]
    for c in sent:
        c.wait_recv()

    row = 2 * lat + member // (MEMBERS // ROWS)
    area = jnp.float32(AREA[0])
    for i in range(1, NLAT):
        area = jnp.where(row == i, jnp.float32(AREA[i]), area)
    weight = field_weight[...] * area
    against = truth[member]
    members = fr[...]
    gap = members - against[None]
    square = gap * gap + DELTA * DELTA
    root = lax.rsqrt(square)
    miss = jnp.sum(square * root - DELTA, axis=0)
    slope_miss = gap * root
    apart = jnp.zeros((BLOCK, FIELDS), f32)
    pull = jnp.zeros((MEMBERS, BLOCK, FIELDS), f32)
    for n in range(MEMBERS):
        gap = members - fr[n][None]
        square = gap * gap + DELTA * DELTA
        root = lax.rsqrt(square)
        apart = apart + jnp.sum(square * root - DELTA, axis=0)
        pull = pull + gap * root
    cells = NLAT * LON * FIELDS
    spread = miss * (1.0 / MEMBERS) - apart * (1.0 / (2.0 * MEMBERS * (MEMBERS - 1)))
    cotangent = weight[None] * (slope_miss - pull * (1.0 / (MEMBERS - 1))) * (1.0 / (MEMBERS * math.sqrt(cells)))
    co_s[...] = cotangent.astype(bf16)
    back = []
    for d in range(1, MEMBERS):
        p = (member + d) % MEMBERS
        c = remote(co_s.at[p], co_r.at[member], ct_s.at[d - 1], ct_r.at[d - 1], others[d - 1])
        c.start()
        back.append(c)
    co_r[member] = co_s[member]
    total.loss_send(0, jnp.full((8, 128), jnp.sum(weight * spread) * (1.0 / cells), f32))
    for c in back:
        c.wait_recv()
    for p in range(MEMBERS):
        fcs[p * BLOCK : (p + 1) * BLOCK, :] = co_r[p].astype(f32)
    co[...] = fcs[...].astype(bf16)

    d_output = jnp.dot(co[...], hp[...], preferred_element_type=f32)
    for c in range(CHUNKS):
        dsum[c] = d_output[:, c * 128 : (c + 1) * 128]
    drr[...] = d_output.astype(bf16)

    def half_grad(base, left, right, which, out, then=()):
        for i, (s, wide) in enumerate(((0, 256), (256, 256), (512, 128))):
            columns = pl.ds(pl.multiple_of(which * 640 + s, 128), wide)
            part = contract(left[:, 0:640], right[:, columns], (0, 0))
            for h in range(wide // 128):
                j = base + (s // 128 + h) * TALL
                out[j : j + TALL] = part[:, h * 128 : (h + 1) * 128].reshape(TALL, 16, 128)
            if i in then:
                total.pair(then[i])

    def edge_grad(left, right, r):
        line = contract(left[:, 640:641], right[...], (0, 0))
        for j in range(2 * WIDE):
            small[1, j % 5, r + 2 + j // 5 : r + 3 + j // 5, :] = line[:, j * 128 : (j + 1) * 128]
        edge = contract(right[:, 1280:1282], left[...], (0, 0))
        for c in range(CHUNKS):
            small[1, c, r : r + 2, :] = edge[:, c * 128 : (c + 1) * 128]

    core = total.core
    half_grad(0, drr, hid, 1 - core, total.away, {1: 0, 2: 1})
    half_grad(0, drr, hid, core, total.own)
    pre[...] = jnp.dot(drr[:, 0:C], down_t[...], preferred_element_type=f32)

    @pl.loop(0, CELLS // 16)
    def _(r):
        rows = pl.ds(pl.multiple_of(r * 16, 16), 16)
        dp[rows, :] = (pre[rows, :] * slope[rows, :]).astype(bf16)

    total.scatter_0(0)
    total.scatter_0(1)
    half_grad(HALF, sc, dp, 1 - core, total.away, {1: 2, 2: 3})
    half_grad(HALF, sc, dp, core, total.own)
    total.loss_next(0)
    head_grad = contract(co[...], rd[...], (0, 0))
    for c in range(CHUNKS):
        small[0, c, 0:64, :] = head_grad[0:64, c * 128 : (c + 1) * 128]
        small[1, c, 0:8, :] = head_grad[64:72, c * 128 : (c + 1) * 128]
    total.scatter_0(2)
    total.scatter_0(3)
    put(dsc, contract(dp[...], up[...], (1, 1)))
    mean_a = jnp.zeros((CELLS, 128), f32)
    mean_b = jnp.zeros((CELLS, 128), f32)
    for c in range(CHUNKS):
        both = dsc[c] * nr[c]
        small[1, c, 33:34, :] = jnp.sum(both, axis=0, keepdims=True)
        mean_a = mean_a + dsc[c] * gn[c]
        mean_b = mean_b + both * gn[c]
    mean_a = jnp.sum(mean_a, axis=1, keepdims=True) * (1.0 / C)
    mean_b = jnp.sum(mean_b, axis=1, keepdims=True) * (1.0 / C)
    for c in range(CHUNKS):
        dsum[c] = dsum[c] + inv[...] * (dsc[c] * gn[c] - mean_a - nr[c] * mean_b)

    total.scatter_1(0)
    total.scatter_1(1)
    total.loss_next(1)
    edge_grad(drr, hid, 39)
    edge_grad(sc, dp, 34)

    @pl.loop(0, CHUNKS)
    def _(c):
        for a in range(5):
            acc = [jnp.zeros((8, 128), f32) for _ in range(5)]
            for i in range(ROWS):
                for t in range(LON // 8):
                    d = dsum[c, i * LON + 8 * t : i * LON + 8 * t + 8, :]
                    for b in range(5):
                        acc[b] = acc[b] + d * win[c, i + a, 6 + b + 8 * t : 14 + b + 8 * t, :]
            for b in range(5):
                tap = 8 + 5 * a + b
                small[1, c, tap : tap + 1, :] = jnp.sum(acc[b], axis=0, keepdims=True)

    for c in range(CHUNKS):
        units = slice(SMALL + c * SMALL_TALL, SMALL + (c + 1) * SMALL_TALL)
        total.away[units] = small[1 - core, c].reshape(SMALL_TALL, 16, 128)
        total.own[units] = small[core, c].reshape(SMALL_TALL, 16, 128)
    total.pair(4)
    total.scatter_2(0)
    total.scatter_0(4)
    total.scatter_1(2)
    total.scatter_1(3)
    total.loss_next(2)
    total.gather_2(0)
    total.scatter_2(1)
    total.scatter_1(4)
    total.gather_1(0)
    total.gather_1(1)
    total.scatter_2(2)
    total.gather_2(1)
    total.gather_0(0)
    total.gather_0(1)
    total.gather_1(2)
    total.gather_1(3)
    total.gather_2(2)
    total.gather_0(2)
    total.gather_0(3)
    total.gather_1(4)
    total.hand_over(0)
    total.hand_over(1)
    total.gather_0(4)
    for part in (2, 3, 4):
        total.hand_over(part)
    total.finish()
    loss_ref[...] = total.loss_take(3)

    @pl.loop(0, CHUNKS - 1)
    def _(c):
        for copy in halo(c):
            copy.wait_send()

    for c in list(thin) + sent + back + total.open:
        c.wait_send()


def gradients(state, conv_kernel, gain, up, down_t, head_t, target, field_weight):
    f32, bf16 = jnp.float32, jnp.bfloat16
    vmem = pl.BlockSpec(memory_space=pltpu.VMEM)
    anywhere = pl.BlockSpec(memory_space=pltpu.HBM)
    V = pltpu.VMEM
    dma = pltpu.SemaphoreType.DMA
    work = dict(
        win=V((CHUNKS, 6, 176, 128), f32),
        ck=V((CHUNKS, 25, 128), f32),
        gn=V((CHUNKS, 1, 128), f32),
        su=V((CHUNKS, CELLS, 128), f32),
        nr=V((CHUNKS, CELLS, 128), f32),
        inv=V((CELLS, 1), f32),
        sc=V((CELLS, 768), bf16),
        rd=V((CELLS, 768), bf16),
        pre=V((CELLS, HID), f32),
        slope=V((CELLS, HID), f32),
        hid=V((CELLS, HID), bf16),
        hp=V((FIELDS, 768), bf16),
        fcs=V((CELLS, FIELDS), f32),
        fs=V((MEMBERS, BLOCK, FIELDS), f32),
        fr=V((MEMBERS, BLOCK, FIELDS), f32),
        truth=V((MEMBERS, BLOCK, FIELDS), f32),
        co_s=V((MEMBERS, BLOCK, FIELDS), bf16),
        co_r=V((MEMBERS, BLOCK, FIELDS), bf16),
        co=V((CELLS, FIELDS), bf16),
        dp=V((CELLS, HID), bf16),
        dsum=V((CHUNKS, CELLS, 128), f32),
        dsc=V((CHUNKS, CELLS, 128), f32),
        small=V((2, CHUNKS, 64, 128), f32),
        thin_s=V((8, LON), f32),
        thin_r=V((2, 8, LON), f32),
        up=V((C, HID), bf16),
        down_t=V((C, HID), bf16),
        drr=V((CELLS, 768), bf16),
        halo_s=dma((2, CHUNKS)),
        halo_r=dma((2, CHUNKS)),
        fc_s=dma((MEMBERS - 1,)),
        fc_r=dma((MEMBERS - 1,)),
        ct_s=dma((MEMBERS - 1,)),
        ct_r=dma((MEMBERS - 1,)),
        wt=dma((8,)),
        state=V((ROWS, LON, C), f32),
        conv_kernel=V((25, C), f32),
        gain=V((C,), f32),
        head_t=V((FIELDS, C), bf16),
        target=V((FIELDS, ROWS, LON), f32),
        field_weight=V((1, FIELDS), f32),
    )
    refs, tree = jax.tree.flatten((work, total_scratch()))

    def kernel(*args):
        step_kernel(*args[:10], *jax.tree.unflatten(tree, args[10:]))

    return pl.pallas_call(
        kernel,
        out_shape=(
            jax.ShapeDtypeStruct((2, UNITS, 16, 128), bf16),
            jax.ShapeDtypeStruct((8, 128), f32),
        ),
        in_specs=[anywhere] * 8,
        out_specs=(vmem, vmem),
        scratch_shapes=refs,
        compiler_params=pltpu.CompilerParams(
            collective_id=0, has_side_effects=True, vmem_limit_bytes=48 * 1024 * 1024
        ),
    )(
        *(
            pltpu.with_memory_space_constraint(a, pltpu.HBM)
            for a in (state, conv_kernel, gain, up, down_t, head_t, target, field_weight)
        )
    )


def unpack_kernel(g_ref, loss, *refs):
    hbm, (up_ref, down_ref, head_ref, kern_ref, gain_ref, loss_ref, small, sem) = refs[:6], refs[6:]
    copies = []

    def send(src, dst):
        copies.append(pltpu.make_async_copy(src, dst, sem.at[len(copies)]))
        copies[-1].start()

    loss_ref[...] = loss[0:1, 0:1]
    send(loss_ref, hbm[5])
    for core in range(2):
        for c in range(CHUNKS):
            start = SMALL + c * SMALL_TALL
            piece = g_ref[core, start : start + SMALL_TALL].astype(jnp.float32)
            small[core, :, c * 128 : (c + 1) * 128] = piece.reshape(64, 128)
    head_ref[0:64, :] = small[0, :, 0:C]
    head_ref[64:72, :] = small[1, 0:8, 0:C]
    send(head_ref, hbm[2])
    kern_ref[...] = small[1, 8:33, 0:C]
    send(kern_ref, hbm[3])
    gain_ref[...] = small[1, 33:34, 0:C].reshape(C)
    send(gain_ref, hbm[4])
    edge = jnp.transpose(small[1, 32:56, :])
    for m, r, out, target in ((0, 39, down_ref, hbm[1]), (1, 34, up_ref, hbm[0])):
        out[640:641, 0:640] = small[1, r + 2 : r + 3, 0:640]
        out[640:641, 640:1280] = small[1, r + 3 : r + 4, 0:640]
        for b in range(5):
            for core in range(2):
                for j in range(WIDE):
                    start = m * HALF + j * TALL + b * 8
                    piece = g_ref[core, start : start + 8].astype(jnp.float32)
                    lane = (core * WIDE + j) * 128
                    out[b * 128 : (b + 1) * 128, lane : lane + 128] = piece.reshape(128, 128)
            end = (b + 1) * 128 + (b == 4)
            out[b * 128 : end, 1280:1282] = edge[b * 128 : end, r - 32 : r - 30]
            rows = pl.ds(b * 128, end - b * 128)
            send(out.at[rows], target.at[rows])
    for c in copies:
        c.wait()


def unpacked(g, loss):
    vmem = pl.BlockSpec(memory_space=pltpu.VMEM)
    hbm = pl.BlockSpec(memory_space=pltpu.HBM)
    shapes = ((C, HID), (C, HID), (FIELDS, C), (25, C), (C,), (1, 1))
    return pl.pallas_call(
        unpack_kernel,
        out_shape=tuple(jax.ShapeDtypeStruct(s, jnp.float32) for s in shapes),
        in_specs=[vmem, vmem],
        out_specs=(hbm,) * 6,
        scratch_shapes=[pltpu.VMEM(s, jnp.float32) for s in shapes]
        + [pltpu.VMEM((2, 64, 768), jnp.float32), pltpu.SemaphoreType.DMA((14,))],
        compiler_params=pltpu.CompilerParams(vmem_limit_bytes=24 * 1024 * 1024),
    )(g, loss)


def local(
    state, conv_kernel, norm_gain, up_weight, down_weight, field_head_weight, target, field_weight
):
    total, loss = gradients(
        jnp.transpose(state[0], (1, 2, 0)),
        conv_kernel,
        norm_gain,
        up_weight,
        down_weight.T,
        field_head_weight.T,
        target,
        field_weight[None],
    )
    up, down_t, head_t, kern, gain_row, loss = unpacked(total, loss)
    return (loss.reshape(()), kern, gain_row, up, down_t.T, head_t.T)


def solution(mesh):
    finer = Mesh(mesh.devices.reshape(4, 2, 2, 2, 8), AXES)
    mem, lat = AXES[:3], AXES[3:]
    in_specs = (P(mem, None, lat, None), P(), P(), P(), P(), P(), P(None, lat, None), P())
    out_specs = (P(), P(), P(), P(), P(), P())
    return jax.shard_map(local, mesh=finer, in_specs=in_specs, out_specs=out_specs, check_vma=False)
```

```python
import math

import jax
import jax.numpy as jnp
import numpy as np
from jax import lax
from jax.experimental import pallas as pl
from jax.experimental.pallas import tpu as pltpu
from jax.sharding import Mesh
from jax.sharding import PartitionSpec as P

AXES = ("mem_0", "mem_1", "mem_2", "lat_0", "lat_1")
MESH_ID = pl.DeviceIdType.MESH
ROWS = 2
LON = 160
CELLS = ROWS * LON
C = 641
HID = 1282
FIELDS = 72
MEMBERS = 16
NLAT = 32
BLOCK = CELLS // MEMBERS
CHUNKS = 6
DELTA = 0.1
EPSILON = 1e-05
AREA = np.cos(
    np.float32(0.5 * math.pi)
    * ((np.arange(NLAT, dtype=np.float32) + np.float32(0.5)) / np.float32(NLAT) - np.float32(1.0))
)

TALL, WIDE = 40, 5
HALF = TALL * WIDE
SMALL = 2 * HALF
SMALL_TALL = 4
UNITS = SMALL + SMALL_TALL * CHUNKS
SIZE = {"x": 4, "y": 4, "z": 8}
PARTS = ((0, 100, "xy"), (100, 100, "yx"), (200, 100, "xy"), (300, 100, "yx"), (400, 24, "xy"))
GROUPS = ((0, 1), (2, 3, 4))


def levels_of(size, order):
    levels = []
    for a in order:
        size = -(-size // SIZE[a])
        levels.append((a, SIZE[a], size))
    return levels


PLANS = tuple((off, size, levels_of(size, order)) for off, size, order in PARTS)


def group_of(group):
    starts, at = {}, 0
    for k in GROUPS[group]:
        starts[k] = at
        at += PLANS[k][2][1][2]
    return starts, at, -(-at // SIZE["z"])


def contract(left, right, dims):
    return lax.dot_general(left, right, ((dims[:1], dims[1:]), ((), ())), preferred_element_type=jnp.float32)


def put(ref, value):
    for c in range(CHUNKS - 1):
        ref[c] = value[:, c * 128 : (c + 1) * 128]
    ref[CHUNKS - 1, :, 0:1] = value[:, 640:641]


def member_device(m):
    return {"mem_0": m // 4, "mem_1": (m // 2) % 2, "mem_2": m % 2}


def device_at(axis, p):
    if axis == "x":
        return {"mem_0": p}
    if axis == "y":
        return {"lat_0": p // 2, "mem_1": p % 2}
    return {"lat_1": p}


def remote(src, dst, s, r, dev):
    return pltpu.make_async_remote_copy(
        src_ref=src, dst_ref=dst, send_sem=s, recv_sem=r, device_id=dev, device_id_type=MESH_ID
    )


class Total:
    def __init__(self, g_ref, own, away, core_in, parts, groups, loss_in, sems):
        self.g, self.own, self.away, self.core_in, self.parts, self.loss_in = g_ref, own, away, core_in, parts, loss_in
        self.sems, self.groups, self.last = sems, groups, []
        self.core = lax.axis_index("mem_2")
        self.sibling = {"mem_2": 1 - self.core}
        self.at = {
            "x": lax.axis_index("mem_0"),
            "y": lax.axis_index("lat_0") * 2 + lax.axis_index("mem_1"),
            "z": lax.axis_index("lat_1"),
        }
        self.open = []
        self.leaving = [[], [], [], []]
        self.first = {}
        self.running = {}

    def peers(self):
        out = []
        for a in "yz":
            out += [device_at(a, (self.at[a] + d) % SIZE[a]) for d in range(1, SIZE[a])]
        return out

    def begin(self, src, dst, s, r, dev):
        c = remote(src, dst, s, r, dev)
        c.start()
        self.open.append(c)
        return c

    def loss_send(self, level, value):
        base, sbase = (0, 2, 6, 10)[level], (0, 1, 4, 7)[level]
        ls, lr = self.sems["loss"]
        if level == 0:
            devices = [self.sibling]
        else:
            a = "xyz"[level - 1]
            devices = [device_at(a, (self.at[a] + d) % SIZE[a]) for d in range(1, SIZE[a])]
        self.loss_in[base] = value
        self.loss_open = [
            self.begin(self.loss_in.at[base], self.loss_in.at[base + 1 + d], ls.at[sbase + d], lr.at[sbase + d], dev)
            for d, dev in enumerate(devices)
        ]

    def loss_take(self, level):
        base = (0, 2, 6, 10)[level]
        for c in self.loss_open:
            c.wait_recv()
        total = self.loss_in[base]
        for d in range(len(self.loss_open)):
            total = total + self.loss_in[base + 1 + d]
        return total

    def loss_next(self, level):
        self.loss_send(level + 1, self.loss_take(level))

    def pair(self, k):
        off, size = PLANS[k][:2]
        s, r = self.sems["pair"]
        units = pl.ds(off, size)
        self.first[k] = self.begin(self.away.at[units], self.core_in.at[units], s.at[k], r.at[k], self.sibling)

    def held(self, start, count):
        return self.own[pl.ds(start, count)] + self.core_in[pl.ds(start, count)]

    def arrive(self, key):
        for c in self.leaving.pop(0):
            c.wait_send()
        self.leaving.append(self.open)
        self.open = []
        for c in self.running[key]:
            c.wait_recv()
        self.running[key] = []

    def spread(self, key, send, recv, sems, row, axis, u):
        s, r = self.sems[sems]
        n = SIZE[axis]
        self.running[key] = []
        for d in range(1, n):
            p = (self.at[axis] + d) % n
            self.running[key].append(
                self.begin(send.at[pl.ds(p * u, u)], recv.at[d - 1], s.at[row, d - 1], r.at[row, d - 1], device_at(axis, p))
            )

    def share(self, key, source, into, sems, row, axis, start):
        s, r = self.sems[sems]
        n = SIZE[axis]
        self.running[key] = [
            self.begin(
                source, into.at[start], s.at[row, d - 1], r.at[row, d - 1], device_at(axis, (self.at[axis] + d) % n)
            )
            for d in range(1, n)
        ]

    def scatter_0(self, k):
        off, size, levels = PLANS[k]
        a, n, u = levels[0]
        send, recv = self.parts[k][:2]
        self.first[k].wait_recv()
        send[...] = self.held(off, size).astype(jnp.bfloat16)
        self.spread(k, send, recv, "scatter_0", k, a, u)

    def scatter_1(self, k):
        off, size, levels = PLANS[k]
        a, n, below = levels[0]
        b, m, u = levels[1]
        came, total, send, recv = self.parts[k][1:5]
        self.arrive(k)
        value = self.held(off + self.at[a] * below, below)
        for d in range(n - 1):
            value = value + came[d].astype(jnp.float32)
        total[0:below] = value
        if m * u > below:
            total[below:] = jnp.zeros((m * u - below, 16, 128), jnp.float32)
        send[...] = total[...].astype(jnp.bfloat16)
        self.spread(k, send, recv, "scatter_1", k, b, u)

    def scatter_2(self, group):
        starts, used, u = group_of(group)
        total, send, recv = self.groups[group][:3]
        if 8 * u > used:
            total[used:] = jnp.zeros((8 * u - used, 16, 128), jnp.float32)
        for k in GROUPS[group]:
            b, m, below = PLANS[k][2][1]
            held, came = self.parts[k][2], self.parts[k][4]
            self.arrive(k)
            value = held[pl.ds(self.at[b] * below, below)]
            for d in range(m - 1):
                value = value + came[d].astype(jnp.float32)
            total[starts[k] : starts[k] + below] = value
        send[...] = total[...].astype(jnp.bfloat16)
        self.spread(("z", group), send, recv, "scatter_2", group, "z", u)

    def gather_2(self, group):
        starts, used, u = group_of(group)
        total, send, recv, into = self.groups[group]
        self.arrive(("z", group))
        mine = pl.ds(self.at["z"] * u, u)
        value = total[mine]
        for d in range(7):
            value = value + recv[d].astype(jnp.float32)
        into[mine] = value.astype(jnp.bfloat16)
        self.share(("z", group), into.at[mine], into, "gather_2", group, "z", mine)

    def gather_1(self, k):
        group = 0 if k in GROUPS[0] else 1
        b, m, u = PLANS[k][2][1]
        start = group_of(group)[0][k]
        source, into = self.groups[group][3], self.parts[k][5]
        self.arrive(("z", group))
        mine = pl.ds(self.at[b] * u, u)
        into[mine] = source[start : start + u]
        self.share(k, source.at[pl.ds(start, u)], into, "gather_1", k, b, mine)

    def to_sibling(self, k, i, start, count):
        s, r = self.sems["back"]
        piece = self.g.at[self.core, pl.ds(start, count)]
        self.last.append(self.begin(piece, piece, s.at[k, i], r.at[k, i], self.sibling))

    def gather_0(self, k):
        off, size, levels = PLANS[k]
        a, n, u = levels[0]
        source = self.parts[k][5]
        self.arrive(k)
        mine = pl.ds(off + self.at[a] * u, u)
        self.g[self.core, mine] = source[0:u]
        self.share(k, source.at[pl.ds(0, u)], self.g.at[self.core], "gather_0", k, a, mine)
        self.to_sibling(k, 0, off + self.at[a] * u, u)

    def hand_over(self, k):
        off, size, levels = PLANS[k]
        a, n, u = levels[0]
        for d in range(1, n):
            self.running[k][d - 1].wait_recv()
            self.to_sibling(k, d, off + ((self.at[a] + n - d) % n) * u, u)

    def finish(self):
        for c in self.last:
            c.wait_recv()


def total_scratch():
    bf16, f32 = jnp.bfloat16, jnp.float32
    V = pltpu.VMEM
    parts, groups = [], []
    for off, size, levels in PLANS:
        (a, n, u), (b, m, v) = levels
        parts.append(
            [
                V((size, 16, 128), bf16),
                V((n - 1, u, 16, 128), bf16),
                V((m * v, 16, 128), f32),
                V((m * v, 16, 128), bf16),
                V((m - 1, v, 16, 128), bf16),
                V((m * v, 16, 128), bf16),
            ]
        )
    for group in range(len(GROUPS)):
        u = group_of(group)[2]
        groups.append(
            [V((8 * u, 16, 128), f32), V((8 * u, 16, 128), bf16), V((7, u, 16, 128), bf16), V((8 * u, 16, 128), bf16)]
        )
    dma = pltpu.SemaphoreType.DMA
    count = len(PLANS)
    pairs = dict(
        pair=(count,),
        scatter_0=(count, 3),
        scatter_1=(count, 3),
        scatter_2=(2, 7),
        gather_2=(2, 7),
        gather_1=(count, 3),
        gather_0=(count, 3),
        back=(count, 4),
        loss=(14,),
    )
    return dict(
        own=V((UNITS, 16, 128), f32),
        away=V((UNITS, 16, 128), f32),
        core_in=V((UNITS, 16, 128), f32),
        parts=parts,
        groups=groups,
        loss_in=V((18, 8, 128), f32),
        sems={name: (dma(shape), dma(shape)) for name, shape in pairs.items()},
    )


def step_kernel(
    state_hbm,
    conv_hbm,
    gain_hbm,
    up_hbm,
    down_hbm,
    head_hbm,
    target_hbm,
    field_hbm,
    g_ref,
    loss_ref,
    w,
    total_refs,
):
    win, ck, gn, su, nr, inv, sc, rd = (w[i] for i in ("win", "ck", "gn", "su", "nr", "inv", "sc", "rd"))
    pre, slope, hid, hp, fcs, fs, fr = (w[i] for i in ("pre", "slope", "hid", "hp", "fcs", "fs", "fr"))
    truth, co_s, co_r, co, dp, dsum, dsc = (w[i] for i in ("truth", "co_s", "co_r", "co", "dp", "dsum", "dsc"))
    small, thin_s, thin_r, up, down_t, drr = (w[i] for i in ("small", "thin_s", "thin_r", "up", "down_t", "drr"))
    halo_s, halo_r, fc_s, fc_r, ct_s, ct_r, wt = (w[i] for i in ("halo_s", "halo_r", "fc_s", "fc_r", "ct_s", "ct_r", "wt"))
    total = Total(g_ref, **total_refs)
    f32, bf16 = jnp.float32, jnp.bfloat16
    lat = lax.axis_index("lat_0") * 8 + lax.axis_index("lat_1")
    member = lax.axis_index("mem_0") * 4 + lax.axis_index("mem_1") * 2 + lax.axis_index("mem_2")

    def lat_device(d):
        p = (lat + d) % 16
        return {"lat_0": p // 8, "lat_1": p % 8}

    above, below = lat_device(1), lat_device(15)
    others = [member_device((member + d) % MEMBERS) for d in range(1, MEMBERS)]
    barrier = pltpu.get_barrier_semaphore()
    greeted = [above, below] + others + total.peers()
    for dev in greeted:
        pl.semaphore_signal(barrier, inc=1, device_id=dev, device_id_type=MESH_ID)
    state, conv_kernel, gain, head_t, target, field_weight = (
        w[i] for i in ("state", "conv_kernel", "gain", "head_t", "target", "field_weight")
    )
    loads = [
        pltpu.make_async_copy(src, dst, wt.at[i])
        for i, (src, dst) in enumerate(
            (
                (state_hbm, state),
                (conv_hbm, conv_kernel),
                (gain_hbm, gain),
                (head_hbm, head_t),
                (target_hbm, target),
                (field_hbm, field_weight),
                (up_hbm, up),
                (down_hbm, down_t),
            )
        )
    ]
    for c in loads:
        c.start()
    weights = loads[6:]

    win[CHUNKS - 1] = jnp.zeros((6, 176, 128), f32)
    loads[0].wait()
    for c in range(CHUNKS - 1):
        win[c, 2:4, 8:168, :] = state[:, :, c * 128 : (c + 1) * 128]
    win[CHUNKS - 1, 2:4, 8:168, 0:1] = state[:, :, 640:641]
    thin_s[...] = jnp.zeros((8, LON), f32)
    for i in range(ROWS):
        thin_s[i : i + 1, :] = jnp.transpose(win[CHUNKS - 1, 2 + i, 8:168, :])[0:1, :]
    pl.semaphore_wait(barrier, len(greeted))

    def halo(c):
        mine = win.at[c, 2:4, 8:168]
        return (
            remote(mine, win.at[c, 0:2, 8:168], halo_s.at[0, c], halo_r.at[0, c], above),
            remote(mine, win.at[c, 4:6, 8:168], halo_s.at[1, c], halo_r.at[1, c], below),
        )

    thin = (
        remote(thin_s, thin_r.at[0], halo_s.at[0, CHUNKS - 1], halo_r.at[0, CHUNKS - 1], above),
        remote(thin_s, thin_r.at[1], halo_s.at[1, CHUNKS - 1], halo_r.at[1, CHUNKS - 1], below),
    )
    for copy in thin:
        copy.start()

    @pl.loop(0, CHUNKS - 1)
    def _(c):
        for copy in halo(c):
            copy.start()

    for c in loads[1:6]:
        c.wait()
    ck[CHUNKS - 1] = jnp.zeros((25, 128), f32)
    put(ck, conv_kernel[...])
    gn[CHUNKS - 1] = jnp.zeros((1, 128), f32)
    put(gn, gain[...].reshape(1, C))
    hp[:, 640:768] = jnp.zeros((FIELDS, 128), bf16)
    hp[:, 0:641] = head_t[...]
    rd[:, 640:768] = jnp.zeros((CELLS, 128), bf16)
    su[CHUNKS - 1] = jnp.zeros((CELLS, 128), f32)
    dsc[CHUNKS - 1] = jnp.zeros((CELLS, 128), f32)
    small[...] = jnp.zeros((2, CHUNKS, 64, 128), f32)
    for i in range(ROWS):
        columns = jnp.transpose(target[:, i, :])
        for b in range(MEMBERS // ROWS):
            truth[i * (MEMBERS // ROWS) + b] = columns[b * BLOCK : (b + 1) * BLOCK, :]

    def wrap(c, rows):
        win[c, rows, 6:8, :] = win[c, rows, 166:168, :]
        win[c, rows, 168:170, :] = win[c, rows, 8:10, :]

    def taps(c, i, rows, acc):
        for a in rows:
            for b in range(5):
                acc = acc + ck[c, 5 * a + b : 5 * a + b + 1, :] * win[c, i + a, 6 + b : 166 + b, :]
        return acc

    own = ((2, 3), (1, 2))
    met = ((0, 1, 4), (0, 3, 4))

    @pl.loop(0, CHUNKS)
    def _(c):
        wrap(c, slice(2, 4))
        for i in range(ROWS):
            su[c, i * LON : (i + 1) * LON] = taps(c, i, own[i], win[c, 2 + i, 8:168, :])

    def meet(c):
        @pl.when(lat == 0)
        def _():
            win[c, 0:2] = jnp.zeros((2, 176, 128), f32)

        @pl.when(lat == 15)
        def _():
            win[c, 4:6] = jnp.zeros((2, 176, 128), f32)

        wrap(c, slice(0, 2))
        wrap(c, slice(4, 6))
        for i in range(ROWS):
            su[c, i * LON : (i + 1) * LON] = taps(c, i, met[i], su[c, i * LON : (i + 1) * LON])

    for side, copy in enumerate(thin):
        copy.wait_recv()
        column = jnp.transpose(thin_r[side])
        for i in range(ROWS):
            win[CHUNKS - 1, 4 * side + i, 8:168, 0:1] = column[:, i : i + 1]
    meet(CHUNKS - 1)

    @pl.loop(0, CHUNKS - 1)
    def _(c):
        for copy in halo(c):
            copy.wait_recv()
        meet(c)

    level = su[0]
    for c in range(1, CHUNKS):
        level = level + su[c]
    mean = jnp.sum(level, axis=1, keepdims=True) * (1.0 / C)
    first_lane = (lax.broadcasted_iota(jnp.int32, (CELLS, 128), 1) < 1).astype(f32)
    square = jnp.zeros((CELLS, 128), f32)
    for c in range(CHUNKS):
        center = su[c] - mean
        if c == CHUNKS - 1:
            center = center * first_lane
        nr[c] = center
        square = square + center * center
    inverse = lax.rsqrt(jnp.sum(square, axis=1, keepdims=True) * (1.0 / C) + EPSILON)
    inv[...] = inverse
    for c in range(CHUNKS):
        normed = nr[c] * inverse
        nr[c] = normed
        sc[:, c * 128 : (c + 1) * 128] = (normed * gn[c]).astype(bf16)

    for c in weights:
        c.wait()
    pre[...] = jnp.dot(sc[:, 0:C], up[...], preferred_element_type=f32)

    @pl.loop(0, CELLS // 16)
    def _(r):
        rows = pl.ds(pl.multiple_of(r * 16, 16), 16)
        x = pre[rows, :]
        cumul = 0.5 * (1.0 + lax.erf(x * (1.0 / math.sqrt(2.0))))
        density = jnp.exp(-0.5 * x * x) * (1.0 / math.sqrt(2.0 * math.pi))
        hid[rows, :] = (x * cumul).astype(bf16)
        slope[rows, :] = cumul + x * density

    mlp = contract(hid[...], down_t[...], (1, 1))
    for c in range(CHUNKS - 1):
        at = slice(c * 128, (c + 1) * 128)
        rd[:, at] = (su[c] + mlp[:, at]).astype(bf16)
    rd[:, 640:641] = (su[CHUNKS - 1, :, 0:1] + mlp[:, 640:641]).astype(bf16)
    fcs[...] = contract(rd[...], hp[...], (1, 1))

    for p in range(MEMBERS):
        fs[p] = fcs[p * BLOCK : (p + 1) * BLOCK, :]
    sent = []
    for d in range(1, MEMBERS):
        p = (member + d) % MEMBERS
        c = remote(fs.at[p], fr.at[member], fc_s.at[d - 1], fc_r.at[d - 1], others[d - 1])
        c.start()
        sent.append(c)
    fr[member] = fs[member]
    for c in sent:
        c.wait_recv()

    row = 2 * lat + member // (MEMBERS // ROWS)
    area = jnp.float32(AREA[0])
    for i in range(1, NLAT):
        area = jnp.where(row == i, jnp.float32(AREA[i]), area)
    weight = field_weight[...] * area
    against = truth[member]
    members = fr[...]
    gap = members - against[None]
    square = gap * gap + DELTA * DELTA
    root = lax.rsqrt(square)
    miss = jnp.sum(square * root - DELTA, axis=0)
    slope_miss = gap * root
    apart = jnp.zeros((BLOCK, FIELDS), f32)
    pull = jnp.zeros((MEMBERS, BLOCK, FIELDS), f32)
    for n in range(MEMBERS):
        gap = members - fr[n][None]
        square = gap * gap + DELTA * DELTA
        root = lax.rsqrt(square)
        apart = apart + jnp.sum(square * root - DELTA, axis=0)
        pull = pull + gap * root
    cells = NLAT * LON * FIELDS
    spread = miss * (1.0 / MEMBERS) - apart * (1.0 / (2.0 * MEMBERS * (MEMBERS - 1)))
    cotangent = weight[None] * (slope_miss - pull * (1.0 / (MEMBERS - 1))) * (1.0 / (MEMBERS * math.sqrt(cells)))
    co_s[...] = cotangent.astype(bf16)
    back = []
    for d in range(1, MEMBERS):
        p = (member + d) % MEMBERS
        c = remote(co_s.at[p], co_r.at[member], ct_s.at[d - 1], ct_r.at[d - 1], others[d - 1])
        c.start()
        back.append(c)
    co_r[member] = co_s[member]
    total.loss_send(0, jnp.full((8, 128), jnp.sum(weight * spread) * (1.0 / cells), f32))
    for c in back:
        c.wait_recv()
    for p in range(MEMBERS):
        fcs[p * BLOCK : (p + 1) * BLOCK, :] = co_r[p].astype(f32)
    co[...] = fcs[...].astype(bf16)

    d_output = jnp.dot(co[...], hp[...], preferred_element_type=f32)
    for c in range(CHUNKS):
        dsum[c] = d_output[:, c * 128 : (c + 1) * 128]
    drr[...] = d_output.astype(bf16)

    def half_grad(base, left, right, which, out, then=()):
        for i, (s, wide) in enumerate(((0, 256), (256, 256), (512, 128))):
            columns = pl.ds(pl.multiple_of(which * 640 + s, 128), wide)
            part = contract(left[:, 0:640], right[:, columns], (0, 0))
            for h in range(wide // 128):
                j = base + (s // 128 + h) * TALL
                out[j : j + TALL] = part[:, h * 128 : (h + 1) * 128].reshape(TALL, 16, 128)
            if i in then:
                total.pair(then[i])

    def edge_grad(left, right, r):
        line = contract(left[:, 640:641], right[...], (0, 0))
        for j in range(2 * WIDE):
            small[1, j % 5, r + 2 + j // 5 : r + 3 + j // 5, :] = line[:, j * 128 : (j + 1) * 128]
        edge = contract(right[:, 1280:1282], left[...], (0, 0))
        for c in range(CHUNKS):
            small[1, c, r : r + 2, :] = edge[:, c * 128 : (c + 1) * 128]

    core = total.core
    half_grad(0, drr, hid, 1 - core, total.away, {1: 0, 2: 1})
    half_grad(0, drr, hid, core, total.own)
    pre[...] = jnp.dot(drr[:, 0:C], down_t[...], preferred_element_type=f32)

    @pl.loop(0, CELLS // 16)
    def _(r):
        rows = pl.ds(pl.multiple_of(r * 16, 16), 16)
        dp[rows, :] = (pre[rows, :] * slope[rows, :]).astype(bf16)

    total.scatter_0(0)
    total.scatter_0(1)
    half_grad(HALF, sc, dp, 1 - core, total.away, {1: 2, 2: 3})
    half_grad(HALF, sc, dp, core, total.own)
    total.loss_next(0)
    head_grad = contract(co[...], rd[...], (0, 0))
    for c in range(CHUNKS):
        small[0, c, 0:64, :] = head_grad[0:64, c * 128 : (c + 1) * 128]
        small[1, c, 0:8, :] = head_grad[64:72, c * 128 : (c + 1) * 128]
    total.scatter_0(2)
    total.scatter_0(3)
    edge_grad(drr, hid, 39)
    edge_grad(sc, dp, 34)
    put(dsc, contract(dp[...], up[...], (1, 1)))
    mean_a = jnp.zeros((CELLS, 128), f32)
    mean_b = jnp.zeros((CELLS, 128), f32)
    for c in range(CHUNKS):
        both = dsc[c] * nr[c]
        small[1, c, 33:34, :] = jnp.sum(both, axis=0, keepdims=True)
        mean_a = mean_a + dsc[c] * gn[c]
        mean_b = mean_b + both * gn[c]
    mean_a = jnp.sum(mean_a, axis=1, keepdims=True) * (1.0 / C)
    mean_b = jnp.sum(mean_b, axis=1, keepdims=True) * (1.0 / C)
    for c in range(CHUNKS):
        dsum[c] = dsum[c] + inv[...] * (dsc[c] * gn[c] - mean_a - nr[c] * mean_b)

    total.scatter_1(0)
    total.scatter_1(1)
    total.loss_next(1)

    @pl.loop(0, CHUNKS)
    def _(c):
        for a in range(5):
            acc = [jnp.zeros((8, 128), f32) for _ in range(5)]
            for i in range(ROWS):
                for t in range(LON // 8):
                    d = dsum[c, i * LON + 8 * t : i * LON + 8 * t + 8, :]
                    for b in range(5):
                        acc[b] = acc[b] + d * win[c, i + a, 6 + b + 8 * t : 14 + b + 8 * t, :]
            for b in range(5):
                tap = 8 + 5 * a + b
                small[1, c, tap : tap + 1, :] = jnp.sum(acc[b], axis=0, keepdims=True)

    for c in range(CHUNKS):
        units = slice(SMALL + c * SMALL_TALL, SMALL + (c + 1) * SMALL_TALL)
        total.away[units] = small[1 - core, c].reshape(SMALL_TALL, 16, 128)
        total.own[units] = small[core, c].reshape(SMALL_TALL, 16, 128)
    total.pair(4)

    @pl.loop(0, CHUNKS - 1)
    def _(c):
        for copy in halo(c):
            copy.wait_send()

    for c in list(thin) + sent + back:
        c.wait_send()
    total.scatter_2(0)
    total.scatter_0(4)
    total.scatter_1(2)
    total.scatter_1(3)
    total.loss_next(2)
    total.scatter_1(4)
    total.gather_2(0)
    total.scatter_2(1)
    total.gather_1(0)
    total.gather_1(1)
    total.gather_2(1)
    total.gather_0(0)
    total.gather_0(1)
    total.gather_1(2)
    total.gather_1(3)
    total.gather_1(4)
    for part in (2, 3, 4):
        total.gather_0(part)
    for part in range(5):
        total.hand_over(part)
    total.finish()
    loss_ref[...] = total.loss_take(3)

    for c in sum(total.leaving, []) + total.open:
        c.wait_send()


def gradients(state, conv_kernel, gain, up, down_t, head_t, target, field_weight):
    f32, bf16 = jnp.float32, jnp.bfloat16
    vmem = pl.BlockSpec(memory_space=pltpu.VMEM)
    anywhere = pl.BlockSpec(memory_space=pltpu.HBM)
    V = pltpu.VMEM
    dma = pltpu.SemaphoreType.DMA
    work = dict(
        win=V((CHUNKS, 6, 176, 128), f32),
        ck=V((CHUNKS, 25, 128), f32),
        gn=V((CHUNKS, 1, 128), f32),
        su=V((CHUNKS, CELLS, 128), f32),
        nr=V((CHUNKS, CELLS, 128), f32),
        inv=V((CELLS, 1), f32),
        sc=V((CELLS, 768), bf16),
        rd=V((CELLS, 768), bf16),
        pre=V((CELLS, HID), f32),
        slope=V((CELLS, HID), f32),
        hid=V((CELLS, HID), bf16),
        hp=V((FIELDS, 768), bf16),
        fcs=V((CELLS, FIELDS), f32),
        fs=V((MEMBERS, BLOCK, FIELDS), f32),
        fr=V((MEMBERS, BLOCK, FIELDS), f32),
        truth=V((MEMBERS, BLOCK, FIELDS), f32),
        co_s=V((MEMBERS, BLOCK, FIELDS), bf16),
        co_r=V((MEMBERS, BLOCK, FIELDS), bf16),
        co=V((CELLS, FIELDS), bf16),
        dp=V((CELLS, HID), bf16),
        dsum=V((CHUNKS, CELLS, 128), f32),
        dsc=V((CHUNKS, CELLS, 128), f32),
        small=V((2, CHUNKS, 64, 128), f32),
        thin_s=V((8, LON), f32),
        thin_r=V((2, 8, LON), f32),
        up=V((C, HID), bf16),
        down_t=V((C, HID), bf16),
        drr=V((CELLS, 768), bf16),
        halo_s=dma((2, CHUNKS)),
        halo_r=dma((2, CHUNKS)),
        fc_s=dma((MEMBERS - 1,)),
        fc_r=dma((MEMBERS - 1,)),
        ct_s=dma((MEMBERS - 1,)),
        ct_r=dma((MEMBERS - 1,)),
        wt=dma((8,)),
        state=V((ROWS, LON, C), f32),
        conv_kernel=V((25, C), f32),
        gain=V((C,), f32),
        head_t=V((FIELDS, C), bf16),
        target=V((FIELDS, ROWS, LON), f32),
        field_weight=V((1, FIELDS), f32),
    )
    refs, tree = jax.tree.flatten((work, total_scratch()))

    def kernel(*args):
        step_kernel(*args[:10], *jax.tree.unflatten(tree, args[10:]))

    return pl.pallas_call(
        kernel,
        out_shape=(
            jax.ShapeDtypeStruct((2, UNITS, 16, 128), bf16),
            jax.ShapeDtypeStruct((8, 128), f32),
        ),
        in_specs=[anywhere] * 8,
        out_specs=(vmem, vmem),
        scratch_shapes=refs,
        compiler_params=pltpu.CompilerParams(
            collective_id=0, has_side_effects=True, vmem_limit_bytes=48 * 1024 * 1024
        ),
    )(
        *(
            pltpu.with_memory_space_constraint(a, pltpu.HBM)
            for a in (state, conv_kernel, gain, up, down_t, head_t, target, field_weight)
        )
    )


def unpack_kernel(g_ref, loss, *refs):
    hbm, (up_ref, down_ref, head_ref, kern_ref, gain_ref, loss_ref, small, sem) = refs[:6], refs[6:]
    copies = []

    def send(src, dst):
        copies.append(pltpu.make_async_copy(src, dst, sem.at[len(copies)]))
        copies[-1].start()

    loss_ref[...] = loss[0:1, 0:1]
    send(loss_ref, hbm[5])
    for core in range(2):
        for c in range(CHUNKS):
            start = SMALL + c * SMALL_TALL
            piece = g_ref[core, start : start + SMALL_TALL].astype(jnp.float32)
            small[core, :, c * 128 : (c + 1) * 128] = piece.reshape(64, 128)
    head_ref[0:64, :] = small[0, :, 0:C]
    head_ref[64:72, :] = small[1, 0:8, 0:C]
    send(head_ref, hbm[2])
    kern_ref[...] = small[1, 8:33, 0:C]
    send(kern_ref, hbm[3])
    gain_ref[...] = small[1, 33:34, 0:C].reshape(C)
    send(gain_ref, hbm[4])
    edge = jnp.transpose(small[1, 32:56, :])
    for m, r, out, target in ((0, 39, down_ref, hbm[1]), (1, 34, up_ref, hbm[0])):
        out[640:641, 0:640] = small[1, r + 2 : r + 3, 0:640]
        out[640:641, 640:1280] = small[1, r + 3 : r + 4, 0:640]
        for b in range(5):
            for core in range(2):
                for j in range(WIDE):
                    start = m * HALF + j * TALL + b * 8
                    piece = g_ref[core, start : start + 8].astype(jnp.float32)
                    lane = (core * WIDE + j) * 128
                    out[b * 128 : (b + 1) * 128, lane : lane + 128] = piece.reshape(128, 128)
            end = (b + 1) * 128 + (b == 4)
            out[b * 128 : end, 1280:1282] = edge[b * 128 : end, r - 32 : r - 30]
            rows = pl.ds(b * 128, end - b * 128)
            send(out.at[rows], target.at[rows])
    for c in copies:
        c.wait()


def unpacked(g, loss):
    vmem = pl.BlockSpec(memory_space=pltpu.VMEM)
    hbm = pl.BlockSpec(memory_space=pltpu.HBM)
    shapes = ((C, HID), (C, HID), (FIELDS, C), (25, C), (C,), (1, 1))
    return pl.pallas_call(
        unpack_kernel,
        out_shape=tuple(jax.ShapeDtypeStruct(s, jnp.float32) for s in shapes),
        in_specs=[vmem, vmem],
        out_specs=(hbm,) * 6,
        scratch_shapes=[pltpu.VMEM(s, jnp.float32) for s in shapes]
        + [pltpu.VMEM((2, 64, 768), jnp.float32), pltpu.SemaphoreType.DMA((14,))],
        compiler_params=pltpu.CompilerParams(vmem_limit_bytes=24 * 1024 * 1024),
    )(g, loss)


def local(
    state, conv_kernel, norm_gain, up_weight, down_weight, field_head_weight, target, field_weight
):
    total, loss = gradients(
        jnp.transpose(state[0], (1, 2, 0)),
        conv_kernel,
        norm_gain,
        up_weight,
        down_weight.T,
        field_head_weight.T,
        target,
        field_weight[None],
    )
    up, down_t, head_t, kern, gain_row, loss = unpacked(total, loss)
    return (loss.reshape(()), kern, gain_row, up, down_t.T, head_t.T)


def solution(mesh):
    finer = Mesh(mesh.devices.reshape(4, 2, 2, 2, 8), AXES)
    mem, lat = AXES[:3], AXES[3:]
    in_specs = (P(mem, None, lat, None), P(), P(), P(), P(), P(), P(None, lat, None), P())
    out_specs = (P(), P(), P(), P(), P(), P())
    return jax.shard_map(local, mesh=finer, in_specs=in_specs, out_specs=out_specs, check_vma=False)
```

```python
import math

import jax
import jax.numpy as jnp
import numpy as np
from jax import lax
from jax.experimental import pallas as pl
from jax.experimental.pallas import tpu as pltpu
from jax.sharding import Mesh
from jax.sharding import PartitionSpec as P

AXES = ("mem_0", "mem_1", "mem_2", "lat_0", "lat_1")
MESH_ID = pl.DeviceIdType.MESH
ROWS = 2
LON = 160
CELLS = ROWS * LON
C = 641
HID = 1282
FIELDS = 72
MEMBERS = 16
NLAT = 32
BLOCK = CELLS // MEMBERS
CHUNKS = 6
DELTA = 0.1
EPSILON = 1e-05
AREA = np.cos(
    np.float32(0.5 * math.pi)
    * ((np.arange(NLAT, dtype=np.float32) + np.float32(0.5)) / np.float32(NLAT) - np.float32(1.0))
)

TALL, WIDE = 40, 5
HALF = TALL * WIDE
SMALL = 2 * HALF
SMALL_TALL = 4
UNITS = SMALL + SMALL_TALL * CHUNKS
SIZE = {"x": 4, "y": 4, "z": 8}
PARTS = ((0, 100, "xy"), (100, 100, "yx"), (200, 100, "xy"), (300, 100, "yx"), (400, 24, "xy"))
GROUPS = ((0, 1), (2, 3, 4))


def levels_of(size, order):
    levels = []
    for a in order:
        size = -(-size // SIZE[a])
        levels.append((a, SIZE[a], size))
    return levels


PLANS = tuple((off, size, levels_of(size, order)) for off, size, order in PARTS)


def group_of(group):
    starts, at = {}, 0
    for k in GROUPS[group]:
        starts[k] = at
        at += PLANS[k][2][1][2]
    return starts, at, -(-at // SIZE["z"])


def contract(left, right, dims):
    return lax.dot_general(left, right, ((dims[:1], dims[1:]), ((), ())), preferred_element_type=jnp.float32)


def put(ref, value):
    for c in range(CHUNKS - 1):
        ref[c] = value[:, c * 128 : (c + 1) * 128]
    ref[CHUNKS - 1, :, 0:1] = value[:, 640:641]


def member_device(m):
    return {"mem_0": m // 4, "mem_1": (m // 2) % 2, "mem_2": m % 2}


def device_at(axis, p):
    if axis == "x":
        return {"mem_0": p}
    if axis == "y":
        return {"lat_0": p // 2, "mem_1": p % 2}
    return {"lat_1": p}


def remote(src, dst, s, r, dev):
    return pltpu.make_async_remote_copy(
        src_ref=src, dst_ref=dst, send_sem=s, recv_sem=r, device_id=dev, device_id_type=MESH_ID
    )


class Total:
    def __init__(self, g_ref, own, away, core_in, parts, groups, loss_in, sems):
        self.g, self.own, self.away, self.core_in, self.parts, self.loss_in = g_ref, own, away, core_in, parts, loss_in
        self.sems, self.groups, self.last = sems, groups, []
        self.core = lax.axis_index("mem_2")
        self.sibling = {"mem_2": 1 - self.core}
        self.at = {
            "x": lax.axis_index("mem_0"),
            "y": lax.axis_index("lat_0") * 2 + lax.axis_index("mem_1"),
            "z": lax.axis_index("lat_1"),
        }
        self.open = []
        self.leaving = [[], [], [], []]
        self.first = {}
        self.running = {}

    def peers(self):
        out = []
        for a in "yz":
            out += [device_at(a, (self.at[a] + d) % SIZE[a]) for d in range(1, SIZE[a])]
        return out

    def begin(self, src, dst, s, r, dev):
        c = remote(src, dst, s, r, dev)
        c.start()
        self.open.append(c)
        return c

    def loss_send(self, level, value):
        base, sbase = (0, 2, 6, 10)[level], (0, 1, 4, 7)[level]
        ls, lr = self.sems["loss"]
        if level == 0:
            devices = [self.sibling]
        else:
            a = "xyz"[level - 1]
            devices = [device_at(a, (self.at[a] + d) % SIZE[a]) for d in range(1, SIZE[a])]
        self.loss_in[base] = value
        self.loss_open = [
            self.begin(self.loss_in.at[base], self.loss_in.at[base + 1 + d], ls.at[sbase + d], lr.at[sbase + d], dev)
            for d, dev in enumerate(devices)
        ]

    def loss_take(self, level):
        base = (0, 2, 6, 10)[level]
        for c in self.loss_open:
            c.wait_recv()
        total = self.loss_in[base]
        for d in range(len(self.loss_open)):
            total = total + self.loss_in[base + 1 + d]
        return total

    def loss_next(self, level):
        self.loss_send(level + 1, self.loss_take(level))

    def pair(self, k):
        off, size = PLANS[k][:2]
        s, r = self.sems["pair"]
        units = pl.ds(off, size)
        self.first[k] = self.begin(self.away.at[units], self.core_in.at[units], s.at[k], r.at[k], self.sibling)

    def held(self, start, count):
        return self.own[pl.ds(start, count)] + self.core_in[pl.ds(start, count)]

    def arrive(self, key):
        for c in self.leaving.pop(0):
            c.wait_send()
        self.leaving.append(self.open)
        self.open = []
        for c in self.running[key]:
            c.wait_recv()
        self.running[key] = []

    def spread(self, key, send, recv, sems, row, axis, u):
        s, r = self.sems[sems]
        n = SIZE[axis]
        self.running[key] = []
        for d in range(1, n):
            p = (self.at[axis] + d) % n
            self.running[key].append(
                self.begin(send.at[pl.ds(p * u, u)], recv.at[d - 1], s.at[row, d - 1], r.at[row, d - 1], device_at(axis, p))
            )

    def share(self, key, source, into, sems, row, axis, start):
        s, r = self.sems[sems]
        n = SIZE[axis]
        self.running[key] = [
            self.begin(
                source, into.at[start], s.at[row, d - 1], r.at[row, d - 1], device_at(axis, (self.at[axis] + d) % n)
            )
            for d in range(1, n)
        ]

    def scatter_0(self, k):
        off, size, levels = PLANS[k]
        a, n, u = levels[0]
        send, recv = self.parts[k][:2]
        self.first[k].wait_recv()
        send[...] = self.held(off, size).astype(jnp.bfloat16)
        self.spread(k, send, recv, "scatter_0", k, a, u)

    def scatter_1(self, k):
        off, size, levels = PLANS[k]
        a, n, below = levels[0]
        b, m, u = levels[1]
        came, total, send, recv = self.parts[k][1:5]
        self.arrive(k)
        value = self.held(off + self.at[a] * below, below)
        for d in range(n - 1):
            value = value + came[d].astype(jnp.float32)
        total[0:below] = value
        if m * u > below:
            total[below:] = jnp.zeros((m * u - below, 16, 128), jnp.float32)
        send[...] = total[...].astype(jnp.bfloat16)
        self.spread(k, send, recv, "scatter_1", k, b, u)

    def scatter_2(self, group):
        starts, used, u = group_of(group)
        total, send, recv = self.groups[group][:3]
        if 8 * u > used:
            total[used:] = jnp.zeros((8 * u - used, 16, 128), jnp.float32)
        for k in GROUPS[group]:
            b, m, below = PLANS[k][2][1]
            held, came = self.parts[k][2], self.parts[k][4]
            self.arrive(k)
            value = held[pl.ds(self.at[b] * below, below)]
            for d in range(m - 1):
                value = value + came[d].astype(jnp.float32)
            total[starts[k] : starts[k] + below] = value
        send[...] = total[...].astype(jnp.bfloat16)
        self.spread(("z", group), send, recv, "scatter_2", group, "z", u)

    def gather_2(self, group):
        starts, used, u = group_of(group)
        total, send, recv, into = self.groups[group]
        self.arrive(("z", group))
        mine = pl.ds(self.at["z"] * u, u)
        value = total[mine]
        for d in range(7):
            value = value + recv[d].astype(jnp.float32)
        into[mine] = value.astype(jnp.bfloat16)
        self.share(("z", group), into.at[mine], into, "gather_2", group, "z", mine)

    def gather_1(self, k):
        group = 0 if k in GROUPS[0] else 1
        b, m, u = PLANS[k][2][1]
        start = group_of(group)[0][k]
        source, into = self.groups[group][3], self.parts[k][5]
        self.arrive(("z", group))
        mine = pl.ds(self.at[b] * u, u)
        into[mine] = source[start : start + u]
        self.share(k, source.at[pl.ds(start, u)], into, "gather_1", k, b, mine)

    def to_sibling(self, k, i, start, count):
        s, r = self.sems["back"]
        piece = self.g.at[self.core, pl.ds(start, count)]
        self.last.append(self.begin(piece, piece, s.at[k, i], r.at[k, i], self.sibling))

    def gather_0(self, k):
        off, size, levels = PLANS[k]
        a, n, u = levels[0]
        source = self.parts[k][5]
        self.arrive(k)
        mine = pl.ds(off + self.at[a] * u, u)
        self.g[self.core, mine] = source[0:u]
        self.share(k, source.at[pl.ds(0, u)], self.g.at[self.core], "gather_0", k, a, mine)
        self.to_sibling(k, 0, off + self.at[a] * u, u)

    def hand_over(self, k):
        off, size, levels = PLANS[k]
        a, n, u = levels[0]
        for d in range(1, n):
            self.running[k][d - 1].wait_recv()
            self.to_sibling(k, d, off + ((self.at[a] + n - d) % n) * u, u)

    def finish(self):
        for c in self.last:
            c.wait_recv()


def total_scratch():
    bf16, f32 = jnp.bfloat16, jnp.float32
    V = pltpu.VMEM
    parts, groups = [], []
    for off, size, levels in PLANS:
        (a, n, u), (b, m, v) = levels
        parts.append(
            [
                V((size, 16, 128), bf16),
                V((n - 1, u, 16, 128), bf16),
                V((m * v, 16, 128), f32),
                V((m * v, 16, 128), bf16),
                V((m - 1, v, 16, 128), bf16),
                V((m * v, 16, 128), bf16),
            ]
        )
    for group in range(len(GROUPS)):
        u = group_of(group)[2]
        groups.append(
            [V((8 * u, 16, 128), f32), V((8 * u, 16, 128), bf16), V((7, u, 16, 128), bf16), V((8 * u, 16, 128), bf16)]
        )
    dma = pltpu.SemaphoreType.DMA
    count = len(PLANS)
    pairs = dict(
        pair=(count,),
        scatter_0=(count, 3),
        scatter_1=(count, 3),
        scatter_2=(2, 7),
        gather_2=(2, 7),
        gather_1=(count, 3),
        gather_0=(count, 3),
        back=(count, 4),
        loss=(14,),
    )
    return dict(
        own=V((UNITS, 16, 128), f32),
        away=V((UNITS, 16, 128), f32),
        core_in=V((UNITS, 16, 128), f32),
        parts=parts,
        groups=groups,
        loss_in=V((18, 8, 128), f32),
        sems={name: (dma(shape), dma(shape)) for name, shape in pairs.items()},
    )


def step_kernel(
    state_hbm,
    conv_hbm,
    gain_hbm,
    up_hbm,
    down_hbm,
    head_hbm,
    target_hbm,
    field_hbm,
    g_ref,
    loss_ref,
    w,
    total_refs,
):
    win, ck, gn, su, nr, inv, sc, rd = (w[i] for i in ("win", "ck", "gn", "su", "nr", "inv", "sc", "rd"))
    pre, slope, hid, hp, fcs, fs, fr = (w[i] for i in ("pre", "slope", "hid", "hp", "fcs", "fs", "fr"))
    truth, co_s, co_r, co, dp, dsum, dsc = (w[i] for i in ("truth", "co_s", "co_r", "co", "dp", "dsum", "dsc"))
    small, thin_s, thin_r, up, down_t, drr = (w[i] for i in ("small", "thin_s", "thin_r", "up", "down_t", "drr"))
    halo_s, halo_r, fc_s, fc_r, ct_s, ct_r, wt = (w[i] for i in ("halo_s", "halo_r", "fc_s", "fc_r", "ct_s", "ct_r", "wt"))
    total = Total(g_ref, **total_refs)
    f32, bf16 = jnp.float32, jnp.bfloat16
    lat = lax.axis_index("lat_0") * 8 + lax.axis_index("lat_1")
    member = lax.axis_index("mem_0") * 4 + lax.axis_index("mem_1") * 2 + lax.axis_index("mem_2")

    def lat_device(d):
        p = (lat + d) % 16
        return {"lat_0": p // 8, "lat_1": p % 8}

    above, below = lat_device(1), lat_device(15)
    others = [member_device((member + d) % MEMBERS) for d in range(1, MEMBERS)]
    barrier = pltpu.get_barrier_semaphore()
    greeted = [above, below] + others + total.peers()
    for dev in greeted:
        pl.semaphore_signal(barrier, inc=1, device_id=dev, device_id_type=MESH_ID)
    state, conv_kernel, gain, head_t, target, field_weight = (
        w[i] for i in ("state", "conv_kernel", "gain", "head_t", "target", "field_weight")
    )
    loads = [
        pltpu.make_async_copy(src, dst, wt.at[i])
        for i, (src, dst) in enumerate(
            (
                (state_hbm, state),
                (conv_hbm, conv_kernel),
                (gain_hbm, gain),
                (head_hbm, head_t),
                (target_hbm, target),
                (field_hbm, field_weight),
                (up_hbm, up),
                (down_hbm, down_t),
            )
        )
    ]
    for c in loads:
        c.start()
    weights = loads[6:]

    win[CHUNKS - 1] = jnp.zeros((6, 176, 128), f32)
    loads[0].wait()
    for c in range(CHUNKS - 1):
        win[c, 2:4, 8:168, :] = state[:, :, c * 128 : (c + 1) * 128]
    win[CHUNKS - 1, 2:4, 8:168, 0:1] = state[:, :, 640:641]
    thin_s[...] = jnp.zeros((8, LON), f32)
    for i in range(ROWS):
        thin_s[i : i + 1, :] = jnp.transpose(win[CHUNKS - 1, 2 + i, 8:168, :])[0:1, :]
    pl.semaphore_wait(barrier, len(greeted))

    def halo(c):
        mine = win.at[c, 2:4, 8:168]
        return (
            remote(mine, win.at[c, 0:2, 8:168], halo_s.at[0, c], halo_r.at[0, c], above),
            remote(mine, win.at[c, 4:6, 8:168], halo_s.at[1, c], halo_r.at[1, c], below),
        )

    thin = (
        remote(thin_s, thin_r.at[0], halo_s.at[0, CHUNKS - 1], halo_r.at[0, CHUNKS - 1], above),
        remote(thin_s, thin_r.at[1], halo_s.at[1, CHUNKS - 1], halo_r.at[1, CHUNKS - 1], below),
    )
    for copy in thin:
        copy.start()

    @pl.loop(0, CHUNKS - 1)
    def _(c):
        for copy in halo(c):
            copy.start()

    for c in loads[1:6]:
        c.wait()
    ck[CHUNKS - 1] = jnp.zeros((25, 128), f32)
    put(ck, conv_kernel[...])
    gn[CHUNKS - 1] = jnp.zeros((1, 128), f32)
    put(gn, gain[...].reshape(1, C))
    hp[:, 640:768] = jnp.zeros((FIELDS, 128), bf16)
    hp[:, 0:641] = head_t[...]
    rd[:, 640:768] = jnp.zeros((CELLS, 128), bf16)
    su[CHUNKS - 1] = jnp.zeros((CELLS, 128), f32)
    dsc[CHUNKS - 1] = jnp.zeros((CELLS, 128), f32)
    small[...] = jnp.zeros((2, CHUNKS, 64, 128), f32)
    for i in range(ROWS):
        columns = jnp.transpose(target[:, i, :])
        for b in range(MEMBERS // ROWS):
            truth[i * (MEMBERS // ROWS) + b] = columns[b * BLOCK : (b + 1) * BLOCK, :]

    def wrap(c, rows):
        win[c, rows, 6:8, :] = win[c, rows, 166:168, :]
        win[c, rows, 168:170, :] = win[c, rows, 8:10, :]

    def taps(c, i, rows, acc):
        for a in rows:
            for b in range(5):
                acc = acc + ck[c, 5 * a + b : 5 * a + b + 1, :] * win[c, i + a, 6 + b : 166 + b, :]
        return acc

    own = ((2, 3), (1, 2))
    met = ((0, 1, 4), (0, 3, 4))

    @pl.loop(0, CHUNKS)
    def _(c):
        wrap(c, slice(2, 4))
        for i in range(ROWS):
            su[c, i * LON : (i + 1) * LON] = taps(c, i, own[i], win[c, 2 + i, 8:168, :])

    def meet(c):
        @pl.when(lat == 0)
        def _():
            win[c, 0:2] = jnp.zeros((2, 176, 128), f32)

        @pl.when(lat == 15)
        def _():
            win[c, 4:6] = jnp.zeros((2, 176, 128), f32)

        wrap(c, slice(0, 2))
        wrap(c, slice(4, 6))
        for i in range(ROWS):
            su[c, i * LON : (i + 1) * LON] = taps(c, i, met[i], su[c, i * LON : (i + 1) * LON])

    for side, copy in enumerate(thin):
        copy.wait_recv()
        column = jnp.transpose(thin_r[side])
        for i in range(ROWS):
            win[CHUNKS - 1, 4 * side + i, 8:168, 0:1] = column[:, i : i + 1]
    meet(CHUNKS - 1)

    @pl.loop(0, CHUNKS - 1)
    def _(c):
        for copy in halo(c):
            copy.wait_recv()
        meet(c)

    level = su[0]
    for c in range(1, CHUNKS):
        level = level + su[c]
    mean = jnp.sum(level, axis=1, keepdims=True) * (1.0 / C)
    first_lane = (lax.broadcasted_iota(jnp.int32, (CELLS, 128), 1) < 1).astype(f32)
    square = jnp.zeros((CELLS, 128), f32)
    for c in range(CHUNKS):
        center = su[c] - mean
        if c == CHUNKS - 1:
            center = center * first_lane
        nr[c] = center
        square = square + center * center
    inverse = lax.rsqrt(jnp.sum(square, axis=1, keepdims=True) * (1.0 / C) + EPSILON)
    inv[...] = inverse
    for c in range(CHUNKS):
        normed = nr[c] * inverse
        nr[c] = normed
        sc[:, c * 128 : (c + 1) * 128] = (normed * gn[c]).astype(bf16)

    for c in weights:
        c.wait()
    pre[...] = jnp.dot(sc[:, 0:C], up[...], preferred_element_type=f32)

    @pl.loop(0, CELLS // 16)
    def _(r):
        rows = pl.ds(pl.multiple_of(r * 16, 16), 16)
        x = pre[rows, :]
        cumul = 0.5 * (1.0 + lax.erf(x * (1.0 / math.sqrt(2.0))))
        density = jnp.exp(-0.5 * x * x) * (1.0 / math.sqrt(2.0 * math.pi))
        hid[rows, :] = (x * cumul).astype(bf16)
        slope[rows, :] = cumul + x * density

    mlp = contract(hid[...], down_t[...], (1, 1))
    for c in range(CHUNKS - 1):
        at = slice(c * 128, (c + 1) * 128)
        rd[:, at] = (su[c] + mlp[:, at]).astype(bf16)
    rd[:, 640:641] = (su[CHUNKS - 1, :, 0:1] + mlp[:, 640:641]).astype(bf16)
    fcs[...] = contract(rd[...], hp[...], (1, 1))

    for p in range(MEMBERS):
        fs[p] = fcs[p * BLOCK : (p + 1) * BLOCK, :]
    sent = []
    for d in range(1, MEMBERS):
        p = (member + d) % MEMBERS
        c = remote(fs.at[p], fr.at[member], fc_s.at[d - 1], fc_r.at[d - 1], others[d - 1])
        c.start()
        sent.append(c)
    fr[member] = fs[member]
    for c in sent:
        c.wait_recv()

    row = 2 * lat + member // (MEMBERS // ROWS)
    area = jnp.float32(AREA[0])
    for i in range(1, NLAT):
        area = jnp.where(row == i, jnp.float32(AREA[i]), area)
    weight = field_weight[...] * area
    against = truth[member]
    members = fr[...]
    gap = members - against[None]
    square = gap * gap + DELTA * DELTA
    root = lax.rsqrt(square)
    miss = jnp.sum(square * root - DELTA, axis=0)
    slope_miss = gap * root
    apart = jnp.zeros((BLOCK, FIELDS), f32)
    pull = jnp.zeros((MEMBERS, BLOCK, FIELDS), f32)
    for n in range(MEMBERS):
        gap = members - fr[n][None]
        square = gap * gap + DELTA * DELTA
        root = lax.rsqrt(square)
        apart = apart + jnp.sum(square * root - DELTA, axis=0)
        pull = pull + gap * root
    cells = NLAT * LON * FIELDS
    spread = miss * (1.0 / MEMBERS) - apart * (1.0 / (2.0 * MEMBERS * (MEMBERS - 1)))
    cotangent = weight[None] * (slope_miss - pull * (1.0 / (MEMBERS - 1))) * (1.0 / (MEMBERS * math.sqrt(cells)))
    co_s[...] = cotangent.astype(bf16)
    back = []
    for d in range(1, MEMBERS):
        p = (member + d) % MEMBERS
        c = remote(co_s.at[p], co_r.at[member], ct_s.at[d - 1], ct_r.at[d - 1], others[d - 1])
        c.start()
        back.append(c)
    co_r[member] = co_s[member]
    total.loss_send(0, jnp.full((8, 128), jnp.sum(weight * spread) * (1.0 / cells), f32))
    for c in back:
        c.wait_recv()
    for p in range(MEMBERS):
        fcs[p * BLOCK : (p + 1) * BLOCK, :] = co_r[p].astype(f32)
    co[...] = fcs[...].astype(bf16)

    d_output = jnp.dot(co[...], hp[...], preferred_element_type=f32)
    for c in range(CHUNKS):
        dsum[c] = d_output[:, c * 128 : (c + 1) * 128]
    drr[...] = d_output.astype(bf16)

    def half_grad(base, left, right, which, out, then=()):
        for i, (s, wide) in enumerate(((0, 256), (256, 256), (512, 128))):
            columns = pl.ds(pl.multiple_of(which * 640 + s, 128), wide)
            part = contract(left[:, 0:640], right[:, columns], (0, 0))
            for h in range(wide // 128):
                j = base + (s // 128 + h) * TALL
                out[j : j + TALL] = part[:, h * 128 : (h + 1) * 128].reshape(TALL, 16, 128)
            if i in then:
                total.pair(then[i])

    def edge_grad(left, right, r):
        line = contract(left[:, 640:641], right[...], (0, 0))
        for j in range(2 * WIDE):
            small[1, j % 5, r + 2 + j // 5 : r + 3 + j // 5, :] = line[:, j * 128 : (j + 1) * 128]
        edge = contract(right[:, 1280:1282], left[...], (0, 0))
        for c in range(CHUNKS):
            small[1, c, r : r + 2, :] = edge[:, c * 128 : (c + 1) * 128]

    core = total.core
    half_grad(0, drr, hid, 1 - core, total.away, {1: 0, 2: 1})
    half_grad(0, drr, hid, core, total.own)
    pre[...] = jnp.dot(drr[:, 0:C], down_t[...], preferred_element_type=f32)

    @pl.loop(0, CELLS // 16)
    def _(r):
        rows = pl.ds(pl.multiple_of(r * 16, 16), 16)
        dp[rows, :] = (pre[rows, :] * slope[rows, :]).astype(bf16)

    total.scatter_0(0)
    total.scatter_0(1)
    half_grad(HALF, sc, dp, 1 - core, total.away, {1: 2, 2: 3})
    half_grad(HALF, sc, dp, core, total.own)
    total.loss_next(0)
    head_grad = contract(co[...], rd[...], (0, 0))
    for c in range(CHUNKS):
        small[0, c, 0:64, :] = head_grad[0:64, c * 128 : (c + 1) * 128]
        small[1, c, 0:8, :] = head_grad[64:72, c * 128 : (c + 1) * 128]
    total.scatter_0(2)
    total.scatter_0(3)
    edge_grad(drr, hid, 39)
    edge_grad(sc, dp, 34)
    put(dsc, contract(dp[...], up[...], (1, 1)))
    mean_a = jnp.zeros((CELLS, 128), f32)
    mean_b = jnp.zeros((CELLS, 128), f32)
    for c in range(CHUNKS):
        both = dsc[c] * nr[c]
        small[1, c, 33:34, :] = jnp.sum(both, axis=0, keepdims=True)
        mean_a = mean_a + dsc[c] * gn[c]
        mean_b = mean_b + both * gn[c]
    mean_a = jnp.sum(mean_a, axis=1, keepdims=True) * (1.0 / C)
    mean_b = jnp.sum(mean_b, axis=1, keepdims=True) * (1.0 / C)
    for c in range(CHUNKS):
        dsum[c] = dsum[c] + inv[...] * (dsc[c] * gn[c] - mean_a - nr[c] * mean_b)

    total.scatter_1(0)
    total.scatter_1(1)
    total.loss_next(1)

    @pl.loop(0, CHUNKS)
    def _(c):
        for a in range(5):
            acc = [jnp.zeros((8, 128), f32) for _ in range(5)]
            for i in range(ROWS):
                for t in range(LON // 8):
                    d = dsum[c, i * LON + 8 * t : i * LON + 8 * t + 8, :]
                    for b in range(5):
                        acc[b] = acc[b] + d * win[c, i + a, 6 + b + 8 * t : 14 + b + 8 * t, :]
            for b in range(5):
                tap = 8 + 5 * a + b
                small[1, c, tap : tap + 1, :] = jnp.sum(acc[b], axis=0, keepdims=True)

    for c in range(CHUNKS):
        units = slice(SMALL + c * SMALL_TALL, SMALL + (c + 1) * SMALL_TALL)
        total.away[units] = small[1 - core, c].reshape(SMALL_TALL, 16, 128)
        total.own[units] = small[core, c].reshape(SMALL_TALL, 16, 128)
    total.pair(4)

    @pl.loop(0, CHUNKS - 1)
    def _(c):
        for copy in halo(c):
            copy.wait_send()

    for c in list(thin) + sent + back:
        c.wait_send()
    total.scatter_2(0)
    total.scatter_1(2)
    total.scatter_1(3)
    total.scatter_0(4)
    total.loss_next(2)
    total.scatter_1(4)
    total.gather_2(0)
    total.scatter_2(1)
    total.gather_1(0)
    total.gather_1(1)
    total.gather_2(1)
    total.gather_0(0)
    total.gather_0(1)
    total.gather_1(2)
    total.gather_1(3)
    total.gather_1(4)
    for part in (2, 3, 4):
        total.gather_0(part)
    for part in range(5):
        total.hand_over(part)
    total.finish()
    loss_ref[...] = total.loss_take(3)

    for c in sum(total.leaving, []) + total.open:
        c.wait_send()


def gradients(state, conv_kernel, gain, up, down_t, head_t, target, field_weight):
    f32, bf16 = jnp.float32, jnp.bfloat16
    vmem = pl.BlockSpec(memory_space=pltpu.VMEM)
    anywhere = pl.BlockSpec(memory_space=pltpu.HBM)
    V = pltpu.VMEM
    dma = pltpu.SemaphoreType.DMA
    work = dict(
        win=V((CHUNKS, 6, 176, 128), f32),
        ck=V((CHUNKS, 25, 128), f32),
        gn=V((CHUNKS, 1, 128), f32),
        su=V((CHUNKS, CELLS, 128), f32),
        nr=V((CHUNKS, CELLS, 128), f32),
        inv=V((CELLS, 1), f32),
        sc=V((CELLS, 768), bf16),
        rd=V((CELLS, 768), bf16),
        pre=V((CELLS, HID), f32),
        slope=V((CELLS, HID), f32),
        hid=V((CELLS, HID), bf16),
        hp=V((FIELDS, 768), bf16),
        fcs=V((CELLS, FIELDS), f32),
        fs=V((MEMBERS, BLOCK, FIELDS), f32),
        fr=V((MEMBERS, BLOCK, FIELDS), f32),
        truth=V((MEMBERS, BLOCK, FIELDS), f32),
        co_s=V((MEMBERS, BLOCK, FIELDS), bf16),
        co_r=V((MEMBERS, BLOCK, FIELDS), bf16),
        co=V((CELLS, FIELDS), bf16),
        dp=V((CELLS, HID), bf16),
        dsum=V((CHUNKS, CELLS, 128), f32),
        dsc=V((CHUNKS, CELLS, 128), f32),
        small=V((2, CHUNKS, 64, 128), f32),
        thin_s=V((8, LON), f32),
        thin_r=V((2, 8, LON), f32),
        up=V((C, HID), bf16),
        down_t=V((C, HID), bf16),
        drr=V((CELLS, 768), bf16),
        halo_s=dma((2, CHUNKS)),
        halo_r=dma((2, CHUNKS)),
        fc_s=dma((MEMBERS - 1,)),
        fc_r=dma((MEMBERS - 1,)),
        ct_s=dma((MEMBERS - 1,)),
        ct_r=dma((MEMBERS - 1,)),
        wt=dma((8,)),
        state=V((ROWS, LON, C), f32),
        conv_kernel=V((25, C), f32),
        gain=V((C,), f32),
        head_t=V((FIELDS, C), bf16),
        target=V((FIELDS, ROWS, LON), f32),
        field_weight=V((1, FIELDS), f32),
    )
    refs, tree = jax.tree.flatten((work, total_scratch()))

    def kernel(*args):
        step_kernel(*args[:10], *jax.tree.unflatten(tree, args[10:]))

    return pl.pallas_call(
        kernel,
        out_shape=(
            jax.ShapeDtypeStruct((2, UNITS, 16, 128), bf16),
            jax.ShapeDtypeStruct((8, 128), f32),
        ),
        in_specs=[anywhere] * 8,
        out_specs=(vmem, vmem),
        scratch_shapes=refs,
        compiler_params=pltpu.CompilerParams(
            collective_id=0, has_side_effects=True, vmem_limit_bytes=48 * 1024 * 1024
        ),
    )(
        *(
            pltpu.with_memory_space_constraint(a, pltpu.HBM)
            for a in (state, conv_kernel, gain, up, down_t, head_t, target, field_weight)
        )
    )


def unpack_kernel(g_ref, loss, *refs):
    hbm, (up_ref, down_ref, head_ref, kern_ref, gain_ref, loss_ref, small, sem) = refs[:6], refs[6:]
    copies = []

    def send(src, dst):
        copies.append(pltpu.make_async_copy(src, dst, sem.at[len(copies)]))
        copies[-1].start()

    loss_ref[...] = loss[0:1, 0:1]
    send(loss_ref, hbm[5])
    for core in range(2):
        for c in range(CHUNKS):
            start = SMALL + c * SMALL_TALL
            piece = g_ref[core, start : start + SMALL_TALL].astype(jnp.float32)
            small[core, :, c * 128 : (c + 1) * 128] = piece.reshape(64, 128)
    head_ref[0:64, :] = small[0, :, 0:C]
    head_ref[64:72, :] = small[1, 0:8, 0:C]
    send(head_ref, hbm[2])
    kern_ref[...] = small[1, 8:33, 0:C]
    send(kern_ref, hbm[3])
    gain_ref[...] = small[1, 33:34, 0:C].reshape(C)
    send(gain_ref, hbm[4])
    edge = jnp.transpose(small[1, 32:56, :])
    for m, r, out, target in ((0, 39, down_ref, hbm[1]), (1, 34, up_ref, hbm[0])):
        out[640:641, 0:640] = small[1, r + 2 : r + 3, 0:640]
        out[640:641, 640:1280] = small[1, r + 3 : r + 4, 0:640]
        for b in range(5):
            for core in range(2):
                for j in range(WIDE):
                    start = m * HALF + j * TALL + b * 8
                    piece = g_ref[core, start : start + 8].astype(jnp.float32)
                    lane = (core * WIDE + j) * 128
                    out[b * 128 : (b + 1) * 128, lane : lane + 128] = piece.reshape(128, 128)
            end = (b + 1) * 128 + (b == 4)
            out[b * 128 : end, 1280:1282] = edge[b * 128 : end, r - 32 : r - 30]
            rows = pl.ds(b * 128, end - b * 128)
            send(out.at[rows], target.at[rows])
    for c in copies:
        c.wait()


def unpacked(g, loss):
    vmem = pl.BlockSpec(memory_space=pltpu.VMEM)
    hbm = pl.BlockSpec(memory_space=pltpu.HBM)
    shapes = ((C, HID), (C, HID), (FIELDS, C), (25, C), (C,), (1, 1))
    return pl.pallas_call(
        unpack_kernel,
        out_shape=tuple(jax.ShapeDtypeStruct(s, jnp.float32) for s in shapes),
        in_specs=[vmem, vmem],
        out_specs=(hbm,) * 6,
        scratch_shapes=[pltpu.VMEM(s, jnp.float32) for s in shapes]
        + [pltpu.VMEM((2, 64, 768), jnp.float32), pltpu.SemaphoreType.DMA((14,))],
        compiler_params=pltpu.CompilerParams(vmem_limit_bytes=24 * 1024 * 1024),
    )(g, loss)


def local(
    state, conv_kernel, norm_gain, up_weight, down_weight, field_head_weight, target, field_weight
):
    total, loss = gradients(
        jnp.transpose(state[0], (1, 2, 0)),
        conv_kernel,
        norm_gain,
        up_weight,
        down_weight.T,
        field_head_weight.T,
        target,
        field_weight[None],
    )
    up, down_t, head_t, kern, gain_row, loss = unpacked(total, loss)
    return (loss.reshape(()), kern, gain_row, up, down_t.T, head_t.T)


def solution(mesh):
    finer = Mesh(mesh.devices.reshape(4, 2, 2, 2, 8), AXES)
    mem, lat = AXES[:3], AXES[3:]
    in_specs = (P(mem, None, lat, None), P(), P(), P(), P(), P(), P(None, lat, None), P())
    out_specs = (P(), P(), P(), P(), P(), P())
    return jax.shard_map(local, mesh=finer, in_specs=in_specs, out_specs=out_specs, check_vma=False)
```
